128 devices in a mesh: gx: 32 (over y, z, core), gy: 4 (over x).
Axes of the slice: x: 4, y: 4, z: 4, core: 2. Of those that a mesh axis runs over, the one named last changes fastest.
Arguments:
- point_feats: bfloat16 [32, 4194304], P(None, ('gx', 'gy')), may hold values from -0.5 to 0.5
- point_targets: bfloat16 [4194304], P(('gx', 'gy')), may hold values from -6 to 6
- point_lists: int32 [524288, 8], P(('gx', 'gy')), may hold values from -1 to 32767, as said below
- brick_adjacency: int32 [4096, 4], P(('gx', 'gy')), may hold values from -1 to 4095, as said below
- voxel_feats: float32 [4096, 32, 512], P(('gx', 'gy')), may hold values from -0.25 to 0.25
- voxel_reg: float32 [4096, 512], P(('gx', 'gy')), may hold values from 0.25 to 2
Outputs:
- solution: float32 [4096, 512], P(('gx', 'gy'))
- residual: float32 [4096, 512], P(('gx', 'gy'))
The draws below stay inside these ranges and needn't reach their ends.
Inputs may be any that keep to these rules, and one draw needn't show every extreme that they name: `point_lists`: row s * 4096 + b lists, in its first slots, distinct indices of the points of source device s in brick b, all within that device's rows b * 8 to b * 8 + 7, then -1 in the remaining slots. Point rows named by no list are unused. `brick_adjacency`: entry k of brick b is the lattice neighbour of b in direction k (minus along the road, plus along the road, minus across, plus across) or -1; the relation is symmetric and -1 wherever the neighbour lies outside the lattice.
All inputs are finite; a program needn't handle non-finite values.
Results may differ from the reference program's by a relative error of at most 0.0003.
Values may be sent and summed in bfloat16 or wider, within the bound.
No kernel may reach another device: no remote copies, remote signals or barrier semaphores. Data moves between devices by JAX's collectives and lax.ppermute only.
A program may use at most 64 MiB of HBM per device.

```python
import math
import jax
import jax.numpy as jnp
from jax import lax

FEAT = 32
VOX = 512
BX = 8
BY = 4
CAPB = 8
ITERS = 3
BR_DEV = 32
NB = 4096
P_DEV = 32768
POINTS = 4194304
LX = 256
LY = 16
N_GX = 32
N_GY = 4
DEVICES = 128


def draw_point_lists(key, part):
    devices = NB // BR_DEV
    key_counts, key_own, key_shared, key_perm = jax.random.split(jax.random.fold_in(key, 11), 4)
    owner = jnp.arange(NB, dtype=jnp.int32) // BR_DEV
    hottest = 4 + 20 * owner // max(devices - 1, 1)
    raw = jax.random.randint(key_counts, (devices, NB), 0, 1 << 20) % hottest[None, :]
    counts = jnp.minimum(raw, CAPB)
    own_pick = jax.random.randint(key_own, (devices,), 0, NB)
    counts = counts.at[jnp.arange(devices), own_pick].set(CAPB)
    shared = jax.random.randint(key_shared, (), 0, NB)
    counts = counts.at[:, shared].set(CAPB)
    counts = counts.at[:, NB - 1].set(CAPB)
    slot = jnp.arange(CAPB, dtype=jnp.int32)
    scores = jax.random.randint(key_perm, (devices, NB, CAPB), 0, 1 << 20) * CAPB + slot[None, None, :]
    order = jnp.argsort(scores, axis=-1).astype(jnp.int32)
    brick = jnp.arange(NB, dtype=jnp.int32)[None, :, None]
    listed = jnp.where(slot[None, None, :] < counts[:, :, None], brick * CAPB + order, -1)
    return listed.reshape(devices * NB, CAPB).astype(jnp.int32)


def draw_brick_adjacency(key, part):
    key_x, key_y = jax.random.split(jax.random.fold_in(key, 7))
    keep_x = jax.random.randint(key_x, (LX - 1, LY), 0, 4) > 0
    keep_y = jax.random.randint(key_y, (LX, LY - 1), 0, 4) > 0
    place_x = jnp.arange(LX, dtype=jnp.int32)[:, None]
    place_y = jnp.arange(LY, dtype=jnp.int32)[None, :]
    ident = (place_x // BX * (LY // BY) + place_y // BY) * BR_DEV + place_x % BX * BY + place_y % BY
    minus_x = jnp.where(jnp.pad(keep_x, ((1, 0), (0, 0))), jnp.pad(ident[:-1], ((1, 0), (0, 0))), -1)
    plus_x = jnp.where(jnp.pad(keep_x, ((0, 1), (0, 0))), jnp.pad(ident[1:], ((0, 1), (0, 0))), -1)
    minus_y = jnp.where(jnp.pad(keep_y, ((0, 0), (1, 0))), jnp.pad(ident[:, :-1], ((0, 0), (1, 0))), -1)
    plus_y = jnp.where(jnp.pad(keep_y, ((0, 0), (0, 1))), jnp.pad(ident[:, 1:], ((0, 0), (0, 1))), -1)
    lattice = jnp.stack([minus_x, plus_x, minus_y, plus_y], axis=-1)
    shaped = lattice.reshape(LX // BX, BX, LY // BY, BY, 4).transpose(0, 2, 1, 3, 4)
    return shaped.reshape(NB, 4).astype(jnp.int32)


def shard_levels(rng, extent, cuts, low, high):
    level = 1.0
    for position, parts in cuts:
        draws = jax.random.uniform(jax.random.fold_in(jax.random.fold_in(rng, 6), position), (parts,), jnp.float32, low / len(cuts), high / len(cuts))
        level = level * jnp.repeat(jnp.exp(draws), extent[position] // parts).reshape((-1,) + (1,) * (len(extent) - 1 - position))
    return level


def scatter_about(rng, extent, scale, limit, cuts=(), held_as=jnp.bfloat16):
    values = scale * jax.random.normal(rng, extent, jnp.float32)
    if cuts:
        values = values * shard_levels(rng, extent, cuts, -0.22, 0.18)
    return jnp.clip(values, -limit, limit).astype(held_as)


def setup_inputs(seed: int = 0) -> dict:
    arg_keys = jax.random.split(jax.random.key(seed), 7)
    return {
        "point_feats": scatter_about(arg_keys[0], (FEAT, POINTS), (DEVICES ** -0.5), 0.5, ((1, 128),)),
        "point_targets": scatter_about(arg_keys[1], (POINTS,), 1.0, 6.0, ((0, 128),)),
        "point_lists": draw_point_lists(jax.random.fold_in(arg_keys[6], 71), 0),
        "brick_adjacency": draw_brick_adjacency(jax.random.fold_in(arg_keys[6], 71), 0),
        "voxel_feats": scatter_about(arg_keys[4], (NB, FEAT, VOX), VOX ** -0.5, 0.25, ((0, 128),), jnp.float32),
        "voxel_reg": jnp.clip(jnp.exp(math.log(2.0) - 2.0794415 * jax.random.uniform(arg_keys[5], (NB, VOX), jnp.float32) ** shard_levels(arg_keys[5], (NB, VOX), ((0, 128),), -0.2, 0.2)), 0.25, 2.0),
    }


coupling_weight = 1.0


def to_lattice(values):
    width = values.shape[-1]
    shaped = values.reshape(N_GX, N_GY, BX, BY, width).transpose(0, 2, 1, 3, 4)
    return shaped.reshape(BX * N_GX, BY * N_GY, width)


def from_lattice(values):
    width = values.shape[-1]
    shaped = values.reshape(N_GX, BX, N_GY, BY, width).transpose(0, 2, 1, 3, 4)
    return shaped.reshape(BR_DEV * N_GX * N_GY, width)


def neighbour_sum(lattice, mask):
    padded = jnp.pad(lattice, ((1, 1), (1, 1), (0, 0)))
    total = mask[..., 0:1] * padded[:-2, 1:-1] + mask[..., 1:2] * padded[2:, 1:-1]
    return total + mask[..., 2:3] * padded[1:-1, :-2] + mask[..., 3:4] * padded[1:-1, 2:]


def reference(point_feats, point_targets, point_lists, brick_adjacency, voxel_feats, voxel_reg):
    devices = N_GX * N_GY
    lists = point_lists.reshape(devices, NB, CAPB)
    base = (jnp.arange(devices, dtype=jnp.int32) * P_DEV)[:, None, None]

    def one_owner(owner):
        rows = lax.dynamic_slice_in_dim(lists, (owner * BR_DEV).astype(jnp.int32), BR_DEV, 1)
        live = rows >= 0
        index = (jnp.where(live, rows, 0) + base).reshape(-1)
        feats = jnp.take(point_feats, index, axis=1).astype(jnp.float32).reshape(FEAT, devices, BR_DEV, CAPB)
        feats = jnp.where(live[None], feats, jnp.zeros((), jnp.float32))
        target = jnp.take(point_targets, index).astype(jnp.float32).reshape(live.shape)
        target = jnp.where(live, target, jnp.zeros((), jnp.float32))
        moment = jnp.einsum("isbc,jsbc->bij", feats, feats, precision=lax.Precision.HIGHEST)
        gathered = jnp.einsum("sbc,isbc->bi", target, feats, precision=lax.Precision.HIGHEST)
        return moment, gathered

    moments, gathered = lax.map(one_owner, jnp.arange(devices, dtype=jnp.int32))
    moments = moments.reshape(NB, FEAT, FEAT)
    gathered = gathered.reshape(NB, FEAT)
    mask = to_lattice((brick_adjacency >= 0).astype(jnp.float32))
    degree = jnp.sum(mask, axis=-1, keepdims=True)

    def operate(vector):
        projected = jnp.einsum("bik,bk->bi", voxel_feats, vector, precision=lax.Precision.HIGHEST)
        lattice = to_lattice(projected)
        coupled = from_lattice(degree * lattice - neighbour_sum(lattice, mask))
        middle = jnp.einsum("bij,bj->bi", moments, projected, precision=lax.Precision.HIGHEST)
        middle = middle + coupling_weight * coupled
        back = jnp.einsum("bik,bi->bk", voxel_feats, middle, precision=lax.Precision.HIGHEST)
        return back + voxel_reg * vector

    rhs = jnp.einsum("bik,bi->bk", voxel_feats, gathered, precision=lax.Precision.HIGHEST)
    solution = jnp.zeros_like(rhs)
    residual, direction = rhs, rhs
    norm_now = jnp.sum(residual * residual)
    for iteration in range(ITERS):
        image = operate(direction)
        alpha = norm_now / jnp.sum(direction * image)
        solution = solution + alpha * direction
        residual = residual - alpha * image
        norm_next = jnp.sum(residual * residual)
        direction = residual + (norm_next / norm_now) * direction
        norm_now = norm_next
    return solution, residual
```

```python
import functools

import jax
import jax.numpy as jnp
from jax import lax
from jax.experimental import pallas as pl
from jax.experimental.pallas import tpu as pltpu
from jax.sharding import Mesh
from jax.sharding import PartitionSpec as P

BX = 8
BY = 4
ITERS = 3
SLOTS = 8
LANES = 128
GX_GY = ("gx_0", "gx_1", "gx_2", "gy")
GX = ("gx_0", "gx_1", "gx_2")
HIGHEST = lax.Precision.HIGHEST


coupling_weight = 1.0


def pack_kernel(lists_ref, feats_ref, targets_ref, out_ref, mask_ref):
    rows = mask_ref.shape[0]
    width = LANES * SLOTS

    @pl.when(pl.program_id(0) == 0)
    def _():
        lane = lax.broadcasted_iota(jnp.int32, (SLOTS, LANES), 1)
        codes = []
        for block in range(rows):
            chosen = lists_ref[:, block * LANES : (block + 1) * LANES]
            offset = chosen - (lane + block * LANES) * SLOTS
            bits = jnp.where(chosen >= 0, lax.shift_left(1, jnp.clip(offset, 0, SLOTS - 1)), 0)
            codes.append(jnp.sum(bits, axis=0, keepdims=True))
        code = jnp.concatenate(codes, axis=0).astype(jnp.float32).astype(jnp.bfloat16)
        brick = lax.broadcasted_iota(jnp.int32, (LANES, width), 0)
        point = lax.broadcasted_iota(jnp.int32, (LANES, width), 1)
        spread = (lax.shift_right_logical(point, 3) == brick).astype(jnp.float32).astype(jnp.bfloat16)
        wide = jnp.dot(code, spread, preferred_element_type=jnp.float32).astype(jnp.int32)
        slot = lax.broadcasted_iota(jnp.int32, (rows, width), 1) & (SLOTS - 1)
        mask_ref[...] = (lax.shift_right_logical(wide, slot) & 1).astype(jnp.float32)

    step = pl.program_id(0)
    dests = out_ref.shape[0]
    feat_count = feats_ref.shape[0]
    for part in range(dests * 256 // width):
        row = mask_ref[pl.ds(step * (dests * 256 // width) + part, 1), :].astype(jnp.bfloat16)
        masked = feats_ref[:, part * width : (part + 1) * width] * row
        for piece in range(width // LANES):
            dest = (part * width + piece * LANES) // 256
            half = piece % 2
            out_ref[dest, half * feat_count : (half + 1) * feat_count, :] = masked[
                :, piece * LANES : (piece + 1) * LANES
            ]
    for dest in range(dests):
        out_ref[dest, 2 * feat_count : 2 * feat_count + 2, :] = targets_ref[2 * dest : 2 * dest + 2, :]


def pack(point_feats, point_targets, point_lists, devices):
    feat_count, points = point_feats.shape
    bricks = point_lists.shape[0]
    steps = 8
    dests = devices // steps
    return pl.pallas_call(
        pack_kernel,
        grid=(steps,),
        in_specs=[
            pl.BlockSpec((SLOTS, bricks), lambda i: (0, 0)),
            pl.BlockSpec((feat_count, points // steps), lambda i: (0, i)),
            pl.BlockSpec((points // steps // LANES, LANES), lambda i: (i, 0)),
        ],
        out_specs=pl.BlockSpec((dests, 2 * feat_count + 2, LANES), lambda i: (i, 0, 0)),
        out_shape=jax.ShapeDtypeStruct((devices, 2 * feat_count + 2, LANES), jnp.bfloat16),
        scratch_shapes=[pltpu.VMEM((bricks // LANES, LANES * SLOTS), jnp.float32)],
        name="pack",
    )(point_lists.T, point_feats, point_targets.reshape(points // LANES, LANES))


def with_halo(x, sides, width):
    edges = {}
    for axis, dim in sides:
        devices, length = (lax.axis_size(axis), x.shape[dim])
        up = [(i, (i + 1) % devices) for i in range(devices - 1)]
        last = lax.slice_in_dim(x, length - width, length, axis=dim)
        leading = lax.slice_in_dim(x, 0, width, axis=dim)
        edges[dim] = (
            lax.ppermute(last, axis, up),
            lax.ppermute(leading, axis, [(b, a) for a, b in up]),
        )
    done = []
    for _, dim in sides:
        low, high = edges[dim]
        around = [(width, width) if d in done else (0, 0) for d in range(x.ndim)]
        x = jnp.concatenate([jnp.pad(low, around), x, jnp.pad(high, around)], axis=dim)
        done.append(dim)
    return x


def neighbour_sum(padded, mask):
    total = mask[..., 0:1] * padded[:-2, 1:-1] + mask[..., 1:2] * padded[2:, 1:-1]
    return total + mask[..., 2:3] * padded[1:-1, :-2] + mask[..., 3:4] * padded[1:-1, 2:]


def everyone(values, devices):
    spread = jnp.broadcast_to(values[None, :], (devices, values.shape[0]))
    return lax.all_to_all(spread, GX_GY, split_axis=0, concat_axis=0, tiled=True)


def krylov_coefficients(basis, devices):
    peaks = [jnp.max(jnp.abs(v)) for v in basis]
    inverse = [jnp.where(p > 1e-37, 1.0 / p, 0.0) for p in peaks]
    scaled = [v * s for v, s in zip(basis, inverse)]
    pairs = [(a, b) for a in range(4) for b in range(a, 4)]
    local = jnp.stack([jnp.sum(scaled[a] * scaled[b]) for a, b in pairs] + peaks)
    shared = everyone(local, devices)
    peak = jnp.max(shared[:, 10:14], axis=0)
    weight = shared[:, 10:14] / peak[None, :]
    gram = [[None] * 4 for _ in range(4)]
    for column, (a, b) in enumerate(pairs):
        value = jnp.sum(shared[:, column] * weight[:, a] * weight[:, b])
        gram[a][b] = gram[b][a] = value
    growth = [peak[k + 1] / peak[k] for k in range(3)]

    def product(left, right):
        total = 0.0
        for a in range(4):
            for b in range(4):
                if left[a] is not None and right[b] is not None:
                    total = total + left[a] * right[b] * gram[a][b]
        return total

    def plus(left, scale, right):
        out = []
        for a, b in zip(left, right):
            out.append(a if b is None else scale * b if a is None else a + scale * b)
        return out

    def image(vector):
        return [None] + [None if vector[k] is None else vector[k] * growth[k] for k in range(3)]

    one = jnp.float32(1.0)
    solution = [None] * 4
    residual = [one, None, None, None]
    direction = list(residual)
    norm_now = product(residual, residual)
    for iteration in range(ITERS):
        carried = image(direction)
        alpha = norm_now / product(direction, carried)
        solution = plus(solution, alpha, direction)
        residual = plus(residual, -alpha, carried)
        if iteration + 1 < ITERS:
            norm_next = product(residual, residual)
            direction = plus(residual, norm_next / norm_now, direction)
            norm_now = norm_next
    zero = jnp.float32(0.0)
    back = [peak[0] / peak[k] for k in range(4)]
    return [[zero if c is None else c * back[k] for k, c in enumerate(cs)] for cs in (solution, residual)]


def shards(point_feats, point_targets, point_lists, brick_adjacency, voxel_feats, voxel_reg):
    feat_count = point_feats.shape[0]
    brick_total, slots = point_lists.shape
    local_bricks = voxel_feats.shape[0]
    devices = brick_total // local_bricks
    sending = pack(point_feats, point_targets, point_lists, devices)
    got = lax.all_to_all(sending, GX_GY, split_axis=0, concat_axis=0, tiled=True)
    got_feats = got[:, : 2 * feat_count].reshape(devices, 2, feat_count, local_bricks // 2, slots)
    got_targets = got[:, 2 * feat_count :].reshape(devices, 2, local_bricks // 2, slots)
    moments = jnp.einsum(
        "shibc,shjbc->hbij", got_feats, got_feats, preferred_element_type=jnp.float32
    ).reshape(local_bricks, feat_count, feat_count)
    gathered = jnp.einsum(
        "shbc,shibc->hbi", got_targets, got_feats, preferred_element_type=jnp.float32
    ).reshape(local_bricks, feat_count)
    mask = (brick_adjacency >= 0).astype(jnp.float32).reshape(BX, BY, 4)
    degree = jnp.sum(mask, axis=-1, keepdims=True)

    weighted = voxel_feats
    grams = []
    for power in range(ITERS):
        grams.append(jnp.einsum("bik,bjk->bij", weighted, voxel_feats, precision=HIGHEST))
        weighted = weighted * voxel_reg[:, None, :]

    def apply(matrix, vector):
        return jnp.sum(matrix * vector[:, None, :], axis=-1)

    chain = [gathered]
    for step in range(ITERS):
        projected = sum(apply(grams[a], chain[step - a]) for a in range(step + 1))
        lattice = projected.reshape(BX, BY, feat_count)
        padded = with_halo(lattice, ((GX, 0), ("gy", 1)), 1)
        coupled = (degree * lattice - neighbour_sum(padded, mask)).reshape(local_bricks, feat_count)
        chain.append(apply(moments, projected) + coupling_weight * coupled)
    basis = []
    for step, values in enumerate(chain):
        vector = jnp.sum(voxel_feats * values[:, :, None], axis=1)
        if step:
            vector = vector + voxel_reg * basis[-1]
        basis.append(vector)
    in_solution, in_residual = krylov_coefficients(basis, devices)
    return (
        sum(c * v for c, v in zip(in_solution, basis)),
        sum(c * v for c, v in zip(in_residual, basis)),
    )


def solution(mesh):
    torus = Mesh(mesh.devices.reshape(4, 4, 2, mesh.shape["gy"]), ("gx_0", "gx_1", "gx_2", "gy"))
    return jax.shard_map(
        shards,
        mesh=torus,
        in_specs=(
            P(None, GX_GY),
            P(GX_GY),
            P(GX_GY, None),
            P(GX_GY, None),
            P(GX_GY, None, None),
            P(GX_GY, None),
        ),
        out_specs=(P(GX_GY, None), P(GX_GY, None)),
        check_vma=False,
    )
```

```python
import functools

import jax
import jax.numpy as jnp
from jax import lax
from jax.experimental import pallas as pl
from jax.experimental.pallas import tpu as pltpu
from jax.sharding import Mesh
from jax.sharding import PartitionSpec as P

BX = 8
BY = 4
ITERS = 3
SLOTS = 8
LANES = 128
FEAT = 32
PITCH = 16
SPAN = 256
REACH = 3
GX_GY = ("gx_0", "gx_1", "gx_2", "gy")
GX = ("gx_0", "gx_1", "gx_2")
HIGHEST = lax.Precision.HIGHEST
PAIRS = tuple((a, b) for a in range(4) for b in range(a, 4))


coupling_weight = 1.0

EARLY = ((8, 2), (8, 1), (1, 2))
LATE = ((8, 2), (1, 3))


def padded(rows):
    return (rows + 7) // 8 * 8


def along_rows(section):
    return padded(section[0] * section[1] * BY)


def across_rows(section):
    rows, depth = section
    return padded(rows * sum(BX + 2 * (depth - k) for k in range(1, depth + 1)))


def message_rows(sections, size):
    return sum(size(section) for section in sections)


def piece(ref, start, rows, index):
    if rows == 8 and len(ref.shape) == 3:
        return ref[index]
    return ref[start + rows * index : start + rows * (index + 1), :]


def brick_at(own, low, high, start, section, a, e):
    rows, depth = section
    if a < 0:
        return piece(low, start, rows, (a + depth) * BY + e)
    if a >= BX:
        return piece(high, start, rows, (a - BX) * BY + e)
    return piece(own, 0, rows, a * BY + e)


def fill_across(sections, owns, low, high, to_low, to_high):
    source = target = 0
    for section, own in zip(sections, owns):
        rows, depth = section
        index = 0
        for away in range(1, depth + 1):
            extra = depth - away
            for a in range(-extra, BX + extra):
                place = slice(target + rows * index, target + rows * (index + 1))
                to_low[place, :] = brick_at(own, low, high, source, section, a, away - 1)
                to_high[place, :] = brick_at(own, low, high, source, section, a, BY - away)
                index += 1
        used, whole = rows * index, across_rows(section)
        if used < whole:
            blank = jnp.zeros((whole - used, LANES), jnp.float32)
            to_low[target + used : target + whole, :] = blank
            to_high[target + used : target + whole, :] = blank
        source += along_rows(section)
        target += whole


def place_bricks(put, sections, which, own, along_low, along_high, across_low, across_high):
    section = sections[which]
    rows, depth = section
    start = message_rows(sections[:which], along_rows)
    for a in range(-depth, BX + depth):
        for e in range(BY):
            put(a, e, brick_at(own, along_low, along_high, start, section, a, e))
    start = message_rows(sections[:which], across_rows)
    index = 0
    for away in range(1, depth + 1):
        extra = depth - away
        for a in range(-extra, BX + extra):
            put(a, -away, piece(across_low, start, rows, index))
            put(a, BY - 1 + away, piece(across_high, start, rows, index))
            index += 1


def lane_of(a, e):
    return (a + REACH) * PITCH + e + REACH


def to_lanes(records, lanes_ref):
    for t in range(8):
        lanes_ref[t * LANES : (t + 1) * LANES, :] = records[:, t, :].T


def times(matrix_ref, vector):
    total = None
    for t in range(8):
        for q in range(4):
            i = 8 * q + t
            row = t * LANES + q * FEAT
            term = matrix_ref[row : row + FEAT, :] * vector[i : i + 1, :]
            total = term if total is None else total + term
    return total


def pack_kernel(lists_ref, feats_ref, targets_ref, out_ref, mask_ref):
    rows = mask_ref.shape[0]
    width = LANES * SLOTS

    @pl.when(pl.program_id(0) == 0)
    def _():
        lane = lax.broadcasted_iota(jnp.int32, (SLOTS, LANES), 1)
        codes = []
        for block in range(rows):
            chosen = lists_ref[:, block * LANES : (block + 1) * LANES]
            offset = chosen - (lane + block * LANES) * SLOTS
            bits = jnp.where(chosen >= 0, lax.shift_left(1, jnp.clip(offset, 0, SLOTS - 1)), 0)
            codes.append(jnp.sum(bits, axis=0, keepdims=True))
        code = jnp.concatenate(codes, axis=0).astype(jnp.float32).astype(jnp.bfloat16)
        brick = lax.broadcasted_iota(jnp.int32, (LANES, width), 0)
        point = lax.broadcasted_iota(jnp.int32, (LANES, width), 1)
        spread = (lax.shift_right_logical(point, 3) == brick).astype(jnp.float32).astype(jnp.bfloat16)
        wide = jnp.dot(code, spread, preferred_element_type=jnp.float32).astype(jnp.int32)
        slot = lax.broadcasted_iota(jnp.int32, (rows, width), 1) & (SLOTS - 1)
        mask_ref[...] = (lax.shift_right_logical(wide, slot) & 1).astype(jnp.float32)

    step = pl.program_id(0)
    dests = out_ref.shape[0]
    feat_count = feats_ref.shape[0]
    for part in range(dests * 256 // width):
        row = mask_ref[pl.ds(step * (dests * 256 // width) + part, 1), :].astype(jnp.bfloat16)
        masked = feats_ref[:, part * width : (part + 1) * width] * row
        for half_block in range(width // LANES):
            dest = (part * width + half_block * LANES) // 256
            half = half_block % 2
            out_ref[dest, half * feat_count : (half + 1) * feat_count, :] = masked[
                :, half_block * LANES : (half_block + 1) * LANES
            ]
    for dest in range(dests):
        out_ref[dest, 2 * feat_count : 2 * feat_count + 2, :] = targets_ref[2 * dest : 2 * dest + 2, :]


def pack(point_feats, point_targets, point_lists, devices):
    feat_count, points = point_feats.shape
    bricks = point_lists.shape[0]
    steps = 8
    dests = devices // steps
    return pl.pallas_call(
        pack_kernel,
        grid=(steps,),
        in_specs=[
            pl.BlockSpec((SLOTS, bricks), lambda i: (0, 0)),
            pl.BlockSpec((feat_count, points // steps), lambda i: (0, i)),
            pl.BlockSpec((points // steps // LANES, LANES), lambda i: (i, 0)),
        ],
        out_specs=pl.BlockSpec((dests, 2 * feat_count + 2, LANES), lambda i: (i, 0, 0)),
        out_shape=jax.ShapeDtypeStruct((devices, 2 * feat_count + 2, LANES), jnp.bfloat16),
        scratch_shapes=[pltpu.VMEM((bricks // LANES, LANES * SLOTS), jnp.float32)],
        name="pack",
    )(point_lists.T, point_feats, point_targets.reshape(points // LANES, LANES))


def prepare_kernel(feats_ref, reg_ref, first_ref, second_ref, third_ref, lanes_ref):
    records = (first_ref, second_ref, third_ref)

    def one(b, carry):
        feats = feats_ref[b]
        reg = reg_ref[pl.ds(b, 1), :]
        once = feats * reg
        left = jnp.concatenate([feats, once, once * reg], axis=0)
        product = lax.dot_general(
            left,
            feats,
            (((1,), (1,)), ((), ())),
            precision=HIGHEST,
            preferred_element_type=jnp.float32,
        )
        for power, record in enumerate(records):
            rows = [product[power * FEAT + 8 * q : power * FEAT + 8 * q + 8, :] for q in range(4)]
            record[b] = jnp.concatenate(rows, axis=1)
        return carry

    lax.fori_loop(0, feats_ref.shape[0], one, 0)
    for power, record in enumerate(records):
        for t in range(8):
            block = jnp.concatenate([record[:, t, :], jnp.zeros((96, LANES), jnp.float32)], axis=0)
            lanes_ref[power, t * LANES : (t + 1) * LANES, :] = block.T


def prepare(voxel_feats, voxel_reg):
    bricks = voxel_feats.shape[0]
    record = jax.ShapeDtypeStruct((bricks, 8, LANES), jnp.float32)
    return pl.pallas_call(
        prepare_kernel,
        out_shape=(record, record, record, jax.ShapeDtypeStruct((3, 8 * LANES, LANES), jnp.float32)),
        compiler_params=pltpu.CompilerParams(vmem_limit_bytes=24 << 20),
        cost_estimate=pl.CostEstimate(flops=600_000_000, bytes_accessed=5_000_000, transcendentals=0),
        name="prepare",
    )(voxel_feats, voxel_reg)


def gather_early_kernel(
    first_ref, second_ref, mask_ref, low_ref, high_ref, below_ref, above_ref,
    first_lanes, second_lanes, mask_lanes, first_store, second_store, mask_store,
):
    for store in (first_store, second_store, mask_store):
        store[...] = jnp.zeros_like(store)

    def put(store):
        def write(a, e, value):
            if len(store.shape) == 3:
                store[lane_of(a, e)] = value
            else:
                store[lane_of(a, e) : lane_of(a, e) + 1, :] = value

        return write

    edges = (low_ref, high_ref, below_ref, above_ref)
    place_bricks(put(first_store), EARLY, 0, first_ref, *edges)
    place_bricks(put(second_store), EARLY, 1, second_ref, *edges)
    place_bricks(put(mask_store), EARLY, 2, mask_ref, *edges)
    to_lanes(first_store, first_lanes)
    to_lanes(second_store, second_lanes)
    mask_lanes[...] = mask_store[...].T[:8, :]


def gather_early(first, second, mask, edges):
    lanes = jax.ShapeDtypeStruct((8 * LANES, SPAN), jnp.float32)
    return pl.pallas_call(
        gather_early_kernel,
        out_shape=(lanes, lanes, jax.ShapeDtypeStruct((8, SPAN), jnp.float32)),
        scratch_shapes=[
            pltpu.VMEM((SPAN, 8, LANES), jnp.float32),
            pltpu.VMEM((SPAN, 8, LANES), jnp.float32),
            pltpu.VMEM((SPAN, LANES), jnp.float32),
        ],
        compiler_params=pltpu.CompilerParams(vmem_limit_bytes=24 << 20),
        cost_estimate=pl.CostEstimate(flops=2_000_000, bytes_accessed=3_000_000, transcendentals=0),
        name="gather_early",
    )(first, second, mask, *edges)


def relay_kernel(sections, count, *refs):
    owns, low, high, to_low, to_high = refs[:count], *refs[count:]
    fill_across(sections, owns, low, high, to_low, to_high)


def relay(sections, owns, low, high, name):
    out = jax.ShapeDtypeStruct((message_rows(sections, across_rows), LANES), jnp.float32)
    return pl.pallas_call(
        functools.partial(relay_kernel, sections, len(owns)),
        out_shape=(out, out),
        name=name,
    )(*owns, low, high)


def along_messages(sections, owns):
    to_low, to_high = [], []
    for (rows, depth), own in zip(sections, owns):
        flat = own.reshape(-1, LANES)
        used = rows * depth * BY
        blank = ((0, padded(used) - used), (0, 0))
        to_low.append(jnp.pad(flat[:used], blank))
        to_high.append(jnp.pad(flat[flat.shape[0] - used :], blank))
    return jnp.concatenate(to_low), jnp.concatenate(to_high)


def swap(to_low, to_high, axis):
    count = lax.axis_size(axis)
    up = [(i, i + 1) for i in range(count - 1)]
    down = [(b, a) for a, b in up]
    return lax.ppermute(to_high, axis, up), lax.ppermute(to_low, axis, down)


def begin_kernel(moments_ref, gathered_ref, lanes_ref, vectors_ref, low_ref, high_ref):
    values = jnp.concatenate(
        [gathered_ref[...], jnp.zeros((LANES - gathered_ref.shape[0], FEAT), jnp.float32)], axis=0
    )
    values = jnp.concatenate([values, jnp.zeros((LANES, LANES - FEAT), jnp.float32)], axis=1).T[:FEAT, :]
    applied = [times(lanes_ref.at[power], values) for power in range(3)]
    vectors = jnp.concatenate([*applied, values], axis=0).T
    vectors_ref[...] = vectors[: vectors_ref.shape[0], :]
    depth = LATE[0][1] * BY
    for k in range(depth):
        low_ref[8 * k : 8 * k + 8, :] = moments_ref[k]
        high_ref[8 * k : 8 * k + 8, :] = moments_ref[BX * BY - depth + k]
    deep = LATE[1][1] * BY
    blank = jnp.zeros((padded(deep) - deep, LANES), jnp.float32)
    low_ref[8 * depth :, :] = jnp.concatenate([vectors[:deep], blank], axis=0)
    high_ref[8 * depth :, :] = jnp.concatenate([vectors[BX * BY - deep : BX * BY], blank], axis=0)


def begin(moments, gathered, lanes):
    message = jax.ShapeDtypeStruct((message_rows(LATE, along_rows), LANES), jnp.float32)
    return pl.pallas_call(
        begin_kernel,
        out_shape=(jax.ShapeDtypeStruct((gathered.shape[0], LANES), jnp.float32), message, message),
        name="begin",
    )(moments, gathered, lanes)


def power_of_two(value):
    scale = jnp.ones_like(value)
    inverse = jnp.ones_like(value)
    for k in (64, 32, 16, 8, 4, 2, 1):
        up, down = 2.0**k, 2.0**-k
        large = value * down >= 1.0
        small = value * up <= 1.0
        value = jnp.where(large, value * down, jnp.where(small, value * up, value))
        scale = jnp.where(large, scale * up, jnp.where(small, scale * down, scale))
        inverse = jnp.where(large, inverse * down, jnp.where(small, inverse * up, inverse))
    return scale, inverse


def krylov_kernel(
    moments_ref, vectors_ref, low_ref, high_ref, below_ref, above_ref, first_ref, second_ref, mask_ref,
    feats_ref, reg_ref, basis_ref, message_ref, moment_store, vector_store, moment_lanes,
):
    moment_store[...] = jnp.zeros_like(moment_store)
    vector_store[...] = jnp.zeros_like(vector_store)

    def put_moment(a, e, value):
        moment_store[lane_of(a, e)] = value

    def put_vector(a, e, value):
        vector_store[lane_of(a, e) : lane_of(a, e) + 1, :] = value

    edges = (low_ref, high_ref, below_ref, above_ref)
    place_bricks(put_moment, LATE, 0, moments_ref, *edges)
    place_bricks(put_vector, LATE, 1, vectors_ref, *edges)
    to_lanes(moment_store, moment_lanes)
    vectors = vector_store[...].T
    masks = mask_ref[...]

    def system(z):
        near = masks[0:1] * pltpu.roll(z, PITCH, 1) + masks[1:2] * pltpu.roll(z, SPAN - PITCH, 1)
        near = near + masks[2:3] * pltpu.roll(z, 1, 1) + masks[3:4] * pltpu.roll(z, SPAN - 1, 1)
        return times(moment_lanes, z) + coupling_weight * (masks[4:5] * z - near)

    one = system(vectors[0:FEAT])
    two = system(times(first_ref, one) + vectors[FEAT : 2 * FEAT])
    three = system(times(first_ref, two) + times(second_ref, one) + vectors[2 * FEAT : 3 * FEAT])
    chain = (vectors[3 * FEAT :], one, two, three)
    for b in range(BX * BY):
        lane = lane_of(b // BY, b % BY)
        feats = feats_ref[b]
        for step, values in enumerate(chain):
            basis_ref[step, b : b + 1, :] = jnp.sum(feats * values[:, lane : lane + 1], axis=0, keepdims=True)
    reg = reg_ref[...]
    basis = [basis_ref[0]]
    for step in range(1, 4):
        basis.append(basis_ref[step] + reg * basis[-1])
        basis_ref[step] = basis[-1]

    def folded(x, combine):
        rows = [x[8 * k : 8 * k + 8, :] for k in range(x.shape[0] // 8)]
        parts = [r[:, LANES * k : LANES * (k + 1)] for r in rows for k in range(x.shape[1] // LANES)]
        while len(parts) > 1:
            parts = [combine(parts[k], parts[k + 1]) for k in range(0, len(parts), 2)]
        return parts[0]

    peaks = [jnp.max(folded(jnp.abs(v), jnp.maximum), axis=0, keepdims=True) for v in basis]
    peaks = jnp.max(jnp.concatenate(peaks + peaks, axis=0), axis=1, keepdims=True)
    scale, inverse = power_of_two(jnp.broadcast_to(peaks, (8, LANES)))
    scaled = [v * inverse[k : k + 1, 0:1] for k, v in enumerate(basis)]
    sums = [jnp.sum(folded(scaled[a] * scaled[b], jnp.add), axis=0, keepdims=True) for a, b in PAIRS]
    sums = jnp.concatenate(sums + [jnp.zeros((16 - len(PAIRS), LANES), jnp.float32)], axis=0)
    sums = jnp.sum(sums, axis=1, keepdims=True)
    lane = lax.broadcasted_iota(jnp.int32, (1, LANES), 1)
    row = jnp.zeros((1, LANES), jnp.float32)
    for k in range(len(PAIRS)):
        row = jnp.where(lane == k, sums[k : k + 1, :], row)
    for k in range(4):
        row = jnp.where(lane == 10 + k, scale[k : k + 1, :], row)
        row = jnp.where(lane == 14 + k, inverse[k : k + 1, :], row)
    message_ref[...] = jnp.broadcast_to(row, message_ref.shape)


def krylov(moments, vectors, edges, first, second, masks, voxel_feats, voxel_reg, devices):
    bricks, _, voxels = voxel_feats.shape
    return pl.pallas_call(
        krylov_kernel,
        out_shape=(
            jax.ShapeDtypeStruct((4, bricks, voxels), jnp.float32),
            jax.ShapeDtypeStruct((devices, LANES), jnp.float32),
        ),
        scratch_shapes=[
            pltpu.VMEM((SPAN, 8, LANES), jnp.float32),
            pltpu.VMEM((SPAN, LANES), jnp.float32),
            pltpu.VMEM((8 * LANES, SPAN), jnp.float32),
        ],
        compiler_params=pltpu.CompilerParams(vmem_limit_bytes=32 << 20),
        name="krylov",
    )(moments, vectors, *edges, first, second, masks, voxel_feats, voxel_reg)


def finish_kernel(shared_ref, basis_ref, solution_ref, residual_ref):
    shared = shared_ref[...]
    lane = lax.broadcasted_iota(jnp.int32, (1, LANES), 1)

    def pick(row, k):
        return jnp.sum(jnp.where(lane == k, row, 0.0), axis=1, keepdims=True)

    largest = jnp.max(shared, axis=0, keepdims=True)
    smallest = jnp.min(shared, axis=0, keepdims=True)
    scale = [pick(largest, 10 + k) for k in range(4)]
    inverse = [pick(smallest, 14 + k) for k in range(4)]
    weight = [shared[:, 10 + k : 11 + k] * inverse[k] for k in range(4)]
    left = jnp.zeros_like(shared)
    right = jnp.zeros_like(shared)
    for k, (a, b) in enumerate(PAIRS):
        left = jnp.where(lane == k, weight[a], left)
        right = jnp.where(lane == k, weight[b], right)
    total = jnp.sum(shared * left * right, axis=0, keepdims=True)
    gram = [[None] * 4 for _ in range(4)]
    for k, (a, b) in enumerate(PAIRS):
        gram[a][b] = gram[b][a] = pick(total, k)
    growth = [scale[k + 1] * inverse[k] for k in range(3)]

    def product(left, right):
        terms = [
            left[a] * right[b] * gram[a][b]
            for a in range(4)
            for b in range(4)
            if left[a] is not None and right[b] is not None
        ]
        return functools.reduce(jnp.add, terms)

    def plus(left, factor, right):
        out = []
        for a, b in zip(left, right):
            out.append(a if b is None else factor * b if a is None else a + factor * b)
        return out

    def image(vector):
        return [None] + [None if vector[k] is None else vector[k] * growth[k] for k in range(3)]

    solution = [None] * 4
    residual = [jnp.ones((1, 1), jnp.float32), None, None, None]
    direction = list(residual)
    norm_now = product(residual, residual)
    for iteration in range(ITERS):
        carried = image(direction)
        alpha = norm_now / product(direction, carried)
        solution = plus(solution, alpha, direction)
        residual = plus(residual, -alpha, carried)
        if iteration + 1 < ITERS:
            norm_next = product(residual, residual)
            direction = plus(residual, norm_next / norm_now, direction)
            norm_now = norm_next
    back = [scale[0] * inverse[k] for k in range(4)]
    for out_ref, coefficients in ((solution_ref, solution), (residual_ref, residual)):
        total = None
        for k, c in enumerate(coefficients):
            if c is not None:
                term = (c * back[k]) * basis_ref[k]
                total = term if total is None else total + term
        out_ref[...] = total


def finish(shared, basis):
    _, bricks, voxels = basis.shape
    out = jax.ShapeDtypeStruct((bricks, voxels), jnp.float32)
    return pl.pallas_call(finish_kernel, out_shape=(out, out), name="finish")(shared, basis)


def shards(point_feats, point_targets, point_lists, brick_adjacency, voxel_feats, voxel_reg):
    feat_count = point_feats.shape[0]
    brick_total, slots = point_lists.shape
    local_bricks = voxel_feats.shape[0]
    devices = brick_total // local_bricks
    sending = pack(point_feats, point_targets, point_lists, devices)
    got = lax.all_to_all(sending, GX_GY, split_axis=0, concat_axis=0, tiled=True)

    first, second, third, lanes = prepare(voxel_feats, voxel_reg)
    mask = (brick_adjacency >= 0).astype(jnp.float32)
    mask = jnp.concatenate([mask, jnp.sum(mask, axis=1, keepdims=True)], axis=1)
    mask = jnp.pad(mask, ((0, 0), (0, LANES - 5)))
    early = (first, second, mask)
    low, high = swap(*along_messages(EARLY, early), GX)
    below, above = swap(*relay(EARLY, early, low, high, "relay_early"), "gy")
    first_lanes, second_lanes, mask_lanes = gather_early(first, second, mask, (low, high, below, above))

    got_feats = got[:, : 2 * feat_count].reshape(devices, 2, feat_count, local_bricks // 2, slots)
    got_targets = got[:, 2 * feat_count :].reshape(devices, 2, local_bricks // 2, slots)
    moments = jnp.einsum("shibc,shjbc->hbij", got_feats, got_feats, preferred_element_type=jnp.float32)
    moments = moments.reshape(local_bricks, 4, 8, feat_count).transpose(0, 2, 1, 3)
    moments = moments.reshape(local_bricks, 8, 4 * feat_count)
    gathered = jnp.einsum(
        "shbc,shibc->hbi", got_targets, got_feats, preferred_element_type=jnp.float32
    ).reshape(local_bricks, feat_count)

    vectors, to_low, to_high = begin(moments, gathered, lanes)
    low, high = swap(to_low, to_high, GX)
    below, above = swap(*relay(LATE, (moments, vectors), low, high, "relay_late"), "gy")
    basis, message = krylov(
        moments, vectors, (low, high, below, above), first_lanes, second_lanes, mask_lanes,
        voxel_feats, voxel_reg, devices,
    )
    shared = lax.all_to_all(message, GX_GY, split_axis=0, concat_axis=0, tiled=True)
    return finish(shared, basis)


def solution(mesh):
    torus = Mesh(mesh.devices.reshape(4, 4, 2, mesh.shape["gy"]), ("gx_0", "gx_1", "gx_2", "gy"))
    return jax.shard_map(
        shards,
        mesh=torus,
        in_specs=(
            P(None, GX_GY),
            P(GX_GY),
            P(GX_GY, None),
            P(GX_GY, None),
            P(GX_GY, None, None),
            P(GX_GY, None),
        ),
        out_specs=(P(GX_GY, None), P(GX_GY, None)),
        check_vma=False,
    )
```

```python
import functools

import jax
import jax.numpy as jnp
from jax import lax
from jax.experimental import pallas as pl
from jax.experimental.pallas import tpu as pltpu
from jax.sharding import Mesh
from jax.sharding import PartitionSpec as P

BX = 8
BY = 4
ITERS = 3
SLOTS = 8
LANES = 128
FEAT = 32
PITCH = 16
SPAN = 256
REACH = 3
GX_GY = ("gx_0", "gx_1", "gx_2", "gy")
GX = ("gx_0", "gx_1", "gx_2")
HIGHEST = lax.Precision.HIGHEST
PAIRS = tuple((a, b) for a in range(4) for b in range(a, 4))


coupling_weight = 1.0

EARLY = ((8, 2), (8, 1), (1, 2))
LATE = ((8, 2), (1, 3))


def padded(rows):
    return (rows + 7) // 8 * 8


def along_rows(section):
    return padded(section[0] * section[1] * BY)


def across_rows(section):
    rows, depth = section
    return padded(rows * sum(BX + 2 * (depth - k) for k in range(1, depth + 1)))


def message_rows(sections, size):
    return sum(size(section) for section in sections)


def piece(ref, start, rows, index):
    if rows == 8 and len(ref.shape) == 3:
        return ref[index]
    return ref[start + rows * index : start + rows * (index + 1), :]


def brick_at(own, low, high, start, section, a, e):
    rows, depth = section
    if a < 0:
        return piece(low, start, rows, (a + depth) * BY + e)
    if a >= BX:
        return piece(high, start, rows, (a - BX) * BY + e)
    return piece(own, 0, rows, a * BY + e)


def fill_across(sections, owns, low, high, to_low, to_high):
    source = target = 0
    for section, own in zip(sections, owns):
        rows, depth = section
        index = 0
        for away in range(1, depth + 1):
            extra = depth - away
            for a in range(-extra, BX + extra):
                place = slice(target + rows * index, target + rows * (index + 1))
                to_low[place, :] = brick_at(own, low, high, source, section, a, away - 1)
                to_high[place, :] = brick_at(own, low, high, source, section, a, BY - away)
                index += 1
        used, whole = rows * index, across_rows(section)
        if used < whole:
            blank = jnp.zeros((whole - used, LANES), jnp.float32)
            to_low[target + used : target + whole, :] = blank
            to_high[target + used : target + whole, :] = blank
        source += along_rows(section)
        target += whole


def place_bricks(put, sections, which, own, along_low, along_high, across_low, across_high):
    section = sections[which]
    rows, depth = section
    start = message_rows(sections[:which], along_rows)
    for a in range(-depth, BX + depth):
        for e in range(BY):
            put(a, e, brick_at(own, along_low, along_high, start, section, a, e))
    start = message_rows(sections[:which], across_rows)
    index = 0
    for away in range(1, depth + 1):
        extra = depth - away
        for a in range(-extra, BX + extra):
            put(a, -away, piece(across_low, start, rows, index))
            put(a, BY - 1 + away, piece(across_high, start, rows, index))
            index += 1


def lane_of(a, e):
    return (a + REACH) * PITCH + e + REACH


def to_lanes(records, lanes_ref):
    for t in range(8):
        lanes_ref[t * LANES : (t + 1) * LANES, :] = records[:, t, :].T


def times(matrix_ref, vector):
    total = None
    for t in range(8):
        for q in range(4):
            i = 8 * q + t
            row = t * LANES + q * FEAT
            term = matrix_ref[row : row + FEAT, :] * vector[i : i + 1, :]
            total = term if total is None else total + term
    return total


def pack_kernel(lists_ref, feats_ref, targets_ref, out_ref, mask_ref):
    rows = mask_ref.shape[0]
    width = LANES * SLOTS

    @pl.when(pl.program_id(0) == 0)
    def _():
        lane = lax.broadcasted_iota(jnp.int32, (SLOTS, LANES), 1)
        codes = []
        for block in range(rows):
            chosen = lists_ref[:, block * LANES : (block + 1) * LANES]
            offset = chosen - (lane + block * LANES) * SLOTS
            bits = jnp.where(chosen >= 0, lax.shift_left(1, jnp.clip(offset, 0, SLOTS - 1)), 0)
            codes.append(jnp.sum(bits, axis=0, keepdims=True))
        code = jnp.concatenate(codes, axis=0).astype(jnp.float32).astype(jnp.bfloat16)
        brick = lax.broadcasted_iota(jnp.int32, (LANES, width), 0)
        point = lax.broadcasted_iota(jnp.int32, (LANES, width), 1)
        spread = (lax.shift_right_logical(point, 3) == brick).astype(jnp.float32).astype(jnp.bfloat16)
        wide = jnp.dot(code, spread, preferred_element_type=jnp.float32).astype(jnp.int32)
        slot = lax.broadcasted_iota(jnp.int32, (rows, width), 1) & (SLOTS - 1)
        mask_ref[...] = (lax.shift_right_logical(wide, slot) & 1).astype(jnp.float32)

    step = pl.program_id(0)
    dests = out_ref.shape[0]
    feat_count = feats_ref.shape[0]
    for part in range(dests * 256 // width):
        row = mask_ref[pl.ds(step * (dests * 256 // width) + part, 1), :].astype(jnp.bfloat16)
        masked = feats_ref[:, part * width : (part + 1) * width] * row
        for half_block in range(width // LANES):
            dest = (part * width + half_block * LANES) // 256
            half = half_block % 2
            out_ref[dest, half * feat_count : (half + 1) * feat_count, :] = masked[
                :, half_block * LANES : (half_block + 1) * LANES
            ]
    for dest in range(dests):
        out_ref[dest, 2 * feat_count : 2 * feat_count + 2, :] = targets_ref[2 * dest : 2 * dest + 2, :]


def pack(point_feats, point_targets, point_lists, devices):
    feat_count, points = point_feats.shape
    bricks = point_lists.shape[0]
    steps = 8
    dests = devices // steps
    return pl.pallas_call(
        pack_kernel,
        grid=(steps,),
        in_specs=[
            pl.BlockSpec((SLOTS, bricks), lambda i: (0, 0)),
            pl.BlockSpec((feat_count, points // steps), lambda i: (0, i)),
            pl.BlockSpec((points // steps // LANES, LANES), lambda i: (i, 0)),
        ],
        out_specs=pl.BlockSpec((dests, 2 * feat_count + 2, LANES), lambda i: (i, 0, 0)),
        out_shape=jax.ShapeDtypeStruct((devices, 2 * feat_count + 2, LANES), jnp.bfloat16),
        scratch_shapes=[pltpu.VMEM((bricks // LANES, LANES * SLOTS), jnp.float32)],
        name="pack",
    )(point_lists.T, point_feats, point_targets.reshape(points // LANES, LANES))


def prepare_kernel(feats_ref, reg_ref, first_ref, second_ref, third_ref, lanes_ref):
    records = (first_ref, second_ref, third_ref)

    def one(b, carry):
        feats = feats_ref[b]
        reg = reg_ref[pl.ds(b, 1), :]
        once = feats * reg
        left = jnp.concatenate([feats, once, once * reg], axis=0)
        product = lax.dot_general(
            left,
            feats,
            (((1,), (1,)), ((), ())),
            precision=HIGHEST,
            preferred_element_type=jnp.float32,
        )
        for power, record in enumerate(records):
            rows = [product[power * FEAT + 8 * q : power * FEAT + 8 * q + 8, :] for q in range(4)]
            record[b] = jnp.concatenate(rows, axis=1)
        return carry

    lax.fori_loop(0, feats_ref.shape[0], one, 0)
    for power, record in enumerate(records):
        for t in range(8):
            block = jnp.concatenate([record[:, t, :], jnp.zeros((96, LANES), jnp.float32)], axis=0)
            lanes_ref[power, t * LANES : (t + 1) * LANES, :] = block.T


def prepare(voxel_feats, voxel_reg):
    bricks = voxel_feats.shape[0]
    record = jax.ShapeDtypeStruct((bricks, 8, LANES), jnp.float32)
    return pl.pallas_call(
        prepare_kernel,
        out_shape=(record, record, record, jax.ShapeDtypeStruct((3, 8 * LANES, LANES), jnp.float32)),
        compiler_params=pltpu.CompilerParams(vmem_limit_bytes=24 << 20),
        cost_estimate=pl.CostEstimate(flops=600_000_000, bytes_accessed=5_000_000, transcendentals=0),
        name="prepare",
    )(voxel_feats, voxel_reg)


def gather_early_kernel(
    first_ref, second_ref, mask_ref, low_ref, high_ref, below_ref, above_ref,
    first_lanes, second_lanes, mask_lanes, first_store, second_store, mask_store,
):
    for store in (first_store, second_store, mask_store):
        store[...] = jnp.zeros_like(store)

    def put(store):
        def write(a, e, value):
            if len(store.shape) == 3:
                store[lane_of(a, e)] = value
            else:
                store[lane_of(a, e) : lane_of(a, e) + 1, :] = value

        return write

    edges = (low_ref, high_ref, below_ref, above_ref)
    place_bricks(put(first_store), EARLY, 0, first_ref, *edges)
    place_bricks(put(second_store), EARLY, 1, second_ref, *edges)
    place_bricks(put(mask_store), EARLY, 2, mask_ref, *edges)
    to_lanes(first_store, first_lanes)
    to_lanes(second_store, second_lanes)
    mask_lanes[...] = mask_store[...].T[:8, :]


def gather_early(first, second, mask, edges):
    lanes = jax.ShapeDtypeStruct((8 * LANES, SPAN), jnp.float32)
    return pl.pallas_call(
        gather_early_kernel,
        out_shape=(lanes, lanes, jax.ShapeDtypeStruct((8, SPAN), jnp.float32)),
        scratch_shapes=[
            pltpu.VMEM((SPAN, 8, LANES), jnp.float32),
            pltpu.VMEM((SPAN, 8, LANES), jnp.float32),
            pltpu.VMEM((SPAN, LANES), jnp.float32),
        ],
        compiler_params=pltpu.CompilerParams(vmem_limit_bytes=24 << 20),
        cost_estimate=pl.CostEstimate(flops=2_000_000, bytes_accessed=3_000_000, transcendentals=0),
        name="gather_early",
    )(first, second, mask, *edges)


def relay_kernel(sections, count, *refs):
    owns, low, high, to_low, to_high = refs[:count], *refs[count:]
    fill_across(sections, owns, low, high, to_low, to_high)


def relay(sections, owns, low, high, name):
    out = jax.ShapeDtypeStruct((message_rows(sections, across_rows), LANES), jnp.float32)
    return pl.pallas_call(
        functools.partial(relay_kernel, sections, len(owns)),
        out_shape=(out, out),
        name=name,
    )(*owns, low, high)


def along_messages(sections, owns):
    to_low, to_high = [], []
    for (rows, depth), own in zip(sections, owns):
        flat = own.reshape(-1, LANES)
        used = rows * depth * BY
        blank = ((0, padded(used) - used), (0, 0))
        to_low.append(jnp.pad(flat[:used], blank))
        to_high.append(jnp.pad(flat[flat.shape[0] - used :], blank))
    return jnp.concatenate(to_low), jnp.concatenate(to_high)


def swap(to_low, to_high, axis):
    count = lax.axis_size(axis)
    up = [(i, i + 1) for i in range(count - 1)]
    down = [(b, a) for a, b in up]
    return lax.ppermute(to_high, axis, up), lax.ppermute(to_low, axis, down)


def begin_kernel(moments_ref, gathered_ref, lanes_ref, vectors_ref, low_ref, high_ref):
    values = jnp.concatenate(
        [gathered_ref[...], jnp.zeros((LANES - gathered_ref.shape[0], FEAT), jnp.float32)], axis=0
    )
    values = jnp.concatenate([values, jnp.zeros((LANES, LANES - FEAT), jnp.float32)], axis=1).T[:FEAT, :]
    applied = [times(lanes_ref.at[power], values) for power in range(3)]
    vectors = jnp.concatenate([*applied, values], axis=0).T
    vectors_ref[...] = vectors[: vectors_ref.shape[0], :]
    depth = LATE[0][1] * BY
    for k in range(depth):
        low_ref[8 * k : 8 * k + 8, :] = moments_ref[k]
        high_ref[8 * k : 8 * k + 8, :] = moments_ref[BX * BY - depth + k]
    deep = LATE[1][1] * BY
    blank = jnp.zeros((padded(deep) - deep, LANES), jnp.float32)
    low_ref[8 * depth :, :] = jnp.concatenate([vectors[:deep], blank], axis=0)
    high_ref[8 * depth :, :] = jnp.concatenate([vectors[BX * BY - deep : BX * BY], blank], axis=0)


def begin(moments, gathered, lanes):
    message = jax.ShapeDtypeStruct((message_rows(LATE, along_rows), LANES), jnp.float32)
    return pl.pallas_call(
        begin_kernel,
        out_shape=(jax.ShapeDtypeStruct((gathered.shape[0], LANES), jnp.float32), message, message),
        name="begin",
    )(moments, gathered, lanes)


def power_of_two(value):
    scale = jnp.ones_like(value)
    inverse = jnp.ones_like(value)
    for k in (64, 32, 16, 8, 4, 2, 1):
        up, down = 2.0**k, 2.0**-k
        large = value * down >= 1.0
        small = value * up <= 1.0
        value = jnp.where(large, value * down, jnp.where(small, value * up, value))
        scale = jnp.where(large, scale * up, jnp.where(small, scale * down, scale))
        inverse = jnp.where(large, inverse * down, jnp.where(small, inverse * up, inverse))
    return scale, inverse


def krylov_kernel(
    moments_ref, vectors_ref, low_ref, high_ref, below_ref, above_ref, first_ref, second_ref, mask_ref,
    feats_ref, reg_ref, basis_ref, message_ref, moment_store, vector_store, moment_lanes,
):
    moment_store[...] = jnp.zeros_like(moment_store)
    vector_store[...] = jnp.zeros_like(vector_store)

    def put_moment(a, e, value):
        moment_store[lane_of(a, e)] = value

    def put_vector(a, e, value):
        vector_store[lane_of(a, e) : lane_of(a, e) + 1, :] = value

    edges = (low_ref, high_ref, below_ref, above_ref)
    place_bricks(put_moment, LATE, 0, moments_ref, *edges)
    place_bricks(put_vector, LATE, 1, vectors_ref, *edges)
    to_lanes(moment_store, moment_lanes)
    vectors = vector_store[...].T
    masks = mask_ref[...]

    def system(z):
        near = masks[0:1] * pltpu.roll(z, PITCH, 1) + masks[1:2] * pltpu.roll(z, SPAN - PITCH, 1)
        near = near + masks[2:3] * pltpu.roll(z, 1, 1) + masks[3:4] * pltpu.roll(z, SPAN - 1, 1)
        return times(moment_lanes, z) + coupling_weight * (masks[4:5] * z - near)

    one = system(vectors[0:FEAT])
    two = system(times(first_ref, one) + vectors[FEAT : 2 * FEAT])
    three = system(times(first_ref, two) + times(second_ref, one) + vectors[2 * FEAT : 3 * FEAT])
    chain = (vectors[3 * FEAT :], one, two, three)
    for b in range(BX * BY):
        lane = lane_of(b // BY, b % BY)
        feats = feats_ref[b]
        for step, values in enumerate(chain):
            basis_ref[step, b : b + 1, :] = jnp.sum(feats * values[:, lane : lane + 1], axis=0, keepdims=True)
    reg = reg_ref[...]
    basis = [basis_ref[0]]
    for step in range(1, 4):
        basis.append(basis_ref[step] + reg * basis[-1])
        basis_ref[step] = basis[-1]

    def folded(x, combine):
        rows = [x[8 * k : 8 * k + 8, :] for k in range(x.shape[0] // 8)]
        parts = [r[:, LANES * k : LANES * (k + 1)] for r in rows for k in range(x.shape[1] // LANES)]
        while len(parts) > 1:
            parts = [combine(parts[k], parts[k + 1]) for k in range(0, len(parts), 2)]
        return parts[0]

    peaks = [jnp.max(folded(jnp.abs(v), jnp.maximum), axis=0, keepdims=True) for v in basis]
    peaks = jnp.max(jnp.concatenate(peaks + peaks, axis=0), axis=1, keepdims=True)
    scale, inverse = power_of_two(jnp.broadcast_to(peaks, (8, LANES)))
    scaled = [v * inverse[k : k + 1, 0:1] for k, v in enumerate(basis)]
    sums = [jnp.sum(folded(scaled[a] * scaled[b], jnp.add), axis=0, keepdims=True) for a, b in PAIRS]
    sums = jnp.concatenate(sums + [jnp.zeros((16 - len(PAIRS), LANES), jnp.float32)], axis=0)
    sums = jnp.sum(sums, axis=1, keepdims=True)
    lane = lax.broadcasted_iota(jnp.int32, (1, LANES), 1)
    row = jnp.zeros((1, LANES), jnp.float32)
    for k in range(len(PAIRS)):
        row = jnp.where(lane == k, sums[k : k + 1, :], row)
    for k in range(4):
        row = jnp.where(lane == 10 + k, scale[k : k + 1, :], row)
        row = jnp.where(lane == 14 + k, inverse[k : k + 1, :], row)
    message_ref[...] = jnp.broadcast_to(row, message_ref.shape)


def krylov(moments, vectors, edges, first, second, masks, voxel_feats, voxel_reg, devices):
    bricks, _, voxels = voxel_feats.shape
    return pl.pallas_call(
        krylov_kernel,
        out_shape=(
            jax.ShapeDtypeStruct((4, bricks, voxels), jnp.float32),
            jax.ShapeDtypeStruct((devices, LANES), jnp.float32),
        ),
        scratch_shapes=[
            pltpu.VMEM((SPAN, 8, LANES), jnp.float32),
            pltpu.VMEM((SPAN, LANES), jnp.float32),
            pltpu.VMEM((8 * LANES, SPAN), jnp.float32),
        ],
        compiler_params=pltpu.CompilerParams(vmem_limit_bytes=32 << 20),
        name="krylov",
    )(moments, vectors, *edges, first, second, masks, voxel_feats, voxel_reg)


def finish_kernel(shared_ref, basis_ref, solution_ref, residual_ref):
    shared = shared_ref[...]
    lane = lax.broadcasted_iota(jnp.int32, (1, LANES), 1)

    def pick(row, k):
        return jnp.sum(jnp.where(lane == k, row, 0.0), axis=1, keepdims=True)

    largest = jnp.max(shared, axis=0, keepdims=True)
    smallest = jnp.min(shared, axis=0, keepdims=True)
    scale = [pick(largest, 10 + k) for k in range(4)]
    inverse = [pick(smallest, 14 + k) for k in range(4)]
    weight = [shared[:, 10 + k : 11 + k] * inverse[k] for k in range(4)]
    left = jnp.zeros_like(shared)
    right = jnp.zeros_like(shared)
    for k, (a, b) in enumerate(PAIRS):
        left = jnp.where(lane == k, weight[a], left)
        right = jnp.where(lane == k, weight[b], right)
    total = jnp.sum(shared * left * right, axis=0, keepdims=True)
    gram = [[None] * 4 for _ in range(4)]
    for k, (a, b) in enumerate(PAIRS):
        gram[a][b] = gram[b][a] = pick(total, k)
    growth = [scale[k + 1] * inverse[k] for k in range(3)]

    def product(left, right):
        terms = [
            left[a] * right[b] * gram[a][b]
            for a in range(4)
            for b in range(4)
            if left[a] is not None and right[b] is not None
        ]
        return functools.reduce(jnp.add, terms)

    def plus(left, factor, right):
        out = []
        for a, b in zip(left, right):
            out.append(a if b is None else factor * b if a is None else a + factor * b)
        return out

    def image(vector):
        return [None] + [None if vector[k] is None else vector[k] * growth[k] for k in range(3)]

    solution = [None] * 4
    residual = [jnp.ones((1, 1), jnp.float32), None, None, None]
    direction = list(residual)
    norm_now = product(residual, residual)
    for iteration in range(ITERS):
        carried = image(direction)
        alpha = norm_now / product(direction, carried)
        solution = plus(solution, alpha, direction)
        residual = plus(residual, -alpha, carried)
        if iteration + 1 < ITERS:
            norm_next = product(residual, residual)
            direction = plus(residual, norm_next / norm_now, direction)
            norm_now = norm_next
    back = [scale[0] * inverse[k] for k in range(4)]
    for out_ref, coefficients in ((solution_ref, solution), (residual_ref, residual)):
        total = None
        for k, c in enumerate(coefficients):
            if c is not None:
                term = (c * back[k]) * basis_ref[k]
                total = term if total is None else total + term
        out_ref[...] = total


def finish(shared, basis):
    _, bricks, voxels = basis.shape
    out = jax.ShapeDtypeStruct((bricks, voxels), jnp.float32)
    return pl.pallas_call(finish_kernel, out_shape=(out, out), name="finish")(shared, basis)


def shards(point_feats, point_targets, point_lists, brick_adjacency, voxel_feats, voxel_reg):
    feat_count = point_feats.shape[0]
    brick_total, slots = point_lists.shape
    local_bricks = voxel_feats.shape[0]
    devices = brick_total // local_bricks
    sending = pack(point_feats, point_targets, point_lists, devices)
    got = lax.all_to_all(sending, GX_GY, split_axis=0, concat_axis=0, tiled=True)

    first, second, third, lanes = prepare(voxel_feats, voxel_reg)
    mask = (brick_adjacency >= 0).astype(jnp.float32)
    mask = jnp.concatenate([mask, jnp.sum(mask, axis=1, keepdims=True)], axis=1)
    mask = jnp.pad(mask, ((0, 0), (0, LANES - 5)))
    early = (first, second, mask)
    low, high = swap(*along_messages(EARLY, early), GX)
    below, above = swap(*relay(EARLY, early, low, high, "relay_early"), "gy")
    first_lanes, second_lanes, mask_lanes = gather_early(first, second, mask, (low, high, below, above))
    got, first_lanes, second_lanes, mask_lanes = lax.optimization_barrier(
        (got, first_lanes, second_lanes, mask_lanes)
    )

    got_feats = got[:, : 2 * feat_count].reshape(devices, 2, feat_count, local_bricks // 2, slots)
    got_targets = got[:, 2 * feat_count :].reshape(devices, 2, local_bricks // 2, slots)
    moments = jnp.einsum("shibc,shjbc->hbij", got_feats, got_feats, preferred_element_type=jnp.float32)
    moments = moments.reshape(local_bricks, 4, 8, feat_count).transpose(0, 2, 1, 3)
    moments = moments.reshape(local_bricks, 8, 4 * feat_count)
    gathered = jnp.einsum(
        "shbc,shibc->hbi", got_targets, got_feats, preferred_element_type=jnp.float32
    ).reshape(local_bricks, feat_count)

    vectors, to_low, to_high = begin(moments, gathered, lanes)
    low, high = swap(to_low, to_high, GX)
    below, above = swap(*relay(LATE, (moments, vectors), low, high, "relay_late"), "gy")
    basis, message = krylov(
        moments, vectors, (low, high, below, above), first_lanes, second_lanes, mask_lanes,
        voxel_feats, voxel_reg, devices,
    )
    shared = lax.all_to_all(message, GX_GY, split_axis=0, concat_axis=0, tiled=True)
    return finish(shared, basis)


def solution(mesh):
    torus = Mesh(mesh.devices.reshape(4, 4, 2, mesh.shape["gy"]), ("gx_0", "gx_1", "gx_2", "gy"))
    return jax.shard_map(
        shards,
        mesh=torus,
        in_specs=(
            P(None, GX_GY),
            P(GX_GY),
            P(GX_GY, None),
            P(GX_GY, None),
            P(GX_GY, None, None),
            P(GX_GY, None),
        ),
        out_specs=(P(GX_GY, None), P(GX_GY, None)),
        check_vma=False,
    )
```

```python
import functools

import jax
import jax.numpy as jnp
from jax import lax
from jax.experimental import pallas as pl
from jax.experimental.pallas import tpu as pltpu
from jax.sharding import Mesh
from jax.sharding import PartitionSpec as P

BX = 8
BY = 4
ITERS = 3
SLOTS = 8
LANES = 128
FEAT = 32
PITCH = 16
SPAN = 256
REACH = 3
GX_GY = ("gx_0", "gx_1", "gx_2", "gy")
GX = ("gx_0", "gx_1", "gx_2")
HIGHEST = lax.Precision.HIGHEST
PAIRS = tuple((a, b) for a in range(4) for b in range(a, 4))


coupling_weight = 1.0

EARLY = ((8, 2), (8, 1), (1, 2))
LATE = ((8, 2), (1, 3))


def padded(rows):
    return (rows + 7) // 8 * 8


def along_rows(section):
    return padded(section[0] * section[1] * BY)


def across_rows(section):
    rows, depth = section
    return padded(rows * sum(BX + 2 * (depth - k) for k in range(1, depth + 1)))


def message_rows(sections, size):
    return sum(size(section) for section in sections)


def piece(ref, start, rows, index):
    if rows == 8 and len(ref.shape) == 3:
        return ref[index]
    return ref[start + rows * index : start + rows * (index + 1), :]


def brick_at(own, low, high, start, section, a, e):
    rows, depth = section
    if a < 0:
        return piece(low, start, rows, (a + depth) * BY + e)
    if a >= BX:
        return piece(high, start, rows, (a - BX) * BY + e)
    return piece(own, 0, rows, a * BY + e)


def fill_across(sections, owns, low, high, to_low, to_high):
    source = target = 0
    for section, own in zip(sections, owns):
        rows, depth = section
        index = 0
        for away in range(1, depth + 1):
            extra = depth - away
            for a in range(-extra, BX + extra):
                place = slice(target + rows * index, target + rows * (index + 1))
                to_low[place, :] = brick_at(own, low, high, source, section, a, away - 1)
                to_high[place, :] = brick_at(own, low, high, source, section, a, BY - away)
                index += 1
        used, whole = rows * index, across_rows(section)
        if used < whole:
            blank = jnp.zeros((whole - used, LANES), jnp.float32)
            to_low[target + used : target + whole, :] = blank
            to_high[target + used : target + whole, :] = blank
        source += along_rows(section)
        target += whole


def place_bricks(put, sections, which, own, along_low, along_high, across_low, across_high):
    section = sections[which]
    rows, depth = section
    start = message_rows(sections[:which], along_rows)
    for a in range(-depth, BX + depth):
        for e in range(BY):
            put(a, e, brick_at(own, along_low, along_high, start, section, a, e))
    start = message_rows(sections[:which], across_rows)
    index = 0
    for away in range(1, depth + 1):
        extra = depth - away
        for a in range(-extra, BX + extra):
            put(a, -away, piece(across_low, start, rows, index))
            put(a, BY - 1 + away, piece(across_high, start, rows, index))
            index += 1


def lane_of(a, e):
    return (a + REACH) * PITCH + e + REACH


def to_lanes(records, lanes_ref):
    for t in range(8):
        lanes_ref[t * LANES : (t + 1) * LANES, :] = records[:, t, :].T


def times(matrix_ref, vector):
    total = None
    for t in range(8):
        for q in range(4):
            i = 8 * q + t
            row = t * LANES + q * FEAT
            term = matrix_ref[row : row + FEAT, :] * vector[i : i + 1, :]
            total = term if total is None else total + term
    return total


def pack_kernel(lists_ref, feats_ref, targets_ref, out_ref, mask_ref):
    rows = mask_ref.shape[0]
    width = LANES * SLOTS

    @pl.when(pl.program_id(0) == 0)
    def _():
        lane = lax.broadcasted_iota(jnp.int32, (SLOTS, LANES), 1)
        codes = []
        for block in range(rows):
            chosen = lists_ref[:, block * LANES : (block + 1) * LANES]
            offset = chosen - (lane + block * LANES) * SLOTS
            bits = jnp.where(chosen >= 0, lax.shift_left(1, jnp.clip(offset, 0, SLOTS - 1)), 0)
            codes.append(jnp.sum(bits, axis=0, keepdims=True))
        code = jnp.concatenate(codes, axis=0).astype(jnp.float32).astype(jnp.bfloat16)
        brick = lax.broadcasted_iota(jnp.int32, (LANES, width), 0)
        point = lax.broadcasted_iota(jnp.int32, (LANES, width), 1)
        spread = (lax.shift_right_logical(point, 3) == brick).astype(jnp.float32).astype(jnp.bfloat16)
        wide = jnp.dot(code, spread, preferred_element_type=jnp.float32).astype(jnp.int32)
        slot = lax.broadcasted_iota(jnp.int32, (rows, width), 1) & (SLOTS - 1)
        mask_ref[...] = (lax.shift_right_logical(wide, slot) & 1).astype(jnp.float32)

    step = pl.program_id(0)
    dests = out_ref.shape[0]
    feat_count = feats_ref.shape[0]
    for part in range(dests * 256 // width):
        row = mask_ref[pl.ds(step * (dests * 256 // width) + part, 1), :].astype(jnp.bfloat16)
        masked = feats_ref[:, part * width : (part + 1) * width] * row
        for half_block in range(width // LANES):
            dest = (part * width + half_block * LANES) // 256
            half = half_block % 2
            out_ref[dest, half * feat_count : (half + 1) * feat_count, :] = masked[
                :, half_block * LANES : (half_block + 1) * LANES
            ]
    for dest in range(dests):
        out_ref[dest, 2 * feat_count : 2 * feat_count + 2, :] = targets_ref[2 * dest : 2 * dest + 2, :]


def pack(point_feats, point_targets, point_lists, devices):
    feat_count, points = point_feats.shape
    bricks = point_lists.shape[0]
    steps = 8
    dests = devices // steps
    return pl.pallas_call(
        pack_kernel,
        grid=(steps,),
        in_specs=[
            pl.BlockSpec((SLOTS, bricks), lambda i: (0, 0)),
            pl.BlockSpec((feat_count, points // steps), lambda i: (0, i)),
            pl.BlockSpec((points // steps // LANES, LANES), lambda i: (i, 0)),
        ],
        out_specs=pl.BlockSpec((dests, 2 * feat_count + 2, LANES), lambda i: (i, 0, 0)),
        out_shape=jax.ShapeDtypeStruct((devices, 2 * feat_count + 2, LANES), jnp.bfloat16),
        scratch_shapes=[pltpu.VMEM((bricks // LANES, LANES * SLOTS), jnp.float32)],
        name="pack",
    )(point_lists.T, point_feats, point_targets.reshape(points // LANES, LANES))


def prepare_kernel(feats_ref, reg_ref, first_ref, second_ref, third_ref, lanes_ref):
    records = (first_ref, second_ref, third_ref)

    def one(b, carry):
        feats = feats_ref[b]
        reg = reg_ref[pl.ds(b, 1), :]
        once = feats * reg
        left = jnp.concatenate([feats, once, once * reg], axis=0)
        product = lax.dot_general(
            left,
            feats,
            (((1,), (1,)), ((), ())),
            precision=HIGHEST,
            preferred_element_type=jnp.float32,
        )
        for power, record in enumerate(records):
            rows = [product[power * FEAT + 8 * q : power * FEAT + 8 * q + 8, :] for q in range(4)]
            record[b] = jnp.concatenate(rows, axis=1)
        return carry

    lax.fori_loop(0, feats_ref.shape[0], one, 0)
    for power, record in enumerate(records):
        for t in range(8):
            block = jnp.concatenate([record[:, t, :], jnp.zeros((96, LANES), jnp.float32)], axis=0)
            lanes_ref[power, t * LANES : (t + 1) * LANES, :] = block.T


def prepare(voxel_feats, voxel_reg):
    bricks = voxel_feats.shape[0]
    record = jax.ShapeDtypeStruct((bricks, 8, LANES), jnp.float32)
    return pl.pallas_call(
        prepare_kernel,
        out_shape=(record, record, record, jax.ShapeDtypeStruct((3, 8 * LANES, LANES), jnp.float32)),
        compiler_params=pltpu.CompilerParams(vmem_limit_bytes=24 << 20),
        cost_estimate=pl.CostEstimate(flops=600_000_000, bytes_accessed=5_000_000, transcendentals=0),
        name="prepare",
    )(voxel_feats, voxel_reg)


def gather_early_kernel(
    first_ref, second_ref, mask_ref, low_ref, high_ref, below_ref, above_ref,
    first_lanes, second_lanes, mask_lanes, first_store, second_store, mask_store,
):
    for store in (first_store, second_store, mask_store):
        store[...] = jnp.zeros_like(store)

    def put(store):
        def write(a, e, value):
            if len(store.shape) == 3:
                store[lane_of(a, e)] = value
            else:
                store[lane_of(a, e) : lane_of(a, e) + 1, :] = value

        return write

    edges = (low_ref, high_ref, below_ref, above_ref)
    place_bricks(put(first_store), EARLY, 0, first_ref, *edges)
    place_bricks(put(second_store), EARLY, 1, second_ref, *edges)
    place_bricks(put(mask_store), EARLY, 2, mask_ref, *edges)
    to_lanes(first_store, first_lanes)
    to_lanes(second_store, second_lanes)
    mask_lanes[...] = mask_store[...].T[:8, :]


def gather_early(first, second, mask, edges):
    lanes = jax.ShapeDtypeStruct((8 * LANES, SPAN), jnp.float32)
    return pl.pallas_call(
        gather_early_kernel,
        out_shape=(lanes, lanes, jax.ShapeDtypeStruct((8, SPAN), jnp.float32)),
        scratch_shapes=[
            pltpu.VMEM((SPAN, 8, LANES), jnp.float32),
            pltpu.VMEM((SPAN, 8, LANES), jnp.float32),
            pltpu.VMEM((SPAN, LANES), jnp.float32),
        ],
        compiler_params=pltpu.CompilerParams(vmem_limit_bytes=24 << 20),
        cost_estimate=pl.CostEstimate(flops=2_000_000, bytes_accessed=3_000_000, transcendentals=0),
        name="gather_early",
    )(first, second, mask, *edges)


def relay_kernel(sections, count, *refs):
    owns, low, high, to_low, to_high = refs[:count], *refs[count:]
    fill_across(sections, owns, low, high, to_low, to_high)


def relay(sections, owns, low, high, name):
    out = jax.ShapeDtypeStruct((message_rows(sections, across_rows), LANES), jnp.float32)
    return pl.pallas_call(
        functools.partial(relay_kernel, sections, len(owns)),
        out_shape=(out, out),
        name=name,
    )(*owns, low, high)


def along_messages(sections, owns):
    to_low, to_high = [], []
    for (rows, depth), own in zip(sections, owns):
        flat = own.reshape(-1, LANES)
        used = rows * depth * BY
        blank = ((0, padded(used) - used), (0, 0))
        to_low.append(jnp.pad(flat[:used], blank))
        to_high.append(jnp.pad(flat[flat.shape[0] - used :], blank))
    return jnp.concatenate(to_low), jnp.concatenate(to_high)


def swap(to_low, to_high, axis):
    count = lax.axis_size(axis)
    up = [(i, i + 1) for i in range(count - 1)]
    down = [(b, a) for a, b in up]
    return lax.ppermute(to_high, axis, up), lax.ppermute(to_low, axis, down)


def moments_kernel(got_ref, lanes_ref, moments_ref, vectors_ref, low_ref, high_ref, turned, sums):
    step = pl.program_id(0)
    sources = got_ref.shape[0]

    @pl.when(step == 0)
    def _():
        sums[...] = jnp.zeros_like(sums)

    for group in range(sources // 4):
        for half in range(2):
            block = got_ref[4 * group : 4 * group + 4, half * FEAT : (half + 1) * FEAT, :]
            turned[half, step * (sources // 4) + group] = block.reshape(LANES, LANES).T
    for half in range(2):
        total = sums[half]
        for source in range(sources):
            feats = got_ref[source, half * FEAT : (half + 1) * FEAT, :].astype(jnp.float32)
            target = got_ref[source, 2 * FEAT : 2 * FEAT + 2, :].astype(jnp.float32)
            total = total + feats * target[half : half + 1, :]
        sums[half] = total

    @pl.when(step == pl.num_programs(0) - 1)
    def _():
        groups = turned.shape[1]
        row = lax.broadcasted_iota(jnp.int32, (1, 16, LANES), 1)
        upper = (row < SLOTS).astype(jnp.float32).astype(jnp.bfloat16)
        lower = (row >= SLOTS).astype(jnp.float32).astype(jnp.bfloat16)
        lane_group = lax.broadcasted_iota(jnp.int32, (1, LANES), 1) // FEAT
        for half in range(2):
            for pair in range(8):
                points = turned[half, :, 16 * pair : 16 * pair + 16, :]
                left = points.reshape(groups * 16, LANES)
                right = jnp.concatenate(
                    [(points * upper).reshape(groups * 16, LANES), (points * lower).reshape(groups * 16, LANES)],
                    axis=1,
                )
                product = lax.dot_general(
                    left, right, (((0,), (0,)), ((), ())), preferred_element_type=jnp.float32
                )
                for k in range(2):
                    square = product[:, k * LANES : (k + 1) * LANES]
                    own = jnp.zeros((FEAT, LANES), jnp.float32)
                    for q in range(4):
                        own = own + jnp.where(lane_group == q, square[q * FEAT : (q + 1) * FEAT, :], 0.0)
                    own = own + pltpu.roll(own, 64, 1)
                    own = own + pltpu.roll(own, 32, 1)
                    record = own[0:8, :]
                    for q in range(1, 4):
                        record = jnp.where(lane_group == q, own[8 * q : 8 * q + 8, :], record)
                    moments_ref[half * 16 + 2 * pair + k] = record
        point = lax.broadcasted_iota(jnp.int32, (LANES, LANES), 0) // SLOTS
        lane = lax.broadcasted_iota(jnp.int32, (LANES, LANES), 1)
        values = jnp.zeros((FEAT, LANES), jnp.float32)
        for half in range(2):
            spread = (lane == point + half * 16).astype(jnp.float32)
            values = values + jnp.dot(
                sums[half], spread, precision=HIGHEST, preferred_element_type=jnp.float32
            )
        applied = [times(lanes_ref.at[power], values) for power in range(3)]
        vectors = jnp.concatenate([*applied, values], axis=0).T
        vectors_ref[...] = vectors[: BX * BY, :]
        depth = LATE[0][1] * BY
        for k in range(depth):
            low_ref[8 * k : 8 * k + 8, :] = moments_ref[k]
            high_ref[8 * k : 8 * k + 8, :] = moments_ref[BX * BY - depth + k]
        deep = LATE[1][1] * BY
        blank = jnp.zeros((padded(deep) - deep, LANES), jnp.float32)
        low_ref[8 * depth :, :] = jnp.concatenate([vectors[:deep], blank], axis=0)
        high_ref[8 * depth :, :] = jnp.concatenate([vectors[BX * BY - deep : BX * BY], blank], axis=0)


def find_moments(got, lanes):
    devices, rows, _ = got.shape
    steps = 4
    bricks = BX * BY
    message = message_rows(LATE, along_rows)
    return pl.pallas_call(
        moments_kernel,
        grid=(steps,),
        in_specs=[
            pl.BlockSpec((devices // steps, rows, LANES), lambda i: (i, 0, 0)),
            pl.BlockSpec(lanes.shape, lambda i: (0, 0, 0)),
        ],
        out_specs=(
            pl.BlockSpec((bricks, 8, LANES), lambda i: (0, 0, 0)),
            pl.BlockSpec((bricks, LANES), lambda i: (0, 0)),
            pl.BlockSpec((message, LANES), lambda i: (0, 0)),
            pl.BlockSpec((message, LANES), lambda i: (0, 0)),
        ),
        out_shape=(
            jax.ShapeDtypeStruct((bricks, 8, LANES), jnp.float32),
            jax.ShapeDtypeStruct((bricks, LANES), jnp.float32),
            jax.ShapeDtypeStruct((message, LANES), jnp.float32),
            jax.ShapeDtypeStruct((message, LANES), jnp.float32),
        ),
        scratch_shapes=[
            pltpu.VMEM((2, devices // 4, LANES, LANES), jnp.bfloat16),
            pltpu.VMEM((2, FEAT, LANES), jnp.float32),
        ],
        compiler_params=pltpu.CompilerParams(vmem_limit_bytes=20 << 20),
        name="moments",
    )(got, lanes)


def power_of_two(value):
    scale = jnp.ones_like(value)
    inverse = jnp.ones_like(value)
    for k in (64, 32, 16, 8, 4, 2, 1):
        up, down = 2.0**k, 2.0**-k
        large = value * down >= 1.0
        small = value * up <= 1.0
        value = jnp.where(large, value * down, jnp.where(small, value * up, value))
        scale = jnp.where(large, scale * up, jnp.where(small, scale * down, scale))
        inverse = jnp.where(large, inverse * down, jnp.where(small, inverse * up, inverse))
    return scale, inverse


def krylov_kernel(
    moments_ref, vectors_ref, low_ref, high_ref, below_ref, above_ref, first_ref, second_ref, mask_ref,
    feats_ref, reg_ref, basis_ref, message_ref, moment_store, vector_store, moment_lanes,
):
    moment_store[...] = jnp.zeros_like(moment_store)
    vector_store[...] = jnp.zeros_like(vector_store)

    def put_moment(a, e, value):
        moment_store[lane_of(a, e)] = value

    def put_vector(a, e, value):
        vector_store[lane_of(a, e) : lane_of(a, e) + 1, :] = value

    edges = (low_ref, high_ref, below_ref, above_ref)
    place_bricks(put_moment, LATE, 0, moments_ref, *edges)
    place_bricks(put_vector, LATE, 1, vectors_ref, *edges)
    to_lanes(moment_store, moment_lanes)
    vectors = vector_store[...].T
    masks = mask_ref[...]

    def system(z):
        near = masks[0:1] * pltpu.roll(z, PITCH, 1) + masks[1:2] * pltpu.roll(z, SPAN - PITCH, 1)
        near = near + masks[2:3] * pltpu.roll(z, 1, 1) + masks[3:4] * pltpu.roll(z, SPAN - 1, 1)
        return times(moment_lanes, z) + coupling_weight * (masks[4:5] * z - near)

    one = system(vectors[0:FEAT])
    two = system(times(first_ref, one) + vectors[FEAT : 2 * FEAT])
    three = system(times(first_ref, two) + times(second_ref, one) + vectors[2 * FEAT : 3 * FEAT])
    chain = (vectors[3 * FEAT :], one, two, three)
    for b in range(BX * BY):
        lane = lane_of(b // BY, b % BY)
        feats = feats_ref[b]
        for step, values in enumerate(chain):
            basis_ref[step, b : b + 1, :] = jnp.sum(feats * values[:, lane : lane + 1], axis=0, keepdims=True)
    reg = reg_ref[...]
    basis = [basis_ref[0]]
    for step in range(1, 4):
        basis.append(basis_ref[step] + reg * basis[-1])
        basis_ref[step] = basis[-1]

    def folded(x, combine):
        rows = [x[8 * k : 8 * k + 8, :] for k in range(x.shape[0] // 8)]
        parts = [r[:, LANES * k : LANES * (k + 1)] for r in rows for k in range(x.shape[1] // LANES)]
        while len(parts) > 1:
            parts = [combine(parts[k], parts[k + 1]) for k in range(0, len(parts), 2)]
        return parts[0]

    peaks = [jnp.max(folded(jnp.abs(v), jnp.maximum), axis=0, keepdims=True) for v in basis]
    peaks = jnp.max(jnp.concatenate(peaks + peaks, axis=0), axis=1, keepdims=True)
    scale, inverse = power_of_two(jnp.broadcast_to(peaks, (8, LANES)))
    scaled = [v * inverse[k : k + 1, 0:1] for k, v in enumerate(basis)]
    sums = [jnp.sum(folded(scaled[a] * scaled[b], jnp.add), axis=0, keepdims=True) for a, b in PAIRS]
    sums = jnp.concatenate(sums + [jnp.zeros((16 - len(PAIRS), LANES), jnp.float32)], axis=0)
    sums = jnp.sum(sums, axis=1, keepdims=True)
    lane = lax.broadcasted_iota(jnp.int32, (1, LANES), 1)
    row = jnp.zeros((1, LANES), jnp.float32)
    for k in range(len(PAIRS)):
        row = jnp.where(lane == k, sums[k : k + 1, :], row)
    for k in range(4):
        row = jnp.where(lane == 10 + k, scale[k : k + 1, :], row)
        row = jnp.where(lane == 14 + k, inverse[k : k + 1, :], row)
    message_ref[...] = jnp.broadcast_to(row, message_ref.shape)


def krylov(moments, vectors, edges, first, second, masks, voxel_feats, voxel_reg, devices):
    bricks, _, voxels = voxel_feats.shape
    return pl.pallas_call(
        krylov_kernel,
        out_shape=(
            jax.ShapeDtypeStruct((4, bricks, voxels), jnp.float32),
            jax.ShapeDtypeStruct((devices, LANES), jnp.float32),
        ),
        scratch_shapes=[
            pltpu.VMEM((SPAN, 8, LANES), jnp.float32),
            pltpu.VMEM((SPAN, LANES), jnp.float32),
            pltpu.VMEM((8 * LANES, SPAN), jnp.float32),
        ],
        compiler_params=pltpu.CompilerParams(vmem_limit_bytes=32 << 20),
        name="krylov",
    )(moments, vectors, *edges, first, second, masks, voxel_feats, voxel_reg)


def finish_kernel(shared_ref, basis_ref, solution_ref, residual_ref):
    shared = shared_ref[...]
    lane = lax.broadcasted_iota(jnp.int32, (1, LANES), 1)

    def pick(row, k):
        return jnp.sum(jnp.where(lane == k, row, 0.0), axis=1, keepdims=True)

    largest = jnp.max(shared, axis=0, keepdims=True)
    smallest = jnp.min(shared, axis=0, keepdims=True)
    scale = [pick(largest, 10 + k) for k in range(4)]
    inverse = [pick(smallest, 14 + k) for k in range(4)]
    weight = [shared[:, 10 + k : 11 + k] * inverse[k] for k in range(4)]
    left = jnp.zeros_like(shared)
    right = jnp.zeros_like(shared)
    for k, (a, b) in enumerate(PAIRS):
        left = jnp.where(lane == k, weight[a], left)
        right = jnp.where(lane == k, weight[b], right)
    total = jnp.sum(shared * left * right, axis=0, keepdims=True)
    gram = [[None] * 4 for _ in range(4)]
    for k, (a, b) in enumerate(PAIRS):
        gram[a][b] = gram[b][a] = pick(total, k)
    growth = [scale[k + 1] * inverse[k] for k in range(3)]

    def product(left, right):
        terms = [
            left[a] * right[b] * gram[a][b]
            for a in range(4)
            for b in range(4)
            if left[a] is not None and right[b] is not None
        ]
        return functools.reduce(jnp.add, terms)

    def plus(left, factor, right):
        out = []
        for a, b in zip(left, right):
            out.append(a if b is None else factor * b if a is None else a + factor * b)
        return out

    def image(vector):
        return [None] + [None if vector[k] is None else vector[k] * growth[k] for k in range(3)]

    solution = [None] * 4
    residual = [jnp.ones((1, 1), jnp.float32), None, None, None]
    direction = list(residual)
    norm_now = product(residual, residual)
    for iteration in range(ITERS):
        carried = image(direction)
        alpha = norm_now / product(direction, carried)
        solution = plus(solution, alpha, direction)
        residual = plus(residual, -alpha, carried)
        if iteration + 1 < ITERS:
            norm_next = product(residual, residual)
            direction = plus(residual, norm_next / norm_now, direction)
            norm_now = norm_next
    back = [scale[0] * inverse[k] for k in range(4)]
    for out_ref, coefficients in ((solution_ref, solution), (residual_ref, residual)):
        total = None
        for k, c in enumerate(coefficients):
            if c is not None:
                term = (c * back[k]) * basis_ref[k]
                total = term if total is None else total + term
        out_ref[...] = total


def finish(shared, basis):
    _, bricks, voxels = basis.shape
    out = jax.ShapeDtypeStruct((bricks, voxels), jnp.float32)
    return pl.pallas_call(finish_kernel, out_shape=(out, out), name="finish")(shared, basis)


def shards(point_feats, point_targets, point_lists, brick_adjacency, voxel_feats, voxel_reg):
    feat_count = point_feats.shape[0]
    brick_total, slots = point_lists.shape
    local_bricks = voxel_feats.shape[0]
    devices = brick_total // local_bricks
    sending = pack(point_feats, point_targets, point_lists, devices)
    got = lax.all_to_all(sending, GX_GY, split_axis=0, concat_axis=0, tiled=True)

    first, second, third, lanes = prepare(voxel_feats, voxel_reg)
    mask = (brick_adjacency >= 0).astype(jnp.float32)
    mask = jnp.concatenate([mask, jnp.sum(mask, axis=1, keepdims=True)], axis=1)
    mask = jnp.pad(mask, ((0, 0), (0, LANES - 5)))
    early = (first, second, mask)
    low, high = swap(*along_messages(EARLY, early), GX)
    below, above = swap(*relay(EARLY, early, low, high, "relay_early"), "gy")
    first_lanes, second_lanes, mask_lanes = gather_early(first, second, mask, (low, high, below, above))
    moments, vectors, to_low, to_high = find_moments(got, lanes)
    low, high = swap(to_low, to_high, GX)
    below, above = swap(*relay(LATE, (moments, vectors), low, high, "relay_late"), "gy")
    basis, message = krylov(
        moments, vectors, (low, high, below, above), first_lanes, second_lanes, mask_lanes,
        voxel_feats, voxel_reg, devices,
    )
    shared = lax.all_to_all(message, GX_GY, split_axis=0, concat_axis=0, tiled=True)
    return finish(shared, basis)


def solution(mesh):
    torus = Mesh(mesh.devices.reshape(4, 4, 2, mesh.shape["gy"]), ("gx_0", "gx_1", "gx_2", "gy"))
    return jax.shard_map(
        shards,
        mesh=torus,
        in_specs=(
            P(None, GX_GY),
            P(GX_GY),
            P(GX_GY, None),
            P(GX_GY, None),
            P(GX_GY, None, None),
            P(GX_GY, None),
        ),
        out_specs=(P(GX_GY, None), P(GX_GY, None)),
        check_vma=False,
    )
```

```python
import functools

import jax
import jax.numpy as jnp
from jax import lax
from jax.experimental import pallas as pl
from jax.experimental.pallas import tpu as pltpu
from jax.sharding import Mesh
from jax.sharding import PartitionSpec as P

BX = 8
BY = 4
ITERS = 3
SLOTS = 8
LANES = 128
FEAT = 32
PITCH = 16
SPAN = 256
REACH = 3
GX_GY = ("gx_0", "gx_1", "gx_2", "gy")
GX = ("gx_0", "gx_1", "gx_2")
HIGHEST = lax.Precision.HIGHEST
PAIRS = tuple((a, b) for a in range(4) for b in range(a, 4))


coupling_weight = 1.0

EARLY = ((8, 2), (8, 1), (1, 2))
LATE = ((8, 2), (1, 3))


def padded(rows):
    return (rows + 7) // 8 * 8


def along_rows(section):
    return padded(section[0] * section[1] * BY)


def across_rows(section):
    rows, depth = section
    return padded(rows * sum(BX + 2 * (depth - k) for k in range(1, depth + 1)))


def message_rows(sections, size):
    return sum(size(section) for section in sections)


def piece(ref, start, rows, index):
    if rows == 8 and len(ref.shape) == 3:
        return ref[index]
    return ref[start + rows * index : start + rows * (index + 1), :]


def brick_at(own, low, high, start, section, a, e):
    rows, depth = section
    if a < 0:
        return piece(low, start, rows, (a + depth) * BY + e)
    if a >= BX:
        return piece(high, start, rows, (a - BX) * BY + e)
    return piece(own, 0, rows, a * BY + e)


def fill_across(sections, owns, low, high, to_low, to_high):
    source = target = 0
    for section, own in zip(sections, owns):
        rows, depth = section
        index = 0
        for away in range(1, depth + 1):
            extra = depth - away
            for a in range(-extra, BX + extra):
                place = slice(target + rows * index, target + rows * (index + 1))
                to_low[place, :] = brick_at(own, low, high, source, section, a, away - 1)
                to_high[place, :] = brick_at(own, low, high, source, section, a, BY - away)
                index += 1
        used, whole = rows * index, across_rows(section)
        if used < whole:
            blank = jnp.zeros((whole - used, LANES), jnp.float32)
            to_low[target + used : target + whole, :] = blank
            to_high[target + used : target + whole, :] = blank
        source += along_rows(section)
        target += whole


def place_bricks(put, sections, which, own, along_low, along_high, across_low, across_high):
    section = sections[which]
    rows, depth = section
    start = message_rows(sections[:which], along_rows)
    for a in range(-depth, BX + depth):
        for e in range(BY):
            put(a, e, brick_at(own, along_low, along_high, start, section, a, e))
    start = message_rows(sections[:which], across_rows)
    index = 0
    for away in range(1, depth + 1):
        extra = depth - away
        for a in range(-extra, BX + extra):
            put(a, -away, piece(across_low, start, rows, index))
            put(a, BY - 1 + away, piece(across_high, start, rows, index))
            index += 1


def lane_of(a, e):
    return (a + REACH) * PITCH + e + REACH


def to_lanes(records, lanes_ref):
    for t in range(8):
        lanes_ref[t * LANES : (t + 1) * LANES, :] = records[:, t, :].T


def times(matrix_ref, vector):
    total = None
    for t in range(8):
        for q in range(4):
            i = 8 * q + t
            row = t * LANES + q * FEAT
            term = matrix_ref[row : row + FEAT, :] * vector[i : i + 1, :]
            total = term if total is None else total + term
    return total


def pack_kernel(lists_ref, feats_ref, targets_ref, out_ref, mask_ref):
    rows = mask_ref.shape[0]
    width = LANES * SLOTS

    @pl.when(pl.program_id(0) == 0)
    def _():
        lane = lax.broadcasted_iota(jnp.int32, (SLOTS, LANES), 1)
        codes = []
        for block in range(rows):
            chosen = lists_ref[:, block * LANES : (block + 1) * LANES]
            offset = chosen - (lane + block * LANES) * SLOTS
            bits = jnp.where(chosen >= 0, lax.shift_left(1, jnp.clip(offset, 0, SLOTS - 1)), 0)
            codes.append(jnp.sum(bits, axis=0, keepdims=True))
        code = jnp.concatenate(codes, axis=0).astype(jnp.float32).astype(jnp.bfloat16)
        brick = lax.broadcasted_iota(jnp.int32, (LANES, width), 0)
        point = lax.broadcasted_iota(jnp.int32, (LANES, width), 1)
        spread = (lax.shift_right_logical(point, 3) == brick).astype(jnp.float32).astype(jnp.bfloat16)
        wide = jnp.dot(code, spread, preferred_element_type=jnp.float32).astype(jnp.int32)
        slot = lax.broadcasted_iota(jnp.int32, (rows, width), 1) & (SLOTS - 1)
        mask_ref[...] = (lax.shift_right_logical(wide, slot) & 1).astype(jnp.float32)

    step = pl.program_id(0)
    dests = out_ref.shape[0]
    feat_count = feats_ref.shape[0]
    for part in range(dests * 256 // width):
        row = mask_ref[pl.ds(step * (dests * 256 // width) + part, 1), :].astype(jnp.bfloat16)
        masked = feats_ref[:, part * width : (part + 1) * width] * row
        for half_block in range(width // LANES):
            dest = (part * width + half_block * LANES) // 256
            half = half_block % 2
            out_ref[dest, half * feat_count : (half + 1) * feat_count, :] = masked[
                :, half_block * LANES : (half_block + 1) * LANES
            ]
    for dest in range(dests):
        out_ref[dest, 2 * feat_count : 2 * feat_count + 2, :] = targets_ref[2 * dest : 2 * dest + 2, :]


def pack(point_feats, point_targets, point_lists, devices):
    feat_count, points = point_feats.shape
    bricks = point_lists.shape[0]
    steps = 8
    dests = devices // steps
    return pl.pallas_call(
        pack_kernel,
        grid=(steps,),
        in_specs=[
            pl.BlockSpec((SLOTS, bricks), lambda i: (0, 0)),
            pl.BlockSpec((feat_count, points // steps), lambda i: (0, i)),
            pl.BlockSpec((points // steps // LANES, LANES), lambda i: (i, 0)),
        ],
        out_specs=pl.BlockSpec((dests, 2 * feat_count + 2, LANES), lambda i: (i, 0, 0)),
        out_shape=jax.ShapeDtypeStruct((devices, 2 * feat_count + 2, LANES), jnp.bfloat16),
        scratch_shapes=[pltpu.VMEM((bricks // LANES, LANES * SLOTS), jnp.float32)],
        name="pack",
    )(point_lists.T, point_feats, point_targets.reshape(points // LANES, LANES))


def prepare_kernel(feats_ref, reg_ref, first_ref, second_ref, third_ref, lanes_ref):
    records = (first_ref, second_ref, third_ref)

    def one(b, carry):
        feats = feats_ref[b]
        reg = reg_ref[pl.ds(b, 1), :]
        once = feats * reg
        left = jnp.concatenate([feats, once, once * reg], axis=0)
        product = lax.dot_general(
            left,
            feats,
            (((1,), (1,)), ((), ())),
            precision=HIGHEST,
            preferred_element_type=jnp.float32,
        )
        for power, record in enumerate(records):
            rows = [product[power * FEAT + 8 * q : power * FEAT + 8 * q + 8, :] for q in range(4)]
            record[b] = jnp.concatenate(rows, axis=1)
        return carry

    lax.fori_loop(0, feats_ref.shape[0], one, 0)
    for power, record in enumerate(records):
        for t in range(8):
            block = jnp.concatenate([record[:, t, :], jnp.zeros((96, LANES), jnp.float32)], axis=0)
            lanes_ref[power, t * LANES : (t + 1) * LANES, :] = block.T


def prepare(voxel_feats, voxel_reg):
    bricks = voxel_feats.shape[0]
    record = jax.ShapeDtypeStruct((bricks, 8, LANES), jnp.float32)
    return pl.pallas_call(
        prepare_kernel,
        out_shape=(record, record, record, jax.ShapeDtypeStruct((3, 8 * LANES, LANES), jnp.float32)),
        compiler_params=pltpu.CompilerParams(vmem_limit_bytes=10 << 20),
        cost_estimate=pl.CostEstimate(flops=600_000_000, bytes_accessed=5_000_000, transcendentals=0),
        name="prepare",
    )(voxel_feats, voxel_reg)


def gather_early_kernel(
    first_ref, second_ref, mask_ref, low_ref, high_ref, below_ref, above_ref,
    first_lanes, second_lanes, mask_lanes, first_store, second_store, mask_store,
):
    for store in (first_store, second_store, mask_store):
        store[...] = jnp.zeros_like(store)

    def put(store):
        def write(a, e, value):
            if len(store.shape) == 3:
                store[lane_of(a, e)] = value
            else:
                store[lane_of(a, e) : lane_of(a, e) + 1, :] = value

        return write

    edges = (low_ref, high_ref, below_ref, above_ref)
    place_bricks(put(first_store), EARLY, 0, first_ref, *edges)
    place_bricks(put(second_store), EARLY, 1, second_ref, *edges)
    place_bricks(put(mask_store), EARLY, 2, mask_ref, *edges)
    to_lanes(first_store, first_lanes)
    to_lanes(second_store, second_lanes)
    mask_lanes[...] = mask_store[...].T[:8, :]


def gather_early(first, second, mask, edges):
    lanes = jax.ShapeDtypeStruct((8 * LANES, SPAN), jnp.float32)
    return pl.pallas_call(
        gather_early_kernel,
        out_shape=(lanes, lanes, jax.ShapeDtypeStruct((8, SPAN), jnp.float32)),
        scratch_shapes=[
            pltpu.VMEM((SPAN, 8, LANES), jnp.float32),
            pltpu.VMEM((SPAN, 8, LANES), jnp.float32),
            pltpu.VMEM((SPAN, LANES), jnp.float32),
        ],
        compiler_params=pltpu.CompilerParams(vmem_limit_bytes=10 << 20),
        cost_estimate=pl.CostEstimate(flops=2_000_000, bytes_accessed=3_000_000, transcendentals=0),
        name="gather_early",
    )(first, second, mask, *edges)


def relay_kernel(sections, count, *refs):
    owns, low, high, to_low, to_high = refs[:count], *refs[count:]
    fill_across(sections, owns, low, high, to_low, to_high)


def relay(sections, owns, low, high, name):
    out = jax.ShapeDtypeStruct((message_rows(sections, across_rows), LANES), jnp.float32)
    return pl.pallas_call(
        functools.partial(relay_kernel, sections, len(owns)),
        out_shape=(out, out),
        compiler_params=pltpu.CompilerParams(vmem_limit_bytes=4 << 20),
        name=name,
    )(*owns, low, high)


def along_messages(sections, owns):
    to_low, to_high = [], []
    for (rows, depth), own in zip(sections, owns):
        flat = own.reshape(-1, LANES)
        used = rows * depth * BY
        blank = ((0, padded(used) - used), (0, 0))
        to_low.append(jnp.pad(flat[:used], blank))
        to_high.append(jnp.pad(flat[flat.shape[0] - used :], blank))
    return jnp.concatenate(to_low), jnp.concatenate(to_high)


def swap(to_low, to_high, axis):
    count = lax.axis_size(axis)
    up = [(i, i + 1) for i in range(count - 1)]
    down = [(b, a) for a, b in up]
    return lax.ppermute(to_high, axis, up), lax.ppermute(to_low, axis, down)


def moments_kernel(got_ref, lanes_ref, moments_ref, vectors_ref, low_ref, high_ref, turned, sums):
    step = pl.program_id(0)
    sources = got_ref.shape[0]

    @pl.when(step == 0)
    def _():
        sums[...] = jnp.zeros_like(sums)

    for group in range(sources // 4):
        for half in range(2):
            block = got_ref[4 * group : 4 * group + 4, half * FEAT : (half + 1) * FEAT, :]
            turned[half, step * (sources // 4) + group] = block.reshape(LANES, LANES).T
    for half in range(2):
        total = sums[half]
        for source in range(sources):
            feats = got_ref[source, half * FEAT : (half + 1) * FEAT, :].astype(jnp.float32)
            target = got_ref[source, 2 * FEAT : 2 * FEAT + 2, :].astype(jnp.float32)
            total = total + feats * target[half : half + 1, :]
        sums[half] = total

    @pl.when(step == pl.num_programs(0) - 1)
    def _():
        groups = turned.shape[1]
        row = lax.broadcasted_iota(jnp.int32, (1, 16, LANES), 1)
        upper = (row < SLOTS).astype(jnp.float32).astype(jnp.bfloat16)
        lower = (row >= SLOTS).astype(jnp.float32).astype(jnp.bfloat16)
        lane_group = lax.broadcasted_iota(jnp.int32, (1, LANES), 1) // FEAT
        for half in range(2):
            for pair in range(8):
                points = turned[half, :, 16 * pair : 16 * pair + 16, :]
                left = points.reshape(groups * 16, LANES)
                right = jnp.concatenate(
                    [(points * upper).reshape(groups * 16, LANES), (points * lower).reshape(groups * 16, LANES)],
                    axis=1,
                )
                product = lax.dot_general(
                    left, right, (((0,), (0,)), ((), ())), preferred_element_type=jnp.float32
                )
                for k in range(2):
                    square = product[:, k * LANES : (k + 1) * LANES]
                    own = jnp.zeros((FEAT, LANES), jnp.float32)
                    for q in range(4):
                        own = own + jnp.where(lane_group == q, square[q * FEAT : (q + 1) * FEAT, :], 0.0)
                    own = own + pltpu.roll(own, 64, 1)
                    own = own + pltpu.roll(own, 32, 1)
                    record = own[0:8, :]
                    for q in range(1, 4):
                        record = jnp.where(lane_group == q, own[8 * q : 8 * q + 8, :], record)
                    moments_ref[half * 16 + 2 * pair + k] = record
        point = lax.broadcasted_iota(jnp.int32, (LANES, LANES), 0) // SLOTS
        lane = lax.broadcasted_iota(jnp.int32, (LANES, LANES), 1)
        values = jnp.zeros((FEAT, LANES), jnp.float32)
        for half in range(2):
            spread = (lane == point + half * 16).astype(jnp.float32)
            values = values + jnp.dot(
                sums[half], spread, precision=HIGHEST, preferred_element_type=jnp.float32
            )
        applied = [times(lanes_ref.at[power], values) for power in range(3)]
        vectors = jnp.concatenate([*applied, values], axis=0).T
        vectors_ref[...] = vectors[: BX * BY, :]
        depth = LATE[0][1] * BY
        for k in range(depth):
            low_ref[8 * k : 8 * k + 8, :] = moments_ref[k]
            high_ref[8 * k : 8 * k + 8, :] = moments_ref[BX * BY - depth + k]
        deep = LATE[1][1] * BY
        blank = jnp.zeros((padded(deep) - deep, LANES), jnp.float32)
        low_ref[8 * depth :, :] = jnp.concatenate([vectors[:deep], blank], axis=0)
        high_ref[8 * depth :, :] = jnp.concatenate([vectors[BX * BY - deep : BX * BY], blank], axis=0)


def find_moments(got, lanes):
    devices, rows, _ = got.shape
    steps = 4
    bricks = BX * BY
    message = message_rows(LATE, along_rows)
    return pl.pallas_call(
        moments_kernel,
        grid=(steps,),
        in_specs=[
            pl.BlockSpec((devices // steps, rows, LANES), lambda i: (i, 0, 0)),
            pl.BlockSpec(lanes.shape, lambda i: (0, 0, 0)),
        ],
        out_specs=(
            pl.BlockSpec((bricks, 8, LANES), lambda i: (0, 0, 0)),
            pl.BlockSpec((bricks, LANES), lambda i: (0, 0)),
            pl.BlockSpec((message, LANES), lambda i: (0, 0)),
            pl.BlockSpec((message, LANES), lambda i: (0, 0)),
        ),
        out_shape=(
            jax.ShapeDtypeStruct((bricks, 8, LANES), jnp.float32),
            jax.ShapeDtypeStruct((bricks, LANES), jnp.float32),
            jax.ShapeDtypeStruct((message, LANES), jnp.float32),
            jax.ShapeDtypeStruct((message, LANES), jnp.float32),
        ),
        scratch_shapes=[
            pltpu.VMEM((2, devices // 4, LANES, LANES), jnp.bfloat16),
            pltpu.VMEM((2, FEAT, LANES), jnp.float32),
        ],
        compiler_params=pltpu.CompilerParams(vmem_limit_bytes=12 << 20),
        name="moments",
    )(got, lanes)


def power_of_two(value):
    scale = jnp.ones_like(value)
    inverse = jnp.ones_like(value)
    for k in (64, 32, 16, 8, 4, 2, 1):
        up, down = 2.0**k, 2.0**-k
        large = value * down >= 1.0
        small = value * up <= 1.0
        value = jnp.where(large, value * down, jnp.where(small, value * up, value))
        scale = jnp.where(large, scale * up, jnp.where(small, scale * down, scale))
        inverse = jnp.where(large, inverse * down, jnp.where(small, inverse * up, inverse))
    return scale, inverse


def krylov_kernel(
    moments_ref, vectors_ref, low_ref, high_ref, below_ref, above_ref, first_ref, second_ref, mask_ref,
    feats_ref, reg_ref, basis_ref, message_ref, moment_store, vector_store, moment_lanes,
):
    moment_store[...] = jnp.zeros_like(moment_store)
    vector_store[...] = jnp.zeros_like(vector_store)

    def put_moment(a, e, value):
        moment_store[lane_of(a, e)] = value

    def put_vector(a, e, value):
        vector_store[lane_of(a, e) : lane_of(a, e) + 1, :] = value

    edges = (low_ref, high_ref, below_ref, above_ref)
    place_bricks(put_moment, LATE, 0, moments_ref, *edges)
    place_bricks(put_vector, LATE, 1, vectors_ref, *edges)
    to_lanes(moment_store, moment_lanes)
    vectors = vector_store[...].T
    masks = mask_ref[...]

    def system(z):
        near = masks[0:1] * pltpu.roll(z, PITCH, 1) + masks[1:2] * pltpu.roll(z, SPAN - PITCH, 1)
        near = near + masks[2:3] * pltpu.roll(z, 1, 1) + masks[3:4] * pltpu.roll(z, SPAN - 1, 1)
        return times(moment_lanes, z) + coupling_weight * (masks[4:5] * z - near)

    one = system(vectors[0:FEAT])
    two = system(times(first_ref, one) + vectors[FEAT : 2 * FEAT])
    three = system(times(first_ref, two) + times(second_ref, one) + vectors[2 * FEAT : 3 * FEAT])
    chain = (vectors[3 * FEAT :], one, two, three)
    for b in range(BX * BY):
        lane = lane_of(b // BY, b % BY)
        feats = feats_ref[b]
        for step, values in enumerate(chain):
            basis_ref[step, b : b + 1, :] = jnp.sum(feats * values[:, lane : lane + 1], axis=0, keepdims=True)
    reg = reg_ref[...]
    basis = [basis_ref[0]]
    for step in range(1, 4):
        basis.append(basis_ref[step] + reg * basis[-1])
        basis_ref[step] = basis[-1]

    def folded(x, combine):
        rows = [x[8 * k : 8 * k + 8, :] for k in range(x.shape[0] // 8)]
        parts = [r[:, LANES * k : LANES * (k + 1)] for r in rows for k in range(x.shape[1] // LANES)]
        while len(parts) > 1:
            parts = [combine(parts[k], parts[k + 1]) for k in range(0, len(parts), 2)]
        return parts[0]

    peaks = [jnp.max(folded(jnp.abs(v), jnp.maximum), axis=0, keepdims=True) for v in basis]
    peaks = jnp.max(jnp.concatenate(peaks + peaks, axis=0), axis=1, keepdims=True)
    scale, inverse = power_of_two(jnp.broadcast_to(peaks, (8, LANES)))
    scaled = [v * inverse[k : k + 1, 0:1] for k, v in enumerate(basis)]
    sums = [jnp.sum(folded(scaled[a] * scaled[b], jnp.add), axis=0, keepdims=True) for a, b in PAIRS]
    sums = jnp.concatenate(sums + [jnp.zeros((16 - len(PAIRS), LANES), jnp.float32)], axis=0)
    sums = jnp.sum(sums, axis=1, keepdims=True)
    lane = lax.broadcasted_iota(jnp.int32, (1, LANES), 1)
    row = jnp.zeros((1, LANES), jnp.float32)
    for k in range(len(PAIRS)):
        row = jnp.where(lane == k, sums[k : k + 1, :], row)
    for k in range(4):
        row = jnp.where(lane == 10 + k, scale[k : k + 1, :], row)
        row = jnp.where(lane == 14 + k, inverse[k : k + 1, :], row)
    message_ref[...] = jnp.broadcast_to(row, message_ref.shape)


def krylov(moments, vectors, edges, first, second, masks, voxel_feats, voxel_reg, devices):
    bricks, _, voxels = voxel_feats.shape
    return pl.pallas_call(
        krylov_kernel,
        out_shape=(
            jax.ShapeDtypeStruct((4, bricks, voxels), jnp.float32),
            jax.ShapeDtypeStruct((devices, LANES), jnp.float32),
        ),
        scratch_shapes=[
            pltpu.VMEM((SPAN, 8, LANES), jnp.float32),
            pltpu.VMEM((SPAN, LANES), jnp.float32),
            pltpu.VMEM((8 * LANES, SPAN), jnp.float32),
        ],
        compiler_params=pltpu.CompilerParams(vmem_limit_bytes=12 << 20),
        name="krylov",
    )(moments, vectors, *edges, first, second, masks, voxel_feats, voxel_reg)


def finish_kernel(shared_ref, basis_ref, solution_ref, residual_ref):
    shared = shared_ref[...]
    lane = lax.broadcasted_iota(jnp.int32, (1, LANES), 1)

    def pick(row, k):
        return jnp.sum(jnp.where(lane == k, row, 0.0), axis=1, keepdims=True)

    largest = jnp.max(shared, axis=0, keepdims=True)
    smallest = jnp.min(shared, axis=0, keepdims=True)
    scale = [pick(largest, 10 + k) for k in range(4)]
    inverse = [pick(smallest, 14 + k) for k in range(4)]
    weight = [shared[:, 10 + k : 11 + k] * inverse[k] for k in range(4)]
    left = jnp.zeros_like(shared)
    right = jnp.zeros_like(shared)
    for k, (a, b) in enumerate(PAIRS):
        left = jnp.where(lane == k, weight[a], left)
        right = jnp.where(lane == k, weight[b], right)
    total = jnp.sum(shared * left * right, axis=0, keepdims=True)
    gram = [[None] * 4 for _ in range(4)]
    for k, (a, b) in enumerate(PAIRS):
        gram[a][b] = gram[b][a] = pick(total, k)
    growth = [scale[k + 1] * inverse[k] for k in range(3)]

    def product(left, right):
        terms = [
            left[a] * right[b] * gram[a][b]
            for a in range(4)
            for b in range(4)
            if left[a] is not None and right[b] is not None
        ]
        return functools.reduce(jnp.add, terms)

    def plus(left, factor, right):
        out = []
        for a, b in zip(left, right):
            out.append(a if b is None else factor * b if a is None else a + factor * b)
        return out

    def image(vector):
        return [None] + [None if vector[k] is None else vector[k] * growth[k] for k in range(3)]

    solution = [None] * 4
    residual = [jnp.ones((1, 1), jnp.float32), None, None, None]
    direction = list(residual)
    norm_now = product(residual, residual)
    for iteration in range(ITERS):
        carried = image(direction)
        alpha = norm_now / product(direction, carried)
        solution = plus(solution, alpha, direction)
        residual = plus(residual, -alpha, carried)
        if iteration + 1 < ITERS:
            norm_next = product(residual, residual)
            direction = plus(residual, norm_next / norm_now, direction)
            norm_now = norm_next
    back = [scale[0] * inverse[k] for k in range(4)]
    for out_ref, coefficients in ((solution_ref, solution), (residual_ref, residual)):
        total = None
        for k, c in enumerate(coefficients):
            if c is not None:
                term = (c * back[k]) * basis_ref[k]
                total = term if total is None else total + term
        out_ref[...] = total


def finish(shared, basis):
    _, bricks, voxels = basis.shape
    out = jax.ShapeDtypeStruct((bricks, voxels), jnp.float32)
    return pl.pallas_call(
        finish_kernel,
        out_shape=(out, out),
        compiler_params=pltpu.CompilerParams(vmem_limit_bytes=4 << 20),
        name="finish",
    )(shared, basis)


def shards(point_feats, point_targets, point_lists, brick_adjacency, voxel_feats, voxel_reg):
    feat_count = point_feats.shape[0]
    brick_total, slots = point_lists.shape
    local_bricks = voxel_feats.shape[0]
    devices = brick_total // local_bricks
    sending = pack(point_feats, point_targets, point_lists, devices)
    got = lax.all_to_all(sending, GX_GY, split_axis=0, concat_axis=0, tiled=True)

    first, second, third, lanes = prepare(voxel_feats, voxel_reg)
    mask = (brick_adjacency >= 0).astype(jnp.float32)
    mask = jnp.concatenate([mask, jnp.sum(mask, axis=1, keepdims=True)], axis=1)
    mask = jnp.pad(mask, ((0, 0), (0, LANES - 5)))
    early = (first, second, mask)
    low, high = swap(*along_messages(EARLY, early), GX)
    below, above = swap(*relay(EARLY, early, low, high, "relay_early"), "gy")
    first_lanes, second_lanes, mask_lanes = gather_early(first, second, mask, (low, high, below, above))
    moments, vectors, to_low, to_high = find_moments(got, lanes)
    low, high = swap(to_low, to_high, GX)
    below, above = swap(*relay(LATE, (moments, vectors), low, high, "relay_late"), "gy")
    basis, message = krylov(
        moments, vectors, (low, high, below, above), first_lanes, second_lanes, mask_lanes,
        voxel_feats, voxel_reg, devices,
    )
    shared = lax.all_to_all(message, GX_GY, split_axis=0, concat_axis=0, tiled=True)
    return finish(shared, basis)


def solution(mesh):
    torus = Mesh(mesh.devices.reshape(4, 4, 2, mesh.shape["gy"]), ("gx_0", "gx_1", "gx_2", "gy"))
    return jax.shard_map(
        shards,
        mesh=torus,
        in_specs=(
            P(None, GX_GY),
            P(GX_GY),
            P(GX_GY, None),
            P(GX_GY, None),
            P(GX_GY, None, None),
            P(GX_GY, None),
        ),
        out_specs=(P(GX_GY, None), P(GX_GY, None)),
        check_vma=False,
    )
```

```python
import functools

import jax
import jax.numpy as jnp
from jax import lax
from jax.experimental import pallas as pl
from jax.experimental.pallas import tpu as pltpu
from jax.sharding import Mesh
from jax.sharding import PartitionSpec as P

BX = 8
BY = 4
ITERS = 3
SLOTS = 8
LANES = 128
FEAT = 32
PITCH = 16
SPAN = 256
REACH = 3
GX_GY = ("gx_0", "gx_1", "gx_2", "gy")
GX = ("gx_0", "gx_1", "gx_2")
HIGHEST = lax.Precision.HIGHEST
PAIRS = tuple((a, b) for a in range(4) for b in range(a, 4))


coupling_weight = 1.0

EARLY = ((8, 2), (8, 1), (1, 2))
LATE = ((8, 2), (1, 3))


def padded(rows):
    return (rows + 7) // 8 * 8


def along_rows(section):
    return padded(section[0] * section[1] * BY)


def across_rows(section):
    rows, depth = section
    return padded(rows * sum(BX + 2 * (depth - k) for k in range(1, depth + 1)))


def message_rows(sections, size):
    return sum(size(section) for section in sections)


def piece(ref, start, rows, index):
    if rows == 8 and len(ref.shape) == 3:
        return ref[index]
    return ref[start + rows * index : start + rows * (index + 1), :]


def brick_at(own, low, high, start, section, a, e):
    rows, depth = section
    if a < 0:
        return piece(low, start, rows, (a + depth) * BY + e)
    if a >= BX:
        return piece(high, start, rows, (a - BX) * BY + e)
    return piece(own, 0, rows, a * BY + e)


def fill_across(sections, owns, low, high, to_low, to_high):
    source = target = 0
    for section, own in zip(sections, owns):
        rows, depth = section
        index = 0
        for away in range(1, depth + 1):
            extra = depth - away
            for a in range(-extra, BX + extra):
                place = slice(target + rows * index, target + rows * (index + 1))
                to_low[place, :] = brick_at(own, low, high, source, section, a, away - 1)
                to_high[place, :] = brick_at(own, low, high, source, section, a, BY - away)
                index += 1
        used, whole = rows * index, across_rows(section)
        if used < whole:
            blank = jnp.zeros((whole - used, LANES), jnp.float32)
            to_low[target + used : target + whole, :] = blank
            to_high[target + used : target + whole, :] = blank
        source += along_rows(section)
        target += whole


def place_bricks(put, sections, which, own, along_low, along_high, across_low, across_high):
    section = sections[which]
    rows, depth = section
    start = message_rows(sections[:which], along_rows)
    for a in range(-depth, BX + depth):
        for e in range(BY):
            put(a, e, brick_at(own, along_low, along_high, start, section, a, e))
    start = message_rows(sections[:which], across_rows)
    index = 0
    for away in range(1, depth + 1):
        extra = depth - away
        for a in range(-extra, BX + extra):
            put(a, -away, piece(across_low, start, rows, index))
            put(a, BY - 1 + away, piece(across_high, start, rows, index))
            index += 1


def lane_of(a, e):
    return (a + REACH) * PITCH + e + REACH


def to_lanes(records, lanes_ref):
    for t in range(8):
        lanes_ref[t * LANES : (t + 1) * LANES, :] = records[:, t, :].T


def times(matrix_ref, vector):
    total = None
    for t in range(8):
        for q in range(4):
            i = 8 * q + t
            row = t * LANES + q * FEAT
            term = matrix_ref[row : row + FEAT, :] * vector[i : i + 1, :]
            total = term if total is None else total + term
    return total


def pack_kernel(lists_ref, feats_ref, targets_ref, out_ref, feats, packed, arrived, left):
    steps = arrived.shape[0]
    devices = out_ref.shape[0]
    bricks = lists_ref.shape[1]
    dests = devices // steps
    width = LANES * SLOTS
    points = bricks * SLOTS // steps
    arriving = [
        pltpu.make_async_copy(
            feats_ref.at[:, k * points : (k + 1) * points], feats.at[:, k * points : (k + 1) * points], arrived.at[k]
        )
        for k in range(steps)
    ]
    leaving = [
        pltpu.make_async_copy(
            packed.at[k * dests : (k + 1) * dests], out_ref.at[k * dests : (k + 1) * dests], left.at[k]
        )
        for k in range(steps)
    ]
    for copy in arriving:
        copy.start()
    rows = bricks // LANES
    lane = lax.broadcasted_iota(jnp.int32, (SLOTS, LANES), 1)
    codes = []
    for block in range(rows):
        chosen = lists_ref[:, block * LANES : (block + 1) * LANES]
        offset = chosen - (lane + block * LANES) * SLOTS
        bits = jnp.where(chosen >= 0, lax.shift_left(1, jnp.clip(offset, 0, SLOTS - 1)), 0)
        codes.append(jnp.sum(bits, axis=0, keepdims=True))
    code = jnp.concatenate(codes, axis=0).astype(jnp.float32).astype(jnp.bfloat16)
    brick = lax.broadcasted_iota(jnp.int32, (LANES, width), 0)
    point = lax.broadcasted_iota(jnp.int32, (LANES, width), 1)
    spread = (lax.shift_right_logical(point, 3) == brick).astype(jnp.float32).astype(jnp.bfloat16)
    wide = jnp.dot(code, spread, preferred_element_type=jnp.float32).astype(jnp.int32)
    slot = lax.broadcasted_iota(jnp.int32, (rows, width), 1) & (SLOTS - 1)
    mask = (lax.shift_right_logical(wide, slot) & 1).astype(jnp.float32)
    for k in range(steps):
        arriving[k].wait()
        for part in range(points // width):
            first = k * points + part * width
            row = mask[first // width : first // width + 1, :].astype(jnp.bfloat16)
            masked = feats[:, first : first + width] * row
            for piece_index in range(width // LANES):
                dest = (first + piece_index * LANES) // (2 * LANES)
                half = piece_index % 2
                packed[dest, half * FEAT : (half + 1) * FEAT, :] = masked[
                    :, piece_index * LANES : (piece_index + 1) * LANES
                ]
        for dest in range(k * dests, (k + 1) * dests):
            packed[dest, 2 * FEAT : 2 * FEAT + 2, :] = targets_ref[2 * dest : 2 * dest + 2, :]
        leaving[k].start()
    for copy in leaving:
        copy.wait()


def pack(point_feats, point_targets, point_lists, devices):
    points = point_feats.shape[1]
    steps = 8
    rows = 2 * FEAT + 2
    return pl.pallas_call(
        pack_kernel,
        in_specs=[
            pl.BlockSpec(memory_space=pltpu.VMEM),
            pl.BlockSpec(memory_space=pl.ANY),
            pl.BlockSpec(memory_space=pltpu.VMEM),
        ],
        out_specs=pl.BlockSpec(memory_space=pl.ANY),
        out_shape=jax.ShapeDtypeStruct((devices, rows, LANES), jnp.bfloat16),
        scratch_shapes=[
            pltpu.VMEM((FEAT, points), jnp.bfloat16),
            pltpu.VMEM((devices, rows, LANES), jnp.bfloat16),
            pltpu.SemaphoreType.DMA((steps,)),
            pltpu.SemaphoreType.DMA((steps,)),
        ],
        name="pack",
    )(point_lists.T, point_feats, point_targets.reshape(points // LANES, LANES))


def spread_rows(square, lane_group):
    square = square + pltpu.roll(square, 64, 1)
    square = square + pltpu.roll(square, 32, 1)
    record = square[0:8, :]
    for q in range(1, 4):
        record = jnp.where(lane_group == q, square[8 * q : 8 * q + 8, :], record)
    return record


def three_parts(x):
    high = x.astype(jnp.bfloat16)
    rest = x - high.astype(jnp.float32)
    middle = rest.astype(jnp.bfloat16)
    return high, middle, (rest - middle.astype(jnp.float32)).astype(jnp.bfloat16)


def prepare_kernel(feats_ref, reg_ref, *records):

    lane_group = lax.broadcasted_iota(jnp.int32, (1, LANES), 1) // FEAT
    together = 4

    def some(step, carry):
        for k in range(together):
            b = step * together + k
            feats = feats_ref[b]
            reg = reg_ref[pl.ds(b, 1), :]
            once = feats * reg
            parts = three_parts(jnp.concatenate([feats, once, once * reg], axis=0))
            left = jnp.concatenate(parts, axis=0)
            right = [part[:FEAT, :] for part in parts]
            right = jnp.concatenate([*right, jnp.zeros_like(right[0])], axis=0)
            product = lax.dot_general(
                left, right, (((1,), (1,)), ((), ())), preferred_element_type=jnp.float32
            )
            size = 3 * FEAT
            total = jnp.where(lane_group < 1, product[2 * size :, :], 0.0)
            total = total + jnp.where(lane_group < 2, product[size : 2 * size, :], 0.0)
            total = total + product[:size, :]
            for power, record in enumerate(records):
                record[b] = spread_rows(total[power * FEAT : (power + 1) * FEAT, :], lane_group)
        return carry

    lax.fori_loop(0, feats_ref.shape[0] // together, some, 0)


def prepare(voxel_feats, voxel_reg):
    bricks = voxel_feats.shape[0]
    record = jax.ShapeDtypeStruct((bricks, 8, LANES), jnp.float32)
    return pl.pallas_call(
        prepare_kernel,
        out_shape=(record, record, record),
        compiler_params=pltpu.CompilerParams(vmem_limit_bytes=10 << 20),
        cost_estimate=pl.CostEstimate(flops=600_000_000, bytes_accessed=5_000_000, transcendentals=0),
        name="prepare",
    )(voxel_feats, voxel_reg)


def gather_early_kernel(
    first_ref, second_ref, mask_ref, low_ref, high_ref, below_ref, above_ref,
    first_lanes, second_lanes, mask_lanes, first_store, second_store, mask_store,
):
    for store in (first_store, second_store, mask_store):
        store[...] = jnp.zeros_like(store)

    def put(store):
        def write(a, e, value):
            if len(store.shape) == 3:
                store[lane_of(a, e)] = value
            else:
                store[lane_of(a, e) : lane_of(a, e) + 1, :] = value

        return write

    edges = (low_ref, high_ref, below_ref, above_ref)
    place_bricks(put(first_store), EARLY, 0, first_ref, *edges)
    place_bricks(put(second_store), EARLY, 1, second_ref, *edges)
    place_bricks(put(mask_store), EARLY, 2, mask_ref, *edges)
    to_lanes(first_store, first_lanes)
    to_lanes(second_store, second_lanes)
    mask_lanes[...] = mask_store[...].T[:8, :]


def gather_early(first, second, mask, edges):
    lanes = jax.ShapeDtypeStruct((8 * LANES, SPAN), jnp.float32)
    return pl.pallas_call(
        gather_early_kernel,
        out_shape=(lanes, lanes, jax.ShapeDtypeStruct((8, SPAN), jnp.float32)),
        scratch_shapes=[
            pltpu.VMEM((SPAN, 8, LANES), jnp.float32),
            pltpu.VMEM((SPAN, 8, LANES), jnp.float32),
            pltpu.VMEM((SPAN, LANES), jnp.float32),
        ],
        compiler_params=pltpu.CompilerParams(vmem_limit_bytes=10 << 20),
        cost_estimate=pl.CostEstimate(flops=2_000_000, bytes_accessed=3_000_000, transcendentals=0),
        name="gather_early",
    )(first, second, mask, *edges)


def relay_kernel(sections, count, *refs):
    owns, low, high, to_low, to_high = refs[:count], *refs[count:]
    fill_across(sections, owns, low, high, to_low, to_high)


def relay(sections, owns, low, high, name):
    out = jax.ShapeDtypeStruct((message_rows(sections, across_rows), LANES), jnp.float32)
    return pl.pallas_call(
        functools.partial(relay_kernel, sections, len(owns)),
        out_shape=(out, out),
        compiler_params=pltpu.CompilerParams(vmem_limit_bytes=4 << 20),
        name=name,
    )(*owns, low, high)


def along_messages(sections, owns):
    to_low, to_high = [], []
    for (rows, depth), own in zip(sections, owns):
        flat = own.reshape(-1, LANES)
        used = rows * depth * BY
        blank = ((0, padded(used) - used), (0, 0))
        to_low.append(jnp.pad(flat[:used], blank))
        to_high.append(jnp.pad(flat[flat.shape[0] - used :], blank))
    return jnp.concatenate(to_low), jnp.concatenate(to_high)


def swap(to_low, to_high, axis):
    count = lax.axis_size(axis)
    up = [(i, i + 1) for i in range(count - 1)]
    down = [(b, a) for a, b in up]
    return lax.ppermute(to_high, axis, up), lax.ppermute(to_low, axis, down)


def moments_kernel(
    got_ref, first_ref, second_ref, third_ref, moments_ref, vectors_ref, low_ref, high_ref, turned, lanes_ref
):
    for power, record in enumerate((first_ref, second_ref, third_ref)):
        for t in range(8):
            block = jnp.concatenate([record[:, t, :], jnp.zeros((LANES - BX * BY, LANES), jnp.float32)], axis=0)
            lanes_ref[power, t * LANES : (t + 1) * LANES, :] = block.T
    sources = got_ref.shape[0]
    for group in range(sources // 4):
        for half in range(2):
            block = got_ref[4 * group : 4 * group + 4, half * FEAT : (half + 1) * FEAT, :]
            turned[half, group] = block.reshape(LANES, LANES).T
    sums = []
    for half in range(2):
        total = jnp.zeros((FEAT, LANES), jnp.float32)
        for source in range(sources):
            feats = got_ref[source, half * FEAT : (half + 1) * FEAT, :].astype(jnp.float32)
            target = got_ref[source, 2 * FEAT : 2 * FEAT + 2, :].astype(jnp.float32)
            total = total + feats * target[half : half + 1, :]
        sums.append(total)

    groups = turned.shape[1]
    row = lax.broadcasted_iota(jnp.int32, (1, 16, LANES), 1)
    upper = (row < SLOTS).astype(jnp.float32).astype(jnp.bfloat16)
    lower = (row >= SLOTS).astype(jnp.float32).astype(jnp.bfloat16)
    lane_group = lax.broadcasted_iota(jnp.int32, (1, LANES), 1) // FEAT
    for half in range(2):
        for pair in range(8):
            points = turned[half, :, 16 * pair : 16 * pair + 16, :]
            left = points.reshape(groups * 16, LANES)
            right = jnp.concatenate(
                [(points * upper).reshape(groups * 16, LANES), (points * lower).reshape(groups * 16, LANES)],
                axis=1,
            )
            product = lax.dot_general(
                left, right, (((0,), (0,)), ((), ())), preferred_element_type=jnp.float32
            )
            for k in range(2):
                square = product[:, k * LANES : (k + 1) * LANES]
                own = jnp.zeros((FEAT, LANES), jnp.float32)
                for q in range(4):
                    own = own + jnp.where(lane_group == q, square[q * FEAT : (q + 1) * FEAT, :], 0.0)
                moments_ref[half * 16 + 2 * pair + k] = spread_rows(own, lane_group)
    point = lax.broadcasted_iota(jnp.int32, (LANES, LANES), 0) // SLOTS
    lane = lax.broadcasted_iota(jnp.int32, (LANES, LANES), 1)
    values = jnp.zeros((FEAT, LANES), jnp.float32)
    for half in range(2):
        spread = (lane == point + half * 16).astype(jnp.float32)
        values = values + jnp.dot(
            sums[half], spread, precision=HIGHEST, preferred_element_type=jnp.float32
        )
    applied = [times(lanes_ref.at[power], values) for power in range(3)]
    vectors = jnp.concatenate([*applied, values], axis=0).T
    vectors_ref[...] = vectors[: BX * BY, :]
    depth = LATE[0][1] * BY
    for k in range(depth):
        low_ref[8 * k : 8 * k + 8, :] = moments_ref[k]
        high_ref[8 * k : 8 * k + 8, :] = moments_ref[BX * BY - depth + k]
    deep = LATE[1][1] * BY
    blank = jnp.zeros((padded(deep) - deep, LANES), jnp.float32)
    low_ref[8 * depth :, :] = jnp.concatenate([vectors[:deep], blank], axis=0)
    high_ref[8 * depth :, :] = jnp.concatenate([vectors[BX * BY - deep : BX * BY], blank], axis=0)


def find_moments(got, records):
    devices = got.shape[0]
    bricks = BX * BY
    message = jax.ShapeDtypeStruct((message_rows(LATE, along_rows), LANES), jnp.float32)
    return pl.pallas_call(
        moments_kernel,
        out_shape=(
            jax.ShapeDtypeStruct((bricks, 8, LANES), jnp.float32),
            jax.ShapeDtypeStruct((bricks, LANES), jnp.float32),
            message,
            message,
        ),
        scratch_shapes=[
            pltpu.VMEM((2, devices // 4, LANES, LANES), jnp.bfloat16),
            pltpu.VMEM((3, 8 * LANES, LANES), jnp.float32),
        ],
        compiler_params=pltpu.CompilerParams(vmem_limit_bytes=12 << 20),
        cost_estimate=pl.CostEstimate(flops=1_000_000_000, bytes_accessed=12_000_000, transcendentals=0),
        name="moments",
    )(got, *records)


def power_of_two(value):
    scale = jnp.ones_like(value)
    inverse = jnp.ones_like(value)
    for k in (64, 32, 16, 8, 4, 2, 1):
        up, down = 2.0**k, 2.0**-k
        large = value * down >= 1.0
        small = value * up <= 1.0
        value = jnp.where(large, value * down, jnp.where(small, value * up, value))
        scale = jnp.where(large, scale * up, jnp.where(small, scale * down, scale))
        inverse = jnp.where(large, inverse * down, jnp.where(small, inverse * up, inverse))
    return scale, inverse


def krylov_kernel(
    moments_ref, vectors_ref, low_ref, high_ref, below_ref, above_ref, first_ref, second_ref, mask_ref,
    feats_ref, reg_ref, basis_ref, message_ref, moment_store, vector_store, moment_lanes,
):
    moment_store[...] = jnp.zeros_like(moment_store)
    vector_store[...] = jnp.zeros_like(vector_store)

    def put_moment(a, e, value):
        moment_store[lane_of(a, e)] = value

    def put_vector(a, e, value):
        vector_store[lane_of(a, e) : lane_of(a, e) + 1, :] = value

    edges = (low_ref, high_ref, below_ref, above_ref)
    place_bricks(put_moment, LATE, 0, moments_ref, *edges)
    place_bricks(put_vector, LATE, 1, vectors_ref, *edges)
    to_lanes(moment_store, moment_lanes)
    vectors = vector_store[...].T
    masks = mask_ref[...]

    def system(z):
        near = masks[0:1] * pltpu.roll(z, PITCH, 1) + masks[1:2] * pltpu.roll(z, SPAN - PITCH, 1)
        near = near + masks[2:3] * pltpu.roll(z, 1, 1) + masks[3:4] * pltpu.roll(z, SPAN - 1, 1)
        return times(moment_lanes, z) + coupling_weight * (masks[4:5] * z - near)

    one = system(vectors[0:FEAT])
    two = system(times(first_ref, one) + vectors[FEAT : 2 * FEAT])
    three = system(times(first_ref, two) + times(second_ref, one) + vectors[2 * FEAT : 3 * FEAT])
    chain = (vectors[3 * FEAT :], one, two, three)
    for b in range(BX * BY):
        lane = lane_of(b // BY, b % BY)
        feats = feats_ref[b]
        for step, values in enumerate(chain):
            basis_ref[step, b : b + 1, :] = jnp.sum(feats * values[:, lane : lane + 1], axis=0, keepdims=True)
    reg = reg_ref[...]
    basis = [basis_ref[0]]
    for step in range(1, 4):
        basis.append(basis_ref[step] + reg * basis[-1])
        basis_ref[step] = basis[-1]

    def folded(x, combine):
        rows = [x[8 * k : 8 * k + 8, :] for k in range(x.shape[0] // 8)]
        parts = [r[:, LANES * k : LANES * (k + 1)] for r in rows for k in range(x.shape[1] // LANES)]
        while len(parts) > 1:
            parts = [combine(parts[k], parts[k + 1]) for k in range(0, len(parts), 2)]
        return parts[0]

    peaks = [jnp.max(folded(jnp.abs(v), jnp.maximum), axis=0, keepdims=True) for v in basis]
    peaks = jnp.max(jnp.concatenate(peaks + peaks, axis=0), axis=1, keepdims=True)
    scale, inverse = power_of_two(jnp.broadcast_to(peaks, (8, LANES)))
    scaled = [v * inverse[k : k + 1, 0:1] for k, v in enumerate(basis)]
    sums = [jnp.sum(folded(scaled[a] * scaled[b], jnp.add), axis=0, keepdims=True) for a, b in PAIRS]
    sums = jnp.concatenate(sums + [jnp.zeros((16 - len(PAIRS), LANES), jnp.float32)], axis=0)
    sums = jnp.sum(sums, axis=1, keepdims=True)
    lane = lax.broadcasted_iota(jnp.int32, (1, LANES), 1)
    row = jnp.zeros((1, LANES), jnp.float32)
    for k in range(len(PAIRS)):
        row = jnp.where(lane == k, sums[k : k + 1, :], row)
    for k in range(4):
        row = jnp.where(lane == 10 + k, scale[k : k + 1, :], row)
        row = jnp.where(lane == 14 + k, inverse[k : k + 1, :], row)
    message_ref[...] = jnp.broadcast_to(row, message_ref.shape)


def krylov(moments, vectors, edges, first, second, masks, voxel_feats, voxel_reg, devices):
    bricks, _, voxels = voxel_feats.shape
    return pl.pallas_call(
        krylov_kernel,
        out_shape=(
            jax.ShapeDtypeStruct((4, bricks, voxels), jnp.float32),
            jax.ShapeDtypeStruct((devices, LANES), jnp.float32),
        ),
        scratch_shapes=[
            pltpu.VMEM((SPAN, 8, LANES), jnp.float32),
            pltpu.VMEM((SPAN, LANES), jnp.float32),
            pltpu.VMEM((8 * LANES, SPAN), jnp.float32),
        ],
        compiler_params=pltpu.CompilerParams(vmem_limit_bytes=12 << 20),
        name="krylov",
    )(moments, vectors, *edges, first, second, masks, voxel_feats, voxel_reg)


def finish_kernel(shared_ref, basis_ref, solution_ref, residual_ref):
    shared = shared_ref[...]
    lane = lax.broadcasted_iota(jnp.int32, (1, LANES), 1)

    def pick(row, k):
        return jnp.sum(jnp.where(lane == k, row, 0.0), axis=1, keepdims=True)

    largest = jnp.max(shared, axis=0, keepdims=True)
    smallest = jnp.min(shared, axis=0, keepdims=True)
    scale = [pick(largest, 10 + k) for k in range(4)]
    inverse = [pick(smallest, 14 + k) for k in range(4)]
    weight = [shared[:, 10 + k : 11 + k] * inverse[k] for k in range(4)]
    left = jnp.zeros_like(shared)
    right = jnp.zeros_like(shared)
    for k, (a, b) in enumerate(PAIRS):
        left = jnp.where(lane == k, weight[a], left)
        right = jnp.where(lane == k, weight[b], right)
    total = jnp.sum(shared * left * right, axis=0, keepdims=True)
    gram = [[None] * 4 for _ in range(4)]
    for k, (a, b) in enumerate(PAIRS):
        gram[a][b] = gram[b][a] = pick(total, k)
    growth = [scale[k + 1] * inverse[k] for k in range(3)]

    def product(left, right):
        terms = [
            left[a] * right[b] * gram[a][b]
            for a in range(4)
            for b in range(4)
            if left[a] is not None and right[b] is not None
        ]
        return functools.reduce(jnp.add, terms)

    def plus(left, factor, right):
        out = []
        for a, b in zip(left, right):
            out.append(a if b is None else factor * b if a is None else a + factor * b)
        return out

    def image(vector):
        return [None] + [None if vector[k] is None else vector[k] * growth[k] for k in range(3)]

    solution = [None] * 4
    residual = [jnp.ones((1, 1), jnp.float32), None, None, None]
    direction = list(residual)
    norm_now = product(residual, residual)
    for iteration in range(ITERS):
        carried = image(direction)
        alpha = norm_now / product(direction, carried)
        solution = plus(solution, alpha, direction)
        residual = plus(residual, -alpha, carried)
        if iteration + 1 < ITERS:
            norm_next = product(residual, residual)
            direction = plus(residual, norm_next / norm_now, direction)
            norm_now = norm_next
    back = [scale[0] * inverse[k] for k in range(4)]
    for out_ref, coefficients in ((solution_ref, solution), (residual_ref, residual)):
        total = None
        for k, c in enumerate(coefficients):
            if c is not None:
                term = (c * back[k]) * basis_ref[k]
                total = term if total is None else total + term
        out_ref[...] = total


def finish(shared, basis):
    _, bricks, voxels = basis.shape
    out = jax.ShapeDtypeStruct((bricks, voxels), jnp.float32)
    return pl.pallas_call(
        finish_kernel,
        out_shape=(out, out),
        compiler_params=pltpu.CompilerParams(vmem_limit_bytes=4 << 20),
        name="finish",
    )(shared, basis)


def shards(point_feats, point_targets, point_lists, brick_adjacency, voxel_feats, voxel_reg):
    feat_count = point_feats.shape[0]
    brick_total, slots = point_lists.shape
    local_bricks = voxel_feats.shape[0]
    devices = brick_total // local_bricks
    sending = pack(point_feats, point_targets, point_lists, devices)
    got = lax.all_to_all(sending, GX_GY, split_axis=0, concat_axis=0, tiled=True)

    first, second, third = prepare(voxel_feats, voxel_reg)
    mask = (brick_adjacency >= 0).astype(jnp.float32)
    mask = jnp.concatenate([mask, jnp.sum(mask, axis=1, keepdims=True)], axis=1)
    mask = jnp.pad(mask, ((0, 0), (0, LANES - 5)))
    early = (first, second, mask)
    low, high = swap(*along_messages(EARLY, early), GX)
    across = relay(EARLY, early, low, high, "relay_early")
    got = lax.optimization_barrier((got, *across))[0]
    below, above = swap(*across, "gy")
    moments, vectors, to_low, to_high = find_moments(got, (first, second, third))
    to_low, to_high, below, above = lax.optimization_barrier((to_low, to_high, below, above))
    first_lanes, second_lanes, mask_lanes = gather_early(first, second, mask, (low, high, below, above))

    low, high = swap(to_low, to_high, GX)
    below, above = swap(*relay(LATE, (moments, vectors), low, high, "relay_late"), "gy")
    basis, message = krylov(
        moments, vectors, (low, high, below, above), first_lanes, second_lanes, mask_lanes,
        voxel_feats, voxel_reg, devices,
    )
    shared = lax.all_to_all(message, GX_GY, split_axis=0, concat_axis=0, tiled=True)
    return finish(shared, basis)


def solution(mesh):
    torus = Mesh(mesh.devices.reshape(4, 4, 2, mesh.shape["gy"]), ("gx_0", "gx_1", "gx_2", "gy"))
    return jax.shard_map(
        shards,
        mesh=torus,
        in_specs=(
            P(None, GX_GY),
            P(GX_GY),
            P(GX_GY, None),
            P(GX_GY, None),
            P(GX_GY, None, None),
            P(GX_GY, None),
        ),
        out_specs=(P(GX_GY, None), P(GX_GY, None)),
        check_vma=False,
    )
```

```python
import functools

import jax
import jax.numpy as jnp
from jax import lax
from jax.experimental import pallas as pl
from jax.experimental.pallas import tpu as pltpu
from jax.sharding import Mesh
from jax.sharding import PartitionSpec as P

BX = 8
BY = 4
ITERS = 3
SLOTS = 8
LANES = 128
FEAT = 32
PITCH = 16
SPAN = 256
REACH = 3
GX_GY = ("gx_0", "gx_1", "gx_2", "gy")
GX = ("gx_0", "gx_1", "gx_2")
HIGHEST = lax.Precision.HIGHEST
PAIRS = tuple((a, b) for a in range(4) for b in range(a, 4))


coupling_weight = 1.0

EARLY = ((8, 2, False), (8, 1, False), (1, 2, False))
LATE = ((8, 2, True), (1, 3, True))
CORNER_ROWS = 24


def padded(rows):
    return (rows + 7) // 8 * 8


def along_rows(section):
    return padded(section[0] * section[1] * BY)


def beyond(section, away):
    return section[1] - away if section[2] else 0


def across_rows(section):
    rows, depth, _ = section
    return padded(rows * sum(BX + 2 * beyond(section, k) for k in range(1, depth + 1)))


def message_rows(sections, size):
    return sum(size(section) for section in sections)


def piece(ref, start, rows, index):
    if rows == 8 and len(ref.shape) == 3:
        return ref[index]
    return ref[start + rows * index : start + rows * (index + 1), :]


def brick_at(own, low, high, start, section, a, e):
    rows, depth, _ = section
    if a < 0:
        return piece(low, start, rows, (a + depth) * BY + e)
    if a >= BX:
        return piece(high, start, rows, (a - BX) * BY + e)
    return piece(own, 0, rows, a * BY + e)


def fill_across(sections, owns, low, high, to_low, to_high):
    source = target = 0
    for section, own in zip(sections, owns):
        rows, depth, _ = section
        index = 0
        for away in range(1, depth + 1):
            extra = beyond(section, away)
            for a in range(-extra, BX + extra):
                place = slice(target + rows * index, target + rows * (index + 1))
                to_low[place, :] = brick_at(own, low, high, source, section, a, away - 1)
                to_high[place, :] = brick_at(own, low, high, source, section, a, BY - away)
                index += 1
        used, whole = rows * index, across_rows(section)
        if used < whole:
            blank = jnp.zeros((whole - used, LANES), jnp.float32)
            to_low[target + used : target + whole, :] = blank
            to_high[target + used : target + whole, :] = blank
        source += along_rows(section)
        target += whole


def place_bricks(put, sections, which, own, along_low, along_high, across_low, across_high):
    section = sections[which]
    rows, depth, _ = section
    start = message_rows(sections[:which], along_rows)
    for a in range(-depth, BX + depth):
        for e in range(BY):
            put(a, e, brick_at(own, along_low, along_high, start, section, a, e))
    start = message_rows(sections[:which], across_rows)
    index = 0
    for away in range(1, depth + 1):
        extra = beyond(section, away)
        for a in range(-extra, BX + extra):
            put(a, -away, piece(across_low, start, rows, index))
            put(a, BY - 1 + away, piece(across_high, start, rows, index))
            index += 1


def lane_of(a, e):
    return (a + REACH) * PITCH + e + REACH


def to_lanes(records, lanes_ref):
    for t in range(8):
        lanes_ref[t * LANES : (t + 1) * LANES, :] = records[:, t, :].T


def times(matrix_ref, vector):
    total = None
    for t in range(8):
        for q in range(4):
            i = 8 * q + t
            row = t * LANES + q * FEAT
            term = matrix_ref[row : row + FEAT, :] * vector[i : i + 1, :]
            total = term if total is None else total + term
    return total


def pack_kernel(lists_ref, feats_ref, targets_ref, out_ref, feats, packed, arrived, left):
    steps = arrived.shape[0]
    devices = out_ref.shape[0]
    bricks = lists_ref.shape[1]
    dests = devices // steps
    width = LANES * SLOTS
    points = bricks * SLOTS // steps
    arriving = [
        pltpu.make_async_copy(
            feats_ref.at[:, k * points : (k + 1) * points], feats.at[:, k * points : (k + 1) * points], arrived.at[k]
        )
        for k in range(steps)
    ]
    leaving = [
        pltpu.make_async_copy(
            packed.at[k * dests : (k + 1) * dests], out_ref.at[k * dests : (k + 1) * dests], left.at[k]
        )
        for k in range(steps)
    ]
    for copy in arriving:
        copy.start()
    rows = bricks // LANES
    lane = lax.broadcasted_iota(jnp.int32, (SLOTS, LANES), 1)
    codes = []
    for block in range(rows):
        chosen = lists_ref[:, block * LANES : (block + 1) * LANES]
        offset = chosen - (lane + block * LANES) * SLOTS
        bits = jnp.where(chosen >= 0, lax.shift_left(1, jnp.clip(offset, 0, SLOTS - 1)), 0)
        codes.append(jnp.sum(bits, axis=0, keepdims=True))
    code = jnp.concatenate(codes, axis=0).astype(jnp.float32).astype(jnp.bfloat16)
    brick = lax.broadcasted_iota(jnp.int32, (LANES, width), 0)
    point = lax.broadcasted_iota(jnp.int32, (LANES, width), 1)
    spread = (lax.shift_right_logical(point, 3) == brick).astype(jnp.float32).astype(jnp.bfloat16)
    wide = jnp.dot(code, spread, preferred_element_type=jnp.float32).astype(jnp.int32)
    slot = lax.broadcasted_iota(jnp.int32, (rows, width), 1) & (SLOTS - 1)
    mask = (lax.shift_right_logical(wide, slot) & 1).astype(jnp.float32)
    for k in range(steps):
        arriving[k].wait()
        for part in range(points // width):
            first = k * points + part * width
            row = mask[first // width : first // width + 1, :].astype(jnp.bfloat16)
            masked = feats[:, first : first + width] * row
            for piece_index in range(width // LANES):
                dest = (first + piece_index * LANES) // (2 * LANES)
                half = piece_index % 2
                packed[dest, half * FEAT : (half + 1) * FEAT, :] = masked[
                    :, piece_index * LANES : (piece_index + 1) * LANES
                ]
        for dest in range(k * dests, (k + 1) * dests):
            packed[dest, 2 * FEAT : 2 * FEAT + 2, :] = targets_ref[2 * dest : 2 * dest + 2, :]
        leaving[k].start()
    for copy in leaving:
        copy.wait()


def pack(point_feats, point_targets, point_lists, devices):
    points = point_feats.shape[1]
    steps = 8
    rows = 2 * FEAT + 2
    return pl.pallas_call(
        pack_kernel,
        in_specs=[
            pl.BlockSpec(memory_space=pltpu.VMEM),
            pl.BlockSpec(memory_space=pl.ANY),
            pl.BlockSpec(memory_space=pltpu.VMEM),
        ],
        out_specs=pl.BlockSpec(memory_space=pl.ANY),
        out_shape=jax.ShapeDtypeStruct((devices, rows, LANES), jnp.bfloat16),
        scratch_shapes=[
            pltpu.VMEM((FEAT, points), jnp.bfloat16),
            pltpu.VMEM((devices, rows, LANES), jnp.bfloat16),
            pltpu.SemaphoreType.DMA((steps,)),
            pltpu.SemaphoreType.DMA((steps,)),
        ],
        name="pack",
    )(point_lists.T, point_feats, point_targets.reshape(points // LANES, LANES))


def spread_rows(square, lane_group):
    square = square + pltpu.roll(square, 64, 1)
    square = square + pltpu.roll(square, 32, 1)
    record = square[0:8, :]
    for q in range(1, 4):
        record = jnp.where(lane_group == q, square[8 * q : 8 * q + 8, :], record)
    return record


def three_parts(x):
    high = x.astype(jnp.bfloat16)
    rest = x - high.astype(jnp.float32)
    middle = rest.astype(jnp.bfloat16)
    return high, middle, (rest - middle.astype(jnp.float32)).astype(jnp.bfloat16)


def prepare_kernel(feats_ref, reg_ref, *records):

    lane_group = lax.broadcasted_iota(jnp.int32, (1, LANES), 1) // FEAT
    together = 4

    def some(step, carry):
        for k in range(together):
            b = step * together + k
            feats = feats_ref[b]
            reg = reg_ref[pl.ds(b, 1), :]
            once = feats * reg
            parts = three_parts(jnp.concatenate([feats, once, once * reg], axis=0))
            left = jnp.concatenate(parts, axis=0)
            right = [part[:FEAT, :] for part in parts]
            right = jnp.concatenate([*right, jnp.zeros_like(right[0])], axis=0)
            product = lax.dot_general(
                left, right, (((1,), (1,)), ((), ())), preferred_element_type=jnp.float32
            )
            size = 3 * FEAT
            total = jnp.where(lane_group < 1, product[2 * size :, :], 0.0)
            total = total + jnp.where(lane_group < 2, product[size : 2 * size, :], 0.0)
            total = total + product[:size, :]
            for power, record in enumerate(records):
                record[b] = spread_rows(total[power * FEAT : (power + 1) * FEAT, :], lane_group)
        return carry

    lax.fori_loop(0, feats_ref.shape[0] // together, some, 0)


def prepare(voxel_feats, voxel_reg):
    bricks = voxel_feats.shape[0]
    record = jax.ShapeDtypeStruct((bricks, 8, LANES), jnp.float32)
    return pl.pallas_call(
        prepare_kernel,
        out_shape=(record, record, record),
        compiler_params=pltpu.CompilerParams(vmem_limit_bytes=10 << 20),
        cost_estimate=pl.CostEstimate(flops=600_000_000, bytes_accessed=5_000_000, transcendentals=0),
        name="prepare",
    )(voxel_feats, voxel_reg)


def gather_early_kernel(
    first_ref, second_ref, mask_ref, low_ref, high_ref, below_ref, above_ref,
    first_lanes, second_lanes, mask_lanes, first_store, second_store, mask_store,
):
    for store in (first_store, second_store, mask_store):
        store[...] = jnp.zeros_like(store)

    def put(store):
        def write(a, e, value):
            if len(store.shape) == 3:
                store[lane_of(a, e)] = value
            else:
                store[lane_of(a, e) : lane_of(a, e) + 1, :] = value

        return write

    edges = (low_ref, high_ref, below_ref, above_ref)
    place_bricks(put(first_store), EARLY, 0, first_ref, *edges)
    place_bricks(put(second_store), EARLY, 1, second_ref, *edges)
    place_bricks(put(mask_store), EARLY, 2, mask_ref, *edges)
    to_lanes(first_store, first_lanes)
    to_lanes(second_store, second_lanes)
    mask_lanes[...] = mask_store[...].T[:8, :]


def gather_early(first, second, mask, edges):
    lanes = jax.ShapeDtypeStruct((8 * LANES, SPAN), jnp.float32)
    return pl.pallas_call(
        gather_early_kernel,
        out_shape=(lanes, lanes, jax.ShapeDtypeStruct((8, SPAN), jnp.float32)),
        scratch_shapes=[
            pltpu.VMEM((SPAN, 8, LANES), jnp.float32),
            pltpu.VMEM((SPAN, 8, LANES), jnp.float32),
            pltpu.VMEM((SPAN, LANES), jnp.float32),
        ],
        compiler_params=pltpu.CompilerParams(vmem_limit_bytes=10 << 20),
        cost_estimate=pl.CostEstimate(flops=2_000_000, bytes_accessed=3_000_000, transcendentals=0),
        name="gather_early",
    )(first, second, mask, *edges)


def across_early_kernel(first_ref, second_ref, mask_ref, to_low, to_high):
    fill_across(EARLY, (first_ref, second_ref, mask_ref), None, None, to_low, to_high)


def across_early(owns):
    out = jax.ShapeDtypeStruct((message_rows(EARLY, across_rows), LANES), jnp.float32)
    return pl.pallas_call(
        across_early_kernel,
        out_shape=(out, out),
        compiler_params=pltpu.CompilerParams(vmem_limit_bytes=4 << 20),
        name="across_early",
    )(*owns)


def across_late_kernel(moments_ref, vectors_ref, low, high, early_low, early_high, to_low, to_high):
    fill_across(LATE, (moments_ref, vectors_ref), low, high, to_low, to_high)
    start = message_rows(LATE, across_rows)
    masks = message_rows(EARLY[:2], along_rows)
    for out, e in ((to_low, 0), (to_high, BY - 1)):
        rows = []
        for k, (source, index) in enumerate(((early_low, BY + e), (early_high, e))):
            out[start + 8 * k : start + 8 * k + 8, :] = source[8 * index : 8 * index + 8, :]
            rows.append(source[masks + index : masks + index + 1, :])
        rows.append(jnp.zeros((6, LANES), jnp.float32))
        out[start + 16 : start + CORNER_ROWS, :] = jnp.concatenate(rows, axis=0)


def across_late(moments, vectors, low, high, early_low, early_high):
    out = jax.ShapeDtypeStruct((message_rows(LATE, across_rows) + CORNER_ROWS, LANES), jnp.float32)
    return pl.pallas_call(
        across_late_kernel,
        out_shape=(out, out),
        compiler_params=pltpu.CompilerParams(vmem_limit_bytes=4 << 20),
        name="across_late",
    )(moments, vectors, low, high, early_low, early_high)


def along_messages(sections, owns):
    to_low, to_high = [], []
    for (rows, depth, _), own in zip(sections, owns):
        flat = own.reshape(-1, LANES)
        used = rows * depth * BY
        blank = ((0, padded(used) - used), (0, 0))
        to_low.append(jnp.pad(flat[:used], blank))
        to_high.append(jnp.pad(flat[flat.shape[0] - used :], blank))
    return jnp.concatenate(to_low), jnp.concatenate(to_high)


def swap(to_low, to_high, axis, even):
    count = lax.axis_size(axis)

    def pairs(start):
        return [pair for a in range(start, count - 1, 2) for pair in ((a, a + 1), (a + 1, a))]

    first = lax.ppermute(jnp.where(even, to_high, to_low), axis, pairs(0))
    second = lax.ppermute(jnp.where(even, to_low, to_high), axis, pairs(1))
    return jnp.where(even, second, first), jnp.where(even, first, second)


def moments_kernel(
    got_ref, first_ref, second_ref, third_ref, moments_ref, vectors_ref, low_ref, high_ref, turned, lanes_ref
):
    for power, record in enumerate((first_ref, second_ref, third_ref)):
        for t in range(8):
            block = jnp.concatenate([record[:, t, :], jnp.zeros((LANES - BX * BY, LANES), jnp.float32)], axis=0)
            lanes_ref[power, t * LANES : (t + 1) * LANES, :] = block.T
    sources = got_ref.shape[0]
    for group in range(sources // 4):
        for half in range(2):
            block = got_ref[4 * group : 4 * group + 4, half * FEAT : (half + 1) * FEAT, :]
            turned[half, group] = block.reshape(LANES, LANES).T
    sums = []
    for half in range(2):
        total = jnp.zeros((FEAT, LANES), jnp.float32)
        for source in range(sources):
            feats = got_ref[source, half * FEAT : (half + 1) * FEAT, :].astype(jnp.float32)
            target = got_ref[source, 2 * FEAT : 2 * FEAT + 2, :].astype(jnp.float32)
            total = total + feats * target[half : half + 1, :]
        sums.append(total)

    groups = turned.shape[1]
    row = lax.broadcasted_iota(jnp.int32, (1, 16, LANES), 1)
    upper = (row < SLOTS).astype(jnp.float32).astype(jnp.bfloat16)
    lower = (row >= SLOTS).astype(jnp.float32).astype(jnp.bfloat16)
    lane_group = lax.broadcasted_iota(jnp.int32, (1, LANES), 1) // FEAT
    for half in range(2):
        for pair in range(8):
            points = turned[half, :, 16 * pair : 16 * pair + 16, :]
            left = points.reshape(groups * 16, LANES)
            right = jnp.concatenate(
                [(points * upper).reshape(groups * 16, LANES), (points * lower).reshape(groups * 16, LANES)],
                axis=1,
            )
            product = lax.dot_general(
                left, right, (((0,), (0,)), ((), ())), preferred_element_type=jnp.float32
            )
            for k in range(2):
                square = product[:, k * LANES : (k + 1) * LANES]
                own = jnp.zeros((FEAT, LANES), jnp.float32)
                for q in range(4):
                    own = own + jnp.where(lane_group == q, square[q * FEAT : (q + 1) * FEAT, :], 0.0)
                moments_ref[half * 16 + 2 * pair + k] = spread_rows(own, lane_group)
    point = lax.broadcasted_iota(jnp.int32, (LANES, LANES), 0) // SLOTS
    lane = lax.broadcasted_iota(jnp.int32, (LANES, LANES), 1)
    values = jnp.zeros((FEAT, LANES), jnp.float32)
    for half in range(2):
        spread = (lane == point + half * 16).astype(jnp.float32)
        values = values + jnp.dot(
            sums[half], spread, precision=HIGHEST, preferred_element_type=jnp.float32
        )
    applied = [times(lanes_ref.at[power], values) for power in range(3)]
    vectors = jnp.concatenate([*applied, values], axis=0).T
    vectors_ref[...] = vectors[: BX * BY, :]
    depth = LATE[0][1] * BY
    for k in range(depth):
        low_ref[8 * k : 8 * k + 8, :] = moments_ref[k]
        high_ref[8 * k : 8 * k + 8, :] = moments_ref[BX * BY - depth + k]
    deep = LATE[1][1] * BY
    blank = jnp.zeros((padded(deep) - deep, LANES), jnp.float32)
    low_ref[8 * depth :, :] = jnp.concatenate([vectors[:deep], blank], axis=0)
    high_ref[8 * depth :, :] = jnp.concatenate([vectors[BX * BY - deep : BX * BY], blank], axis=0)


def find_moments(got, records):
    devices = got.shape[0]
    bricks = BX * BY
    message = jax.ShapeDtypeStruct((message_rows(LATE, along_rows), LANES), jnp.float32)
    return pl.pallas_call(
        moments_kernel,
        out_shape=(
            jax.ShapeDtypeStruct((bricks, 8, LANES), jnp.float32),
            jax.ShapeDtypeStruct((bricks, LANES), jnp.float32),
            message,
            message,
        ),
        scratch_shapes=[
            pltpu.VMEM((2, devices // 4, LANES, LANES), jnp.bfloat16),
            pltpu.VMEM((3, 8 * LANES, LANES), jnp.float32),
        ],
        compiler_params=pltpu.CompilerParams(vmem_limit_bytes=12 << 20),
        cost_estimate=pl.CostEstimate(flops=1_000_000_000, bytes_accessed=12_000_000, transcendentals=0),
        name="moments",
    )(got, *records)


def power_of_two(value):
    scale = jnp.ones_like(value)
    inverse = jnp.ones_like(value)
    for k in (64, 32, 16, 8, 4, 2, 1):
        up, down = 2.0**k, 2.0**-k
        large = value * down >= 1.0
        small = value * up <= 1.0
        value = jnp.where(large, value * down, jnp.where(small, value * up, value))
        scale = jnp.where(large, scale * up, jnp.where(small, scale * down, scale))
        inverse = jnp.where(large, inverse * down, jnp.where(small, inverse * up, inverse))
    return scale, inverse


def krylov_kernel(
    moments_ref, vectors_ref, low_ref, high_ref, below_ref, above_ref, first_ref, second_ref, mask_ref,
    feats_ref, reg_ref, basis_ref, message_ref, moment_store, vector_store, moment_lanes,
    corner_store, corner_masks, corner_lanes,
):
    moment_store[...] = jnp.zeros_like(moment_store)
    corner_store[...] = jnp.zeros_like(corner_store)
    corner_masks[...] = jnp.zeros_like(corner_masks)
    vector_store[...] = jnp.zeros_like(vector_store)

    def put_moment(a, e, value):
        moment_store[lane_of(a, e)] = value

    def put_vector(a, e, value):
        vector_store[lane_of(a, e) : lane_of(a, e) + 1, :] = value

    edges = (low_ref, high_ref, below_ref, above_ref)
    place_bricks(put_moment, LATE, 0, moments_ref, *edges)
    place_bricks(put_vector, LATE, 1, vectors_ref, *edges)
    start = message_rows(LATE, across_rows)
    for ref, e in ((below_ref, -1), (above_ref, BY)):
        for k, a in enumerate((-1, BX)):
            place = lane_of(a, e) % LANES
            corner_store[place] = ref[start + 8 * k : start + 8 * k + 8, :]
            corner_masks[place : place + 1, :] = ref[start + 16 + k : start + 17 + k, :]
    to_lanes(moment_store, moment_lanes)
    to_lanes(corner_store, corner_lanes)
    vectors = vector_store[...].T
    lane = lax.broadcasted_iota(jnp.int32, (1, LANES), 1)
    front = (lane == lane_of(-1, -1)) | (lane == lane_of(-1, BY))
    rear = (lane == lane_of(BX, -1) % LANES) | (lane == lane_of(BX, BY) % LANES)

    def both_tiles(x):
        return jnp.concatenate([jnp.where(front, x, 0.0), jnp.where(rear, x, 0.0)], axis=1)

    masks = mask_ref[...] + both_tiles(corner_masks[...].T[:8, :])

    def system(z):
        near = masks[0:1] * pltpu.roll(z, PITCH, 1) + masks[1:2] * pltpu.roll(z, SPAN - PITCH, 1)
        near = near + masks[2:3] * pltpu.roll(z, 1, 1) + masks[3:4] * pltpu.roll(z, SPAN - 1, 1)
        return times(moment_lanes, z) + coupling_weight * (masks[4:5] * z - near)

    one = system(vectors[0:FEAT])
    corners = times(corner_lanes, jnp.where(front, one[:, :LANES], one[:, LANES:]))
    two = system(times(first_ref, one) + both_tiles(corners) + vectors[FEAT : 2 * FEAT])
    three = system(times(first_ref, two) + times(second_ref, one) + vectors[2 * FEAT : 3 * FEAT])
    chain = (vectors[3 * FEAT :], one, two, three)
    for b in range(BX * BY):
        place = lane_of(b // BY, b % BY)
        feats = feats_ref[b]
        for step, values in enumerate(chain):
            basis_ref[step, b : b + 1, :] = jnp.sum(feats * values[:, place : place + 1], axis=0, keepdims=True)
    reg = reg_ref[...]
    basis = [basis_ref[0]]
    for step in range(1, 4):
        basis.append(basis_ref[step] + reg * basis[-1])
        basis_ref[step] = basis[-1]

    def folded(x, combine):
        rows = [x[8 * k : 8 * k + 8, :] for k in range(x.shape[0] // 8)]
        parts = [r[:, LANES * k : LANES * (k + 1)] for r in rows for k in range(x.shape[1] // LANES)]
        while len(parts) > 1:
            parts = [combine(parts[k], parts[k + 1]) for k in range(0, len(parts), 2)]
        return parts[0]

    peaks = [jnp.max(folded(jnp.abs(v), jnp.maximum), axis=0, keepdims=True) for v in basis]
    peaks = jnp.max(jnp.concatenate(peaks + peaks, axis=0), axis=1, keepdims=True)
    scale, inverse = power_of_two(jnp.broadcast_to(peaks, (8, LANES)))
    scaled = [v * inverse[k : k + 1, 0:1] for k, v in enumerate(basis)]
    sums = [jnp.sum(folded(scaled[a] * scaled[b], jnp.add), axis=0, keepdims=True) for a, b in PAIRS]
    sums = jnp.concatenate(sums + [jnp.zeros((16 - len(PAIRS), LANES), jnp.float32)], axis=0)
    sums = jnp.sum(sums, axis=1, keepdims=True)
    row = jnp.zeros((1, LANES), jnp.float32)
    for k in range(len(PAIRS)):
        row = jnp.where(lane == k, sums[k : k + 1, :], row)
    for k in range(4):
        row = jnp.where(lane == 10 + k, scale[k : k + 1, :], row)
        row = jnp.where(lane == 14 + k, inverse[k : k + 1, :], row)
    message_ref[...] = jnp.broadcast_to(row, message_ref.shape)


def krylov(moments, vectors, edges, first, second, masks, voxel_feats, voxel_reg, devices):
    bricks, _, voxels = voxel_feats.shape
    return pl.pallas_call(
        krylov_kernel,
        out_shape=(
            jax.ShapeDtypeStruct((4, bricks, voxels), jnp.float32),
            jax.ShapeDtypeStruct((devices, LANES), jnp.float32),
        ),
        scratch_shapes=[
            pltpu.VMEM((SPAN, 8, LANES), jnp.float32),
            pltpu.VMEM((SPAN, LANES), jnp.float32),
            pltpu.VMEM((8 * LANES, SPAN), jnp.float32),
            pltpu.VMEM((LANES, 8, LANES), jnp.float32),
            pltpu.VMEM((LANES, LANES), jnp.float32),
            pltpu.VMEM((8 * LANES, LANES), jnp.float32),
        ],
        compiler_params=pltpu.CompilerParams(vmem_limit_bytes=12 << 20),
        name="krylov",
    )(moments, vectors, *edges, first, second, masks, voxel_feats, voxel_reg)


def finish_kernel(shared_ref, basis_ref, solution_ref, residual_ref):
    shared = shared_ref[...]
    lane = lax.broadcasted_iota(jnp.int32, (1, LANES), 1)

    def pick(row, k):
        return jnp.sum(jnp.where(lane == k, row, 0.0), axis=1, keepdims=True)

    largest = jnp.max(shared, axis=0, keepdims=True)
    smallest = jnp.min(shared, axis=0, keepdims=True)
    scale = [pick(largest, 10 + k) for k in range(4)]
    inverse = [pick(smallest, 14 + k) for k in range(4)]
    weight = [shared[:, 10 + k : 11 + k] * inverse[k] for k in range(4)]
    left = jnp.zeros_like(shared)
    right = jnp.zeros_like(shared)
    for k, (a, b) in enumerate(PAIRS):
        left = jnp.where(lane == k, weight[a], left)
        right = jnp.where(lane == k, weight[b], right)
    total = jnp.sum(shared * left * right, axis=0, keepdims=True)
    gram = [[None] * 4 for _ in range(4)]
    for k, (a, b) in enumerate(PAIRS):
        gram[a][b] = gram[b][a] = pick(total, k)
    growth = [scale[k + 1] * inverse[k] for k in range(3)]

    def product(left, right):
        terms = [
            left[a] * right[b] * gram[a][b]
            for a in range(4)
            for b in range(4)
            if left[a] is not None and right[b] is not None
        ]
        return functools.reduce(jnp.add, terms)

    def plus(left, factor, right):
        out = []
        for a, b in zip(left, right):
            out.append(a if b is None else factor * b if a is None else a + factor * b)
        return out

    def image(vector):
        return [None] + [None if vector[k] is None else vector[k] * growth[k] for k in range(3)]

    solution = [None] * 4
    residual = [jnp.ones((1, 1), jnp.float32), None, None, None]
    direction = list(residual)
    norm_now = product(residual, residual)
    for iteration in range(ITERS):
        carried = image(direction)
        alpha = norm_now / product(direction, carried)
        solution = plus(solution, alpha, direction)
        residual = plus(residual, -alpha, carried)
        if iteration + 1 < ITERS:
            norm_next = product(residual, residual)
            direction = plus(residual, norm_next / norm_now, direction)
            norm_now = norm_next
    back = [scale[0] * inverse[k] for k in range(4)]
    for out_ref, coefficients in ((solution_ref, solution), (residual_ref, residual)):
        total = None
        for k, c in enumerate(coefficients):
            if c is not None:
                term = (c * back[k]) * basis_ref[k]
                total = term if total is None else total + term
        out_ref[...] = total


def finish(shared, basis):
    _, bricks, voxels = basis.shape
    out = jax.ShapeDtypeStruct((bricks, voxels), jnp.float32)
    return pl.pallas_call(
        finish_kernel,
        out_shape=(out, out),
        compiler_params=pltpu.CompilerParams(vmem_limit_bytes=4 << 20),
        name="finish",
    )(shared, basis)


def shards(point_feats, point_targets, point_lists, brick_adjacency, voxel_feats, voxel_reg):
    feat_count = point_feats.shape[0]
    brick_total, slots = point_lists.shape
    local_bricks = voxel_feats.shape[0]
    devices = brick_total // local_bricks
    sending = pack(point_feats, point_targets, point_lists, devices)
    got = lax.all_to_all(sending, GX_GY, split_axis=0, concat_axis=0, tiled=True)

    first, second, third = prepare(voxel_feats, voxel_reg)
    mask = (brick_adjacency >= 0).astype(jnp.float32)
    mask = jnp.concatenate([mask, jnp.sum(mask, axis=1, keepdims=True)], axis=1)
    mask = jnp.pad(mask, ((0, 0), (0, LANES - 5)))
    early = (first, second, mask)
    along_even = lax.axis_index("gx_2") == 0
    across_even = lax.axis_index("gy") % 2 == 0
    early_low, early_high = swap(*along_messages(EARLY, early), GX, along_even)
    early_below, early_above = swap(*across_early(early), "gy", across_even)

    moments, vectors, to_low, to_high = find_moments(got, (first, second, third))
    low, high = swap(to_low, to_high, GX, along_even)
    first_lanes, second_lanes, mask_lanes = gather_early(
        first, second, mask, (early_low, early_high, early_below, early_above)
    )
    below, above = swap(
        *across_late(moments, vectors, low, high, early_low, early_high), "gy", across_even
    )
    basis, message = krylov(
        moments, vectors, (low, high, below, above), first_lanes, second_lanes, mask_lanes,
        voxel_feats, voxel_reg, devices,
    )
    shared = lax.all_to_all(message, GX_GY, split_axis=0, concat_axis=0, tiled=True)
    return finish(shared, basis)


def solution(mesh):
    torus = Mesh(mesh.devices.reshape(4, 4, 2, mesh.shape["gy"]), ("gx_0", "gx_1", "gx_2", "gy"))
    return jax.shard_map(
        shards,
        mesh=torus,
        in_specs=(
            P(None, GX_GY),
            P(GX_GY),
            P(GX_GY, None),
            P(GX_GY, None),
            P(GX_GY, None, None),
            P(GX_GY, None),
        ),
        out_specs=(P(GX_GY, None), P(GX_GY, None)),
        check_vma=False,
    )
```

```python
import functools

import jax
import jax.numpy as jnp
from jax import lax
from jax.experimental import pallas as pl
from jax.experimental.pallas import tpu as pltpu
from jax.sharding import Mesh
from jax.sharding import PartitionSpec as P

BX = 8
BY = 4
ITERS = 3
SLOTS = 8
LANES = 128
FEAT = 32
PITCH = 16
SPAN = 256
REACH = 3
GX_GY = ("gx_0", "gx_1", "gx_2", "gy")
GX = ("gx_0", "gx_1", "gx_2")
HIGHEST = lax.Precision.HIGHEST
PAIRS = tuple((a, b) for a in range(4) for b in range(a, 4))


coupling_weight = 1.0

EARLY = ((8, 2, False), (8, 1, False), (1, 2, False))
LATE = ((8, 2, True), (1, 3, True))
CORNER_ROWS = 24


def padded(rows):
    return (rows + 7) // 8 * 8


def along_rows(section):
    return padded(section[0] * section[1] * BY)


def beyond(section, away):
    return section[1] - away if section[2] else 0


def across_rows(section):
    rows, depth, _ = section
    return padded(rows * sum(BX + 2 * beyond(section, k) for k in range(1, depth + 1)))


def message_rows(sections, size):
    return sum(size(section) for section in sections)


def piece(ref, start, rows, index):
    if rows == 8 and len(ref.shape) == 3:
        return ref[index]
    return ref[start + rows * index : start + rows * (index + 1), :]


def brick_at(own, low, high, start, section, a, e):
    rows, depth, _ = section
    if a < 0:
        return piece(low, start, rows, (a + depth) * BY + e)
    if a >= BX:
        return piece(high, start, rows, (a - BX) * BY + e)
    return piece(own, 0, rows, a * BY + e)


def fill_across(sections, owns, low, high, to_low, to_high):
    source = target = 0
    for section, own in zip(sections, owns):
        rows, depth, _ = section
        index = 0
        for away in range(1, depth + 1):
            extra = beyond(section, away)
            for a in range(-extra, BX + extra):
                place = slice(target + rows * index, target + rows * (index + 1))
                to_low[place, :] = brick_at(own, low, high, source, section, a, away - 1)
                to_high[place, :] = brick_at(own, low, high, source, section, a, BY - away)
                index += 1
        used, whole = rows * index, across_rows(section)
        if used < whole:
            blank = jnp.zeros((whole - used, LANES), jnp.float32)
            to_low[target + used : target + whole, :] = blank
            to_high[target + used : target + whole, :] = blank
        source += along_rows(section)
        target += whole


def place_bricks(put, sections, which, own, along_low, along_high, across_low, across_high):
    section = sections[which]
    rows, depth, _ = section
    start = message_rows(sections[:which], along_rows)
    for a in range(-depth, BX + depth):
        for e in range(BY):
            put(a, e, brick_at(own, along_low, along_high, start, section, a, e))
    start = message_rows(sections[:which], across_rows)
    index = 0
    for away in range(1, depth + 1):
        extra = beyond(section, away)
        for a in range(-extra, BX + extra):
            put(a, -away, piece(across_low, start, rows, index))
            put(a, BY - 1 + away, piece(across_high, start, rows, index))
            index += 1


def lane_of(a, e):
    return (a + REACH) * PITCH + e + REACH


def to_lanes(records, lanes_ref):
    for t in range(8):
        lanes_ref[t * LANES : (t + 1) * LANES, :] = records[:, t, :].T


def times(matrix_ref, vector):
    total = None
    for t in range(8):
        for q in range(4):
            i = 8 * q + t
            row = t * LANES + q * FEAT
            term = matrix_ref[row : row + FEAT, :] * vector[i : i + 1, :]
            total = term if total is None else total + term
    return total


def pack_kernel(
    lists_hbm, feats_ref, targets_hbm, out_ref, lists_ref, feats, targets_ref, packed, arrived, left, small
):
    steps = arrived.shape[0]
    lists_copy = pltpu.make_async_copy(lists_hbm, lists_ref, small.at[0])
    targets_copy = pltpu.make_async_copy(targets_hbm, targets_ref, small.at[1])
    lists_copy.start()
    targets_copy.start()
    devices = out_ref.shape[0]
    bricks = lists_ref.shape[1]
    dests = devices // steps
    width = LANES * SLOTS
    points = bricks * SLOTS // steps
    arriving = [
        pltpu.make_async_copy(
            feats_ref.at[:, k * points : (k + 1) * points], feats.at[:, k * points : (k + 1) * points], arrived.at[k]
        )
        for k in range(steps)
    ]
    leaving = [
        pltpu.make_async_copy(
            packed.at[k * dests : (k + 1) * dests], out_ref.at[k * dests : (k + 1) * dests], left.at[k]
        )
        for k in range(steps)
    ]
    for copy in arriving:
        copy.start()
    lists_copy.wait()
    rows = bricks // LANES
    lane = lax.broadcasted_iota(jnp.int32, (SLOTS, LANES), 1)
    codes = []
    for block in range(rows):
        chosen = lists_ref[:, block * LANES : (block + 1) * LANES]
        offset = chosen - (lane + block * LANES) * SLOTS
        bits = jnp.where(chosen >= 0, lax.shift_left(1, jnp.clip(offset, 0, SLOTS - 1)), 0)
        codes.append(jnp.sum(bits, axis=0, keepdims=True))
    code = jnp.concatenate(codes, axis=0).astype(jnp.float32).astype(jnp.bfloat16)
    brick = lax.broadcasted_iota(jnp.int32, (LANES, width), 0)
    point = lax.broadcasted_iota(jnp.int32, (LANES, width), 1)
    spread = (lax.shift_right_logical(point, 3) == brick).astype(jnp.float32).astype(jnp.bfloat16)
    wide = jnp.dot(code, spread, preferred_element_type=jnp.float32).astype(jnp.int32)
    slot = lax.broadcasted_iota(jnp.int32, (rows, width), 1) & (SLOTS - 1)
    mask = (lax.shift_right_logical(wide, slot) & 1).astype(jnp.float32)
    targets_copy.wait()
    for k in range(steps):
        arriving[k].wait()
        for part in range(points // width):
            first = k * points + part * width
            row = mask[first // width : first // width + 1, :].astype(jnp.bfloat16)
            masked = feats[:, first : first + width] * row
            for piece_index in range(width // LANES):
                dest = (first + piece_index * LANES) // (2 * LANES)
                half = piece_index % 2
                packed[dest, half * FEAT : (half + 1) * FEAT, :] = masked[
                    :, piece_index * LANES : (piece_index + 1) * LANES
                ]
        for dest in range(k * dests, (k + 1) * dests):
            packed[dest, 2 * FEAT : 2 * FEAT + 2, :] = targets_ref[2 * dest : 2 * dest + 2, :]
        leaving[k].start()
    for copy in leaving:
        copy.wait()


def pack(point_feats, point_targets, point_lists, devices):
    points = point_feats.shape[1]
    steps = 8
    rows = 2 * FEAT + 2
    return pl.pallas_call(
        pack_kernel,
        in_specs=[
            pl.BlockSpec(memory_space=pl.ANY),
            pl.BlockSpec(memory_space=pl.ANY),
            pl.BlockSpec(memory_space=pl.ANY),
        ],
        out_specs=pl.BlockSpec(memory_space=pl.ANY),
        out_shape=jax.ShapeDtypeStruct((devices, rows, LANES), jnp.bfloat16),
        scratch_shapes=[
            pltpu.VMEM(point_lists.shape[::-1], jnp.int32),
            pltpu.VMEM((FEAT, points), jnp.bfloat16),
            pltpu.VMEM((points // LANES, LANES), jnp.bfloat16),
            pltpu.VMEM((devices, rows, LANES), jnp.bfloat16),
            pltpu.SemaphoreType.DMA((steps,)),
            pltpu.SemaphoreType.DMA((steps,)),
            pltpu.SemaphoreType.DMA((2,)),
        ],
        name="pack",
    )(point_lists.T, point_feats, point_targets.reshape(points // LANES, LANES))


def spread_rows(square, lane_group):
    square = square + pltpu.roll(square, 64, 1)
    square = square + pltpu.roll(square, 32, 1)
    record = square[0:8, :]
    for q in range(1, 4):
        record = jnp.where(lane_group == q, square[8 * q : 8 * q + 8, :], record)
    return record


def three_parts(x):
    high = x.astype(jnp.bfloat16)
    rest = x - high.astype(jnp.float32)
    middle = rest.astype(jnp.bfloat16)
    return high, middle, (rest - middle.astype(jnp.float32)).astype(jnp.bfloat16)


def prepare_kernel(feats_ref, reg_ref, *records):

    lane_group = lax.broadcasted_iota(jnp.int32, (1, LANES), 1) // FEAT
    together = 4

    def some(step, carry):
        for k in range(together):
            b = step * together + k
            feats = feats_ref[b]
            reg = reg_ref[pl.ds(b, 1), :]
            once = feats * reg
            parts = three_parts(jnp.concatenate([feats, once, once * reg], axis=0))
            left = jnp.concatenate(parts, axis=0)
            right = [part[:FEAT, :] for part in parts]
            right = jnp.concatenate([*right, jnp.zeros_like(right[0])], axis=0)
            product = lax.dot_general(
                left, right, (((1,), (1,)), ((), ())), preferred_element_type=jnp.float32
            )
            size = 3 * FEAT
            total = jnp.where(lane_group < 1, product[2 * size :, :], 0.0)
            total = total + jnp.where(lane_group < 2, product[size : 2 * size, :], 0.0)
            total = total + product[:size, :]
            for power, record in enumerate(records):
                record[b] = spread_rows(total[power * FEAT : (power + 1) * FEAT, :], lane_group)
        return carry

    lax.fori_loop(0, feats_ref.shape[0] // together, some, 0)


def prepare(voxel_feats, voxel_reg):
    bricks = voxel_feats.shape[0]
    record = jax.ShapeDtypeStruct((bricks, 8, LANES), jnp.float32)
    return pl.pallas_call(
        prepare_kernel,
        out_shape=(record, record, record),
        compiler_params=pltpu.CompilerParams(vmem_limit_bytes=10 << 20),
        cost_estimate=pl.CostEstimate(flops=600_000_000, bytes_accessed=5_000_000, transcendentals=0),
        name="prepare",
    )(voxel_feats, voxel_reg)


def gather_early_kernel(
    first_ref, second_ref, mask_ref, low_ref, high_ref, below_ref, above_ref,
    first_lanes, second_lanes, mask_lanes, first_store, second_store, mask_store,
):
    for store in (first_store, second_store, mask_store):
        store[...] = jnp.zeros_like(store)

    def put(store):
        def write(a, e, value):
            if len(store.shape) == 3:
                store[lane_of(a, e)] = value
            else:
                store[lane_of(a, e) : lane_of(a, e) + 1, :] = value

        return write

    edges = (low_ref, high_ref, below_ref, above_ref)
    place_bricks(put(first_store), EARLY, 0, first_ref, *edges)
    place_bricks(put(second_store), EARLY, 1, second_ref, *edges)
    place_bricks(put(mask_store), EARLY, 2, mask_ref, *edges)
    to_lanes(first_store, first_lanes)
    to_lanes(second_store, second_lanes)
    mask_lanes[...] = mask_store[...].T[:8, :]


def gather_early(first, second, mask, edges):
    lanes = jax.ShapeDtypeStruct((8 * LANES, SPAN), jnp.float32)
    return pl.pallas_call(
        gather_early_kernel,
        out_shape=(lanes, lanes, jax.ShapeDtypeStruct((8, SPAN), jnp.float32)),
        scratch_shapes=[
            pltpu.VMEM((SPAN, 8, LANES), jnp.float32),
            pltpu.VMEM((SPAN, 8, LANES), jnp.float32),
            pltpu.VMEM((SPAN, LANES), jnp.float32),
        ],
        compiler_params=pltpu.CompilerParams(vmem_limit_bytes=10 << 20),
        cost_estimate=pl.CostEstimate(flops=2_000_000, bytes_accessed=3_000_000, transcendentals=0),
        name="gather_early",
    )(first, second, mask, *edges)


def across_early_kernel(first_ref, second_ref, mask_ref, to_low, to_high):
    fill_across(EARLY, (first_ref, second_ref, mask_ref), None, None, to_low, to_high)


def across_early(owns):
    out = jax.ShapeDtypeStruct((message_rows(EARLY, across_rows), LANES), jnp.float32)
    return pl.pallas_call(
        across_early_kernel,
        out_shape=(out, out),
        compiler_params=pltpu.CompilerParams(vmem_limit_bytes=4 << 20),
        name="across_early",
    )(*owns)


def across_late_kernel(moments_ref, vectors_ref, low, high, early_low, early_high, to_low, to_high):
    fill_across(LATE, (moments_ref, vectors_ref), low, high, to_low, to_high)
    start = message_rows(LATE, across_rows)
    masks = message_rows(EARLY[:2], along_rows)
    for out, e in ((to_low, 0), (to_high, BY - 1)):
        rows = []
        for k, (source, index) in enumerate(((early_low, BY + e), (early_high, e))):
            out[start + 8 * k : start + 8 * k + 8, :] = source[8 * index : 8 * index + 8, :]
            rows.append(source[masks + index : masks + index + 1, :])
        rows.append(jnp.zeros((6, LANES), jnp.float32))
        out[start + 16 : start + CORNER_ROWS, :] = jnp.concatenate(rows, axis=0)


def across_late(moments, vectors, low, high, early_low, early_high):
    out = jax.ShapeDtypeStruct((message_rows(LATE, across_rows) + CORNER_ROWS, LANES), jnp.float32)
    return pl.pallas_call(
        across_late_kernel,
        out_shape=(out, out),
        compiler_params=pltpu.CompilerParams(vmem_limit_bytes=4 << 20),
        name="across_late",
    )(moments, vectors, low, high, early_low, early_high)


def along_messages(sections, owns):
    to_low, to_high = [], []
    for (rows, depth, _), own in zip(sections, owns):
        flat = own.reshape(-1, LANES)
        used = rows * depth * BY
        blank = ((0, padded(used) - used), (0, 0))
        to_low.append(jnp.pad(flat[:used], blank))
        to_high.append(jnp.pad(flat[flat.shape[0] - used :], blank))
    return jnp.concatenate(to_low), jnp.concatenate(to_high)


def swap(to_low, to_high, axis, even):
    count = lax.axis_size(axis)

    def pairs(start):
        return [pair for a in range(start, count - 1, 2) for pair in ((a, a + 1), (a + 1, a))]

    first = lax.ppermute(jnp.where(even, to_high, to_low), axis, pairs(0))
    second = lax.ppermute(jnp.where(even, to_low, to_high), axis, pairs(1))
    return jnp.where(even, second, first), jnp.where(even, first, second)


def moments_kernel(
    got_ref, first_ref, second_ref, third_ref, moments_ref, vectors_ref, low_ref, high_ref, turned, lanes_ref
):
    for t in range(8):
        block = [record[:, t, :] for record in (first_ref, second_ref, third_ref)]
        block = jnp.concatenate([*block, jnp.zeros((BX * BY, LANES), jnp.float32)], axis=0)
        lanes_ref[t * LANES : (t + 1) * LANES, :] = block.T
    sources = got_ref.shape[0]
    for group in range(sources // 4):
        for half in range(2):
            block = got_ref[4 * group : 4 * group + 4, half * FEAT : (half + 1) * FEAT, :]
            turned[half, group] = block.astype(jnp.float32).reshape(LANES, LANES).T
    sums = []
    for half in range(2):
        total = jnp.zeros((FEAT, LANES), jnp.float32)
        for source in range(sources):
            feats = got_ref[source, half * FEAT : (half + 1) * FEAT, :].astype(jnp.float32)
            target = got_ref[source, 2 * FEAT : 2 * FEAT + 2, :].astype(jnp.float32)
            total = total + feats * target[half : half + 1, :]
        sums.append(total)

    groups = turned.shape[1]
    lane_group = lax.broadcasted_iota(jnp.int32, (1, LANES), 1) // FEAT
    for half in range(2):
        for pair in range(8):
            for k in range(2):
                b = 2 * pair + k
                points = turned[half, :, 8 * b : 8 * b + 8, :].reshape(groups * 8, LANES)
                square = lax.dot_general(
                    points.T.astype(jnp.bfloat16),
                    points.astype(jnp.bfloat16),
                    (((1,), (0,)), ((), ())),
                    preferred_element_type=jnp.float32,
                )
                own = jnp.zeros((FEAT, LANES), jnp.float32)
                for q in range(4):
                    own = own + jnp.where(lane_group == q, square[q * FEAT : (q + 1) * FEAT, :], 0.0)
                moments_ref[half * 16 + b] = spread_rows(own, lane_group)
    point = lax.broadcasted_iota(jnp.int32, (LANES, LANES), 0) // SLOTS
    lane = lax.broadcasted_iota(jnp.int32, (LANES, LANES), 1)
    values = jnp.zeros((FEAT, LANES), jnp.float32)
    for half in range(2):
        spread = (lane % (BX * BY) == point + half * 16).astype(jnp.float32)
        values = values + jnp.dot(
            sums[half], spread, precision=HIGHEST, preferred_element_type=jnp.float32
        )
    values = times(lanes_ref, values) + jnp.where(lane_group == 3, values, 0.0)
    values = jnp.concatenate([values, jnp.zeros((LANES - FEAT, LANES), jnp.float32)], axis=0).T
    bricks = BX * BY
    vectors = jnp.concatenate([values[k * bricks : (k + 1) * bricks, :FEAT] for k in range(4)], axis=1)
    vectors_ref[...] = vectors
    depth = LATE[0][1] * BY
    for k in range(depth):
        low_ref[8 * k : 8 * k + 8, :] = moments_ref[k]
        high_ref[8 * k : 8 * k + 8, :] = moments_ref[BX * BY - depth + k]
    deep = LATE[1][1] * BY
    blank = jnp.zeros((padded(deep) - deep, LANES), jnp.float32)
    low_ref[8 * depth :, :] = jnp.concatenate([vectors[:deep], blank], axis=0)
    high_ref[8 * depth :, :] = jnp.concatenate([vectors[BX * BY - deep : BX * BY], blank], axis=0)


def find_moments(got, records):
    devices = got.shape[0]
    bricks = BX * BY
    message = jax.ShapeDtypeStruct((message_rows(LATE, along_rows), LANES), jnp.float32)
    return pl.pallas_call(
        moments_kernel,
        out_shape=(
            jax.ShapeDtypeStruct((bricks, 8, LANES), jnp.float32),
            jax.ShapeDtypeStruct((bricks, LANES), jnp.float32),
            message,
            message,
        ),
        scratch_shapes=[
            pltpu.VMEM((2, devices // 4, LANES, LANES), jnp.float32),
            pltpu.VMEM((8 * LANES, LANES), jnp.float32),
        ],
        compiler_params=pltpu.CompilerParams(vmem_limit_bytes=12 << 20),
        cost_estimate=pl.CostEstimate(flops=1_000_000_000, bytes_accessed=12_000_000, transcendentals=0),
        name="moments",
    )(got, *records)


def power_of_two(value):
    scale = jnp.ones_like(value)
    inverse = jnp.ones_like(value)
    for k in (64, 32, 16, 8, 4, 2, 1):
        up, down = 2.0**k, 2.0**-k
        large = value * down >= 1.0
        small = value * up <= 1.0
        value = jnp.where(large, value * down, jnp.where(small, value * up, value))
        scale = jnp.where(large, scale * up, jnp.where(small, scale * down, scale))
        inverse = jnp.where(large, inverse * down, jnp.where(small, inverse * up, inverse))
    return scale, inverse


def krylov_kernel(
    moments_ref, vectors_ref, low_ref, high_ref, below_ref, above_ref, first_ref, second_ref, mask_ref,
    feats_ref, reg_ref, basis_ref, message_ref, moment_store, vector_store, moment_lanes,
    corner_store, corner_masks, corner_lanes,
):
    moment_store[...] = jnp.zeros_like(moment_store)
    corner_store[...] = jnp.zeros_like(corner_store)
    corner_masks[...] = jnp.zeros_like(corner_masks)
    vector_store[...] = jnp.zeros_like(vector_store)

    def put_moment(a, e, value):
        moment_store[lane_of(a, e)] = value

    def put_vector(a, e, value):
        vector_store[lane_of(a, e) : lane_of(a, e) + 1, :] = value

    edges = (low_ref, high_ref, below_ref, above_ref)
    place_bricks(put_moment, LATE, 0, moments_ref, *edges)
    place_bricks(put_vector, LATE, 1, vectors_ref, *edges)
    start = message_rows(LATE, across_rows)
    for ref, e in ((below_ref, -1), (above_ref, BY)):
        for k, a in enumerate((-1, BX)):
            place = lane_of(a, e) % LANES
            corner_store[place] = ref[start + 8 * k : start + 8 * k + 8, :]
            corner_masks[place : place + 1, :] = ref[start + 16 + k : start + 17 + k, :]
    to_lanes(moment_store, moment_lanes)
    to_lanes(corner_store, corner_lanes)
    vectors = vector_store[...].T
    lane = lax.broadcasted_iota(jnp.int32, (1, LANES), 1)
    front = (lane == lane_of(-1, -1)) | (lane == lane_of(-1, BY))
    rear = (lane == lane_of(BX, -1) % LANES) | (lane == lane_of(BX, BY) % LANES)

    def both_tiles(x):
        return jnp.concatenate([jnp.where(front, x, 0.0), jnp.where(rear, x, 0.0)], axis=1)

    masks = mask_ref[...] + both_tiles(corner_masks[...].T[:8, :])

    def system(z):
        near = masks[0:1] * pltpu.roll(z, PITCH, 1) + masks[1:2] * pltpu.roll(z, SPAN - PITCH, 1)
        near = near + masks[2:3] * pltpu.roll(z, 1, 1) + masks[3:4] * pltpu.roll(z, SPAN - 1, 1)
        return times(moment_lanes, z) + coupling_weight * (masks[4:5] * z - near)

    one = system(vectors[0:FEAT])
    corners = times(corner_lanes, jnp.where(front, one[:, :LANES], one[:, LANES:]))
    two = system(times(first_ref, one) + both_tiles(corners) + vectors[FEAT : 2 * FEAT])
    three = system(times(first_ref, two) + times(second_ref, one) + vectors[2 * FEAT : 3 * FEAT])
    chain = (vectors[3 * FEAT :], one, two, three)
    for b in range(BX * BY):
        place = lane_of(b // BY, b % BY)
        feats = feats_ref[b]
        for step, values in enumerate(chain):
            basis_ref[step, b : b + 1, :] = jnp.sum(feats * values[:, place : place + 1], axis=0, keepdims=True)
    reg = reg_ref[...]
    basis = [basis_ref[0]]
    for step in range(1, 4):
        basis.append(basis_ref[step] + reg * basis[-1])
        basis_ref[step] = basis[-1]

    def folded(x, combine):
        rows = [x[8 * k : 8 * k + 8, :] for k in range(x.shape[0] // 8)]
        parts = [r[:, LANES * k : LANES * (k + 1)] for r in rows for k in range(x.shape[1] // LANES)]
        while len(parts) > 1:
            parts = [combine(parts[k], parts[k + 1]) for k in range(0, len(parts), 2)]
        return parts[0]

    peaks = [jnp.max(folded(jnp.abs(v), jnp.maximum), axis=0, keepdims=True) for v in basis]
    peaks = jnp.max(jnp.concatenate(peaks + peaks, axis=0), axis=1, keepdims=True)
    scale, inverse = power_of_two(jnp.broadcast_to(peaks, (8, LANES)))
    scaled = [v * inverse[k : k + 1, 0:1] for k, v in enumerate(basis)]
    sums = [jnp.sum(folded(scaled[a] * scaled[b], jnp.add), axis=0, keepdims=True) for a, b in PAIRS]
    sums = jnp.concatenate(sums + [jnp.zeros((16 - len(PAIRS), LANES), jnp.float32)], axis=0)
    sums = jnp.sum(sums, axis=1, keepdims=True)
    row = jnp.zeros((1, LANES), jnp.float32)
    for k in range(len(PAIRS)):
        row = jnp.where(lane == k, sums[k : k + 1, :], row)
    for k in range(4):
        row = jnp.where(lane == 10 + k, scale[k : k + 1, :], row)
        row = jnp.where(lane == 14 + k, inverse[k : k + 1, :], row)
    message_ref[...] = jnp.broadcast_to(row, message_ref.shape)


def krylov(moments, vectors, edges, first, second, masks, voxel_feats, voxel_reg, devices):
    bricks, _, voxels = voxel_feats.shape
    return pl.pallas_call(
        krylov_kernel,
        out_shape=(
            jax.ShapeDtypeStruct((4, bricks, voxels), jnp.float32),
            jax.ShapeDtypeStruct((devices, LANES), jnp.float32),
        ),
        scratch_shapes=[
            pltpu.VMEM((SPAN, 8, LANES), jnp.float32),
            pltpu.VMEM((SPAN, LANES), jnp.float32),
            pltpu.VMEM((8 * LANES, SPAN), jnp.float32),
            pltpu.VMEM((LANES, 8, LANES), jnp.float32),
            pltpu.VMEM((LANES, LANES), jnp.float32),
            pltpu.VMEM((8 * LANES, LANES), jnp.float32),
        ],
        compiler_params=pltpu.CompilerParams(vmem_limit_bytes=12 << 20),
        name="krylov",
    )(moments, vectors, *edges, first, second, masks, voxel_feats, voxel_reg)


def finish_kernel(shared_ref, basis_ref, solution_ref, residual_ref):
    shared = shared_ref[...]
    lane = lax.broadcasted_iota(jnp.int32, (1, LANES), 1)

    def pick(row, k):
        return jnp.sum(jnp.where(lane == k, row, 0.0), axis=1, keepdims=True)

    largest = jnp.max(shared, axis=0, keepdims=True)
    smallest = jnp.min(shared, axis=0, keepdims=True)
    scale = [pick(largest, 10 + k) for k in range(4)]
    inverse = [pick(smallest, 14 + k) for k in range(4)]
    weight = [shared[:, 10 + k : 11 + k] * inverse[k] for k in range(4)]
    left = jnp.zeros_like(shared)
    right = jnp.zeros_like(shared)
    for k, (a, b) in enumerate(PAIRS):
        left = jnp.where(lane == k, weight[a], left)
        right = jnp.where(lane == k, weight[b], right)
    total = jnp.sum(shared * left * right, axis=0, keepdims=True)
    gram = [[None] * 4 for _ in range(4)]
    for k, (a, b) in enumerate(PAIRS):
        gram[a][b] = gram[b][a] = pick(total, k)
    growth = [scale[k + 1] * inverse[k] for k in range(3)]

    def product(left, right):
        terms = [
            left[a] * right[b] * gram[a][b]
            for a in range(4)
            for b in range(4)
            if left[a] is not None and right[b] is not None
        ]
        return functools.reduce(jnp.add, terms)

    def plus(left, factor, right):
        out = []
        for a, b in zip(left, right):
            out.append(a if b is None else factor * b if a is None else a + factor * b)
        return out

    def image(vector):
        return [None] + [None if vector[k] is None else vector[k] * growth[k] for k in range(3)]

    solution = [None] * 4
    residual = [jnp.ones((1, 1), jnp.float32), None, None, None]
    direction = list(residual)
    norm_now = product(residual, residual)
    for iteration in range(ITERS):
        carried = image(direction)
        alpha = norm_now / product(direction, carried)
        solution = plus(solution, alpha, direction)
        residual = plus(residual, -alpha, carried)
        if iteration + 1 < ITERS:
            norm_next = product(residual, residual)
            direction = plus(residual, norm_next / norm_now, direction)
            norm_now = norm_next
    back = [scale[0] * inverse[k] for k in range(4)]
    for out_ref, coefficients in ((solution_ref, solution), (residual_ref, residual)):
        total = None
        for k, c in enumerate(coefficients):
            if c is not None:
                term = (c * back[k]) * basis_ref[k]
                total = term if total is None else total + term
        out_ref[...] = total


def finish(shared, basis):
    _, bricks, voxels = basis.shape
    out = jax.ShapeDtypeStruct((bricks, voxels), jnp.float32)
    return pl.pallas_call(
        finish_kernel,
        out_shape=(out, out),
        compiler_params=pltpu.CompilerParams(vmem_limit_bytes=4 << 20),
        name="finish",
    )(shared, basis)


def shards(point_feats, point_targets, point_lists, brick_adjacency, voxel_feats, voxel_reg):
    feat_count = point_feats.shape[0]
    brick_total, slots = point_lists.shape
    local_bricks = voxel_feats.shape[0]
    devices = brick_total // local_bricks
    sending = pack(point_feats, point_targets, point_lists, devices)
    got = lax.all_to_all(sending, GX_GY, split_axis=0, concat_axis=0, tiled=True)

    first, second, third = prepare(voxel_feats, voxel_reg)
    mask = (brick_adjacency >= 0).astype(jnp.float32)
    mask = jnp.concatenate([mask, jnp.sum(mask, axis=1, keepdims=True)], axis=1)
    mask = jnp.pad(mask, ((0, 0), (0, LANES - 5)))
    early = (first, second, mask)
    along_even = lax.axis_index("gx_2") == 0
    across_even = lax.axis_index("gy") % 2 == 0
    early_low, early_high = swap(*along_messages(EARLY, early), GX, along_even)
    early_below, early_above = swap(*across_early(early), "gy", across_even)

    moments, vectors, to_low, to_high = find_moments(got, (first, second, third))
    low, high = swap(to_low, to_high, GX, along_even)
    first_lanes, second_lanes, mask_lanes = gather_early(
        first, second, mask, (early_low, early_high, early_below, early_above)
    )
    below, above = swap(
        *across_late(moments, vectors, low, high, early_low, early_high), "gy", across_even
    )
    basis, message = krylov(
        moments, vectors, (low, high, below, above), first_lanes, second_lanes, mask_lanes,
        voxel_feats, voxel_reg, devices,
    )
    shared = lax.all_to_all(message, GX_GY, split_axis=0, concat_axis=0, tiled=True)
    return finish(shared, basis)


def solution(mesh):
    torus = Mesh(mesh.devices.reshape(4, 4, 2, mesh.shape["gy"]), ("gx_0", "gx_1", "gx_2", "gy"))
    return jax.shard_map(
        shards,
        mesh=torus,
        in_specs=(
            P(None, GX_GY),
            P(GX_GY),
            P(GX_GY, None),
            P(GX_GY, None),
            P(GX_GY, None, None),
            P(GX_GY, None),
        ),
        out_specs=(P(GX_GY, None), P(GX_GY, None)),
        check_vma=False,
    )
```

```python
import functools

import jax
import jax.numpy as jnp
from jax import lax
from jax.experimental import pallas as pl
from jax.experimental.pallas import tpu as pltpu
from jax.sharding import Mesh
from jax.sharding import PartitionSpec as P

BX = 8
BY = 4
ITERS = 3
SLOTS = 8
LANES = 128
FEAT = 32
PITCH = 16
SPAN = 256
REACH = 3
GX_GY = ("gx_0", "gx_1", "gx_2", "gy")
GX = ("gx_0", "gx_1", "gx_2")
HIGHEST = lax.Precision.HIGHEST
PAIRS = tuple((a, b) for a in range(4) for b in range(a, 4))


coupling_weight = 1.0

EARLY = ((8, 2, False), (8, 1, False), (1, 2, False))
LATE = ((8, 1, True), (1, 3, True))
CORNER_ROWS = 24


def padded(rows):
    return (rows + 7) // 8 * 8


def along_rows(section):
    return padded(section[0] * section[1] * BY)


def beyond(section, away):
    return section[1] - away if section[2] else 0


def across_rows(section):
    rows, depth, _ = section
    return padded(rows * sum(BX + 2 * beyond(section, k) for k in range(1, depth + 1)))


def message_rows(sections, size):
    return sum(size(section) for section in sections)


def piece(ref, start, rows, index):
    if rows == 8 and len(ref.shape) == 3:
        return ref[index]
    return ref[start + rows * index : start + rows * (index + 1), :]


def brick_at(own, low, high, start, section, a, e):
    rows, depth, _ = section
    if a < 0:
        return piece(low, start, rows, (a + depth) * BY + e)
    if a >= BX:
        return piece(high, start, rows, (a - BX) * BY + e)
    return piece(own, 0, rows, a * BY + e)


def fill_across(sections, owns, low, high, to_low, to_high):
    source = target = 0
    for section, own in zip(sections, owns):
        rows, depth, _ = section
        index = 0
        for away in range(1, depth + 1):
            extra = beyond(section, away)
            for a in range(-extra, BX + extra):
                place = slice(target + rows * index, target + rows * (index + 1))
                to_low[place, :] = brick_at(own, low, high, source, section, a, away - 1)
                to_high[place, :] = brick_at(own, low, high, source, section, a, BY - away)
                index += 1
        used, whole = rows * index, across_rows(section)
        if used < whole:
            blank = jnp.zeros((whole - used, LANES), jnp.float32)
            to_low[target + used : target + whole, :] = blank
            to_high[target + used : target + whole, :] = blank
        source += along_rows(section)
        target += whole


def place_bricks(put, sections, which, own, along_low, along_high, across_low, across_high):
    section = sections[which]
    rows, depth, _ = section
    start = message_rows(sections[:which], along_rows)
    for a in range(-depth, BX + depth):
        for e in range(BY):
            put(a, e, brick_at(own, along_low, along_high, start, section, a, e))
    start = message_rows(sections[:which], across_rows)
    index = 0
    for away in range(1, depth + 1):
        extra = beyond(section, away)
        for a in range(-extra, BX + extra):
            put(a, -away, piece(across_low, start, rows, index))
            put(a, BY - 1 + away, piece(across_high, start, rows, index))
            index += 1


def lane_of(a, e):
    return (a + REACH) * PITCH + e + REACH


def to_lanes(records, lanes_ref):
    for t in range(8):
        lanes_ref[t * LANES : (t + 1) * LANES, :] = records[:, t, :].T


def times(matrix_ref, vector):
    total = None
    for t in range(8):
        for q in range(4):
            i = 8 * q + t
            row = t * LANES + q * FEAT
            term = matrix_ref[row : row + FEAT, :] * vector[i : i + 1, :]
            total = term if total is None else total + term
    return total


def pack_kernel(
    lists_hbm, feats_ref, targets_hbm, out_ref, lists_ref, feats, targets_ref, packed, arrived, left, small
):
    steps = arrived.shape[0]
    lists_copy = pltpu.make_async_copy(lists_hbm, lists_ref, small.at[0])
    targets_copy = pltpu.make_async_copy(targets_hbm, targets_ref, small.at[1])
    lists_copy.start()
    targets_copy.start()
    devices = out_ref.shape[0]
    bricks = lists_ref.shape[1]
    dests = devices // steps
    width = LANES * SLOTS
    points = bricks * SLOTS // steps
    arriving = [
        pltpu.make_async_copy(
            feats_ref.at[:, k * points : (k + 1) * points], feats.at[:, k * points : (k + 1) * points], arrived.at[k]
        )
        for k in range(steps)
    ]
    leaving = [
        pltpu.make_async_copy(
            packed.at[k * dests : (k + 1) * dests], out_ref.at[k * dests : (k + 1) * dests], left.at[k]
        )
        for k in range(steps)
    ]
    for copy in arriving:
        copy.start()
    lists_copy.wait()
    rows = bricks // LANES
    lane = lax.broadcasted_iota(jnp.int32, (SLOTS, LANES), 1)
    codes = []
    for block in range(rows):
        chosen = lists_ref[:, block * LANES : (block + 1) * LANES]
        offset = chosen - (lane + block * LANES) * SLOTS
        bits = jnp.where(chosen >= 0, lax.shift_left(1, jnp.clip(offset, 0, SLOTS - 1)), 0)
        codes.append(jnp.sum(bits, axis=0, keepdims=True))
    code = jnp.concatenate(codes, axis=0).astype(jnp.float32).astype(jnp.bfloat16)
    brick = lax.broadcasted_iota(jnp.int32, (LANES, width), 0)
    point = lax.broadcasted_iota(jnp.int32, (LANES, width), 1)
    spread = (lax.shift_right_logical(point, 3) == brick).astype(jnp.float32).astype(jnp.bfloat16)
    wide = jnp.dot(code, spread, preferred_element_type=jnp.float32).astype(jnp.int32)
    slot = lax.broadcasted_iota(jnp.int32, (rows, width), 1) & (SLOTS - 1)
    mask = (lax.shift_right_logical(wide, slot) & 1).astype(jnp.float32)
    targets_copy.wait()
    for k in range(steps):
        arriving[k].wait()
        for part in range(points // width):
            first = k * points + part * width
            row = mask[first // width : first // width + 1, :].astype(jnp.bfloat16)
            masked = feats[:, first : first + width] * row
            for piece_index in range(width // LANES):
                dest = (first + piece_index * LANES) // (2 * LANES)
                half = piece_index % 2
                packed[dest, half * FEAT : (half + 1) * FEAT, :] = masked[
                    :, piece_index * LANES : (piece_index + 1) * LANES
                ]
        for dest in range(k * dests, (k + 1) * dests):
            packed[dest, 2 * FEAT : 2 * FEAT + 2, :] = targets_ref[2 * dest : 2 * dest + 2, :]
        leaving[k].start()
    for copy in leaving:
        copy.wait()


def pack(point_feats, point_targets, point_lists, devices):
    points = point_feats.shape[1]
    steps = 8
    rows = 2 * FEAT + 2
    return pl.pallas_call(
        pack_kernel,
        in_specs=[
            pl.BlockSpec(memory_space=pl.ANY),
            pl.BlockSpec(memory_space=pl.ANY),
            pl.BlockSpec(memory_space=pl.ANY),
        ],
        out_specs=pl.BlockSpec(memory_space=pl.ANY),
        out_shape=jax.ShapeDtypeStruct((devices, rows, LANES), jnp.bfloat16),
        scratch_shapes=[
            pltpu.VMEM(point_lists.shape[::-1], jnp.int32),
            pltpu.VMEM((FEAT, points), jnp.bfloat16),
            pltpu.VMEM((points // LANES, LANES), jnp.bfloat16),
            pltpu.VMEM((devices, rows, LANES), jnp.bfloat16),
            pltpu.SemaphoreType.DMA((steps,)),
            pltpu.SemaphoreType.DMA((steps,)),
            pltpu.SemaphoreType.DMA((2,)),
        ],
        name="pack",
    )(point_lists.T, point_feats, point_targets.reshape(points // LANES, LANES))


def spread_rows(square, lane_group):
    square = square + pltpu.roll(square, 64, 1)
    square = square + pltpu.roll(square, 32, 1)
    record = square[0:8, :]
    for q in range(1, 4):
        record = jnp.where(lane_group == q, square[8 * q : 8 * q + 8, :], record)
    return record


def three_parts(x):
    high = x.astype(jnp.bfloat16)
    rest = x - high.astype(jnp.float32)
    middle = rest.astype(jnp.bfloat16)
    return high, middle, (rest - middle.astype(jnp.float32)).astype(jnp.bfloat16)


def prepare_kernel(feats_ref, reg_ref, *records):

    lane_group = lax.broadcasted_iota(jnp.int32, (1, LANES), 1) // FEAT
    together = 4

    def some(step, carry):
        for k in range(together):
            b = step * together + k
            feats = feats_ref[b]
            reg = reg_ref[pl.ds(b, 1), :]
            once = feats * reg
            parts = three_parts(jnp.concatenate([feats, once, once * reg], axis=0))
            left = jnp.concatenate(parts, axis=0)
            right = [part[:FEAT, :] for part in parts]
            right = jnp.concatenate([*right, jnp.zeros_like(right[0])], axis=0)
            product = lax.dot_general(
                left, right, (((1,), (1,)), ((), ())), preferred_element_type=jnp.float32
            )
            size = 3 * FEAT
            total = jnp.where(lane_group < 1, product[2 * size :, :], 0.0)
            total = total + jnp.where(lane_group < 2, product[size : 2 * size, :], 0.0)
            total = total + product[:size, :]
            for power, record in enumerate(records):
                record[b] = spread_rows(total[power * FEAT : (power + 1) * FEAT, :], lane_group)
        return carry

    lax.fori_loop(0, feats_ref.shape[0] // together, some, 0)


def prepare(voxel_feats, voxel_reg):
    bricks = voxel_feats.shape[0]
    record = jax.ShapeDtypeStruct((bricks, 8, LANES), jnp.float32)
    return pl.pallas_call(
        prepare_kernel,
        out_shape=(record, record, record),
        compiler_params=pltpu.CompilerParams(vmem_limit_bytes=10 << 20),
        cost_estimate=pl.CostEstimate(flops=600_000_000, bytes_accessed=5_000_000, transcendentals=0),
        name="prepare",
    )(voxel_feats, voxel_reg)


def gather_early_kernel(
    first_ref, second_ref, mask_ref, low_ref, high_ref, below_ref, above_ref,
    first_lanes, second_lanes, mask_lanes, first_store, second_store, mask_store,
):
    for store in (first_store, second_store, mask_store):
        store[...] = jnp.zeros_like(store)

    def put(store):
        def write(a, e, value):
            if len(store.shape) == 3:
                store[lane_of(a, e)] = value
            else:
                store[lane_of(a, e) : lane_of(a, e) + 1, :] = value

        return write

    edges = (low_ref, high_ref, below_ref, above_ref)
    place_bricks(put(first_store), EARLY, 0, first_ref, *edges)
    place_bricks(put(second_store), EARLY, 1, second_ref, *edges)
    place_bricks(put(mask_store), EARLY, 2, mask_ref, *edges)
    to_lanes(first_store, first_lanes)
    to_lanes(second_store, second_lanes)
    mask_lanes[...] = mask_store[...].T[:8, :]


def gather_early(first, second, mask, edges):
    lanes = jax.ShapeDtypeStruct((8 * LANES, SPAN), jnp.float32)
    return pl.pallas_call(
        gather_early_kernel,
        out_shape=(lanes, lanes, jax.ShapeDtypeStruct((8, SPAN), jnp.float32)),
        scratch_shapes=[
            pltpu.VMEM((SPAN, 8, LANES), jnp.float32),
            pltpu.VMEM((SPAN, 8, LANES), jnp.float32),
            pltpu.VMEM((SPAN, LANES), jnp.float32),
        ],
        compiler_params=pltpu.CompilerParams(vmem_limit_bytes=10 << 20),
        cost_estimate=pl.CostEstimate(flops=2_000_000, bytes_accessed=3_000_000, transcendentals=0),
        name="gather_early",
    )(first, second, mask, *edges)


def across_early_kernel(first_ref, second_ref, mask_ref, to_low, to_high):
    fill_across(EARLY, (first_ref, second_ref, mask_ref), None, None, to_low, to_high)


def across_early(owns):
    out = jax.ShapeDtypeStruct((message_rows(EARLY, across_rows), LANES), jnp.float32)
    return pl.pallas_call(
        across_early_kernel,
        out_shape=(out, out),
        compiler_params=pltpu.CompilerParams(vmem_limit_bytes=4 << 20),
        name="across_early",
    )(*owns)


def across_late_kernel(moments_ref, vectors_ref, low, high, early_low, early_high, to_low, to_high):
    fill_across(LATE, (moments_ref, vectors_ref), low, high, to_low, to_high)
    start = message_rows(LATE, across_rows)
    masks = message_rows(EARLY[:2], along_rows)
    for out, e in ((to_low, 0), (to_high, BY - 1)):
        rows = []
        for k, (source, index) in enumerate(((early_low, BY + e), (early_high, e))):
            out[start + 8 * k : start + 8 * k + 8, :] = source[8 * index : 8 * index + 8, :]
            rows.append(source[masks + index : masks + index + 1, :])
        rows.append(jnp.zeros((6, LANES), jnp.float32))
        out[start + 16 : start + CORNER_ROWS, :] = jnp.concatenate(rows, axis=0)


def across_late(moments, vectors, low, high, early_low, early_high):
    out = jax.ShapeDtypeStruct((message_rows(LATE, across_rows) + CORNER_ROWS, LANES), jnp.float32)
    return pl.pallas_call(
        across_late_kernel,
        out_shape=(out, out),
        compiler_params=pltpu.CompilerParams(vmem_limit_bytes=4 << 20),
        name="across_late",
    )(moments, vectors, low, high, early_low, early_high)


def along_messages(sections, owns):
    to_low, to_high = [], []
    for (rows, depth, _), own in zip(sections, owns):
        flat = own.reshape(-1, LANES)
        used = rows * depth * BY
        blank = ((0, padded(used) - used), (0, 0))
        to_low.append(jnp.pad(flat[:used], blank))
        to_high.append(jnp.pad(flat[flat.shape[0] - used :], blank))
    return jnp.concatenate(to_low), jnp.concatenate(to_high)


def swap(to_low, to_high, axis, even):
    count = lax.axis_size(axis)

    def pairs(start):
        return [pair for a in range(start, count - 1, 2) for pair in ((a, a + 1), (a + 1, a))]

    second = lax.ppermute(jnp.where(even, to_low, to_high), axis, pairs(1))
    first = lax.ppermute(jnp.where(even, to_high, to_low), axis, pairs(0))
    return jnp.where(even, second, first), jnp.where(even, first, second)


def moments_kernel(
    got_ref, first_ref, second_ref, third_ref, moments_ref, vectors_ref, gathered_ref, low_ref, high_ref,
    turned, lanes_ref, moment_lanes,
):
    for t in range(8):
        block = [record[:, t, :] for record in (first_ref, second_ref, third_ref)]
        block = jnp.concatenate([*block, jnp.zeros((BX * BY, LANES), jnp.float32)], axis=0)
        lanes_ref[t * LANES : (t + 1) * LANES, :] = block.T
    sources = got_ref.shape[0]
    for group in range(sources // 4):
        for half in range(2):
            block = got_ref[4 * group : 4 * group + 4, half * FEAT : (half + 1) * FEAT, :]
            turned[half, group] = block.astype(jnp.float32).reshape(LANES, LANES).T
    sums = []
    for half in range(2):
        total = jnp.zeros((FEAT, LANES), jnp.float32)
        for source in range(sources):
            feats = got_ref[source, half * FEAT : (half + 1) * FEAT, :].astype(jnp.float32)
            target = got_ref[source, 2 * FEAT : 2 * FEAT + 2, :].astype(jnp.float32)
            total = total + feats * target[half : half + 1, :]
        sums.append(total)

    groups = turned.shape[1]
    lane_group = lax.broadcasted_iota(jnp.int32, (1, LANES), 1) // FEAT
    for half in range(2):
        for pair in range(8):
            for k in range(2):
                b = 2 * pair + k
                points = turned[half, :, 8 * b : 8 * b + 8, :].reshape(groups * 8, LANES)
                square = lax.dot_general(
                    points.T.astype(jnp.bfloat16),
                    points.astype(jnp.bfloat16),
                    (((1,), (0,)), ((), ())),
                    preferred_element_type=jnp.float32,
                )
                own = jnp.zeros((FEAT, LANES), jnp.float32)
                for q in range(4):
                    own = own + jnp.where(lane_group == q, square[q * FEAT : (q + 1) * FEAT, :], 0.0)
                moments_ref[half * 16 + b] = spread_rows(own, lane_group)
    point = lax.broadcasted_iota(jnp.int32, (LANES, LANES), 0) // SLOTS
    lane = lax.broadcasted_iota(jnp.int32, (LANES, LANES), 1)
    values = jnp.zeros((FEAT, LANES), jnp.float32)
    for half in range(2):
        spread = (lane % (BX * BY) == point + half * 16).astype(jnp.float32)
        values = values + jnp.dot(
            sums[half], spread, precision=HIGHEST, preferred_element_type=jnp.float32
        )
    gathered_ref[...] = values
    values = times(lanes_ref, values)
    for t in range(8):
        block = [moments_ref[:, t, :], jnp.zeros((LANES - BX * BY, LANES), jnp.float32)]
        moment_lanes[t * LANES : (t + 1) * LANES, :] = jnp.concatenate(block, axis=0).T
    values = jnp.where(lane_group == 3, pltpu.roll(times(moment_lanes, values), 96, 1), values)
    values = jnp.concatenate([values, jnp.zeros((LANES - FEAT, LANES), jnp.float32)], axis=0).T
    bricks = BX * BY
    vectors = jnp.concatenate([values[k * bricks : (k + 1) * bricks, :FEAT] for k in range(4)], axis=1)
    vectors_ref[...] = vectors
    depth = LATE[0][1] * BY
    for k in range(depth):
        low_ref[8 * k : 8 * k + 8, :] = moments_ref[k]
        high_ref[8 * k : 8 * k + 8, :] = moments_ref[BX * BY - depth + k]
    deep = LATE[1][1] * BY
    blank = jnp.zeros((padded(deep) - deep, LANES), jnp.float32)
    low_ref[8 * depth :, :] = jnp.concatenate([vectors[:deep], blank], axis=0)
    high_ref[8 * depth :, :] = jnp.concatenate([vectors[BX * BY - deep : BX * BY], blank], axis=0)


def find_moments(got, records):
    devices = got.shape[0]
    bricks = BX * BY
    message = jax.ShapeDtypeStruct((message_rows(LATE, along_rows), LANES), jnp.float32)
    return pl.pallas_call(
        moments_kernel,
        out_shape=(
            jax.ShapeDtypeStruct((bricks, 8, LANES), jnp.float32),
            jax.ShapeDtypeStruct((bricks, LANES), jnp.float32),
            jax.ShapeDtypeStruct((FEAT, LANES), jnp.float32),
            message,
            message,
        ),
        scratch_shapes=[
            pltpu.VMEM((2, devices // 4, LANES, LANES), jnp.float32),
            pltpu.VMEM((8 * LANES, LANES), jnp.float32),
            pltpu.VMEM((8 * LANES, LANES), jnp.float32),
        ],
        compiler_params=pltpu.CompilerParams(vmem_limit_bytes=12 << 20),
        cost_estimate=pl.CostEstimate(flops=1_000_000_000, bytes_accessed=12_000_000, transcendentals=0),
        name="moments",
    )(got, *records)


def power_of_two(value):
    scale = jnp.ones_like(value)
    inverse = jnp.ones_like(value)
    for k in (64, 32, 16, 8, 4, 2, 1):
        up, down = 2.0**k, 2.0**-k
        large = value * down >= 1.0
        small = value * up <= 1.0
        value = jnp.where(large, value * down, jnp.where(small, value * up, value))
        scale = jnp.where(large, scale * up, jnp.where(small, scale * down, scale))
        inverse = jnp.where(large, inverse * down, jnp.where(small, inverse * up, inverse))
    return scale, inverse


def krylov_kernel(
    moments_ref, vectors_ref, gathered_ref, low_ref, high_ref, below_ref, above_ref, first_ref, second_ref, mask_ref,
    feats_ref, reg_ref, basis_ref, message_ref, moment_store, vector_store, moment_lanes,
    corner_store, corner_masks, corner_lanes,
):
    moment_store[...] = jnp.zeros_like(moment_store)
    corner_store[...] = jnp.zeros_like(corner_store)
    corner_masks[...] = jnp.zeros_like(corner_masks)
    vector_store[...] = jnp.zeros_like(vector_store)

    def put_moment(a, e, value):
        moment_store[lane_of(a, e)] = value

    def put_vector(a, e, value):
        vector_store[lane_of(a, e) : lane_of(a, e) + 1, :] = value

    edges = (low_ref, high_ref, below_ref, above_ref)
    place_bricks(put_moment, LATE, 0, moments_ref, *edges)
    place_bricks(put_vector, LATE, 1, vectors_ref, *edges)
    start = message_rows(LATE, across_rows)
    for ref, e in ((below_ref, -1), (above_ref, BY)):
        for k, a in enumerate((-1, BX)):
            place = lane_of(a, e) % LANES
            corner_store[place] = ref[start + 8 * k : start + 8 * k + 8, :]
            corner_masks[place : place + 1, :] = ref[start + 16 + k : start + 17 + k, :]
    to_lanes(moment_store, moment_lanes)
    to_lanes(corner_store, corner_lanes)
    vectors = vector_store[...].T
    lane = lax.broadcasted_iota(jnp.int32, (1, LANES), 1)
    front = (lane == lane_of(-1, -1)) | (lane == lane_of(-1, BY))
    rear = (lane == lane_of(BX, -1) % LANES) | (lane == lane_of(BX, BY) % LANES)

    def both_tiles(x):
        return jnp.concatenate([jnp.where(front, x, 0.0), jnp.where(rear, x, 0.0)], axis=1)

    masks = mask_ref[...] + both_tiles(corner_masks[...].T[:8, :])

    def coupled(z):
        near = masks[0:1] * pltpu.roll(z, PITCH, 1) + masks[1:2] * pltpu.roll(z, SPAN - PITCH, 1)
        near = near + masks[2:3] * pltpu.roll(z, 1, 1) + masks[3:4] * pltpu.roll(z, SPAN - 1, 1)
        return coupling_weight * (masks[4:5] * z - near)

    def system(z):
        return times(moment_lanes, z) + coupled(z)

    one = vectors[3 * FEAT :] + coupled(vectors[0:FEAT])
    corners = times(corner_lanes, jnp.where(front, one[:, :LANES], one[:, LANES:]))
    two = system(times(first_ref, one) + both_tiles(corners) + vectors[FEAT : 2 * FEAT])
    three = system(times(first_ref, two) + times(second_ref, one) + vectors[2 * FEAT : 3 * FEAT])
    gathered = gathered_ref[...]
    for b in range(BX * BY):
        place = lane_of(b // BY, b % BY)
        feats = feats_ref[b]
        columns = [gathered[:, b : b + 1]] + [values[:, place : place + 1] for values in (one, two, three)]
        for step, column in enumerate(columns):
            basis_ref[step, b : b + 1, :] = jnp.sum(feats * column, axis=0, keepdims=True)
    reg = reg_ref[...]
    basis = [basis_ref[0]]
    for step in range(1, 4):
        basis.append(basis_ref[step] + reg * basis[-1])
        basis_ref[step] = basis[-1]

    def folded(x, combine):
        rows = [x[8 * k : 8 * k + 8, :] for k in range(x.shape[0] // 8)]
        parts = [r[:, LANES * k : LANES * (k + 1)] for r in rows for k in range(x.shape[1] // LANES)]
        while len(parts) > 1:
            parts = [combine(parts[k], parts[k + 1]) for k in range(0, len(parts), 2)]
        return parts[0]

    peaks = [jnp.max(folded(jnp.abs(v), jnp.maximum), axis=0, keepdims=True) for v in basis]
    peaks = jnp.max(jnp.concatenate(peaks + peaks, axis=0), axis=1, keepdims=True)
    scale, inverse = power_of_two(jnp.broadcast_to(peaks, (8, LANES)))
    scaled = [v * inverse[k : k + 1, 0:1] for k, v in enumerate(basis)]
    sums = [jnp.sum(folded(scaled[a] * scaled[b], jnp.add), axis=0, keepdims=True) for a, b in PAIRS]
    sums = jnp.concatenate(sums + [jnp.zeros((16 - len(PAIRS), LANES), jnp.float32)], axis=0)
    sums = jnp.sum(sums, axis=1, keepdims=True)
    row = jnp.zeros((1, LANES), jnp.float32)
    for k in range(len(PAIRS)):
        row = jnp.where(lane == k, sums[k : k + 1, :], row)
    for k in range(4):
        row = jnp.where(lane == 10 + k, scale[k : k + 1, :], row)
        row = jnp.where(lane == 14 + k, inverse[k : k + 1, :], row)
    message_ref[...] = jnp.broadcast_to(row, message_ref.shape)


def krylov(moments, vectors, gathered, edges, first, second, masks, voxel_feats, voxel_reg, devices):
    bricks, _, voxels = voxel_feats.shape
    return pl.pallas_call(
        krylov_kernel,
        out_shape=(
            jax.ShapeDtypeStruct((4, bricks, voxels), jnp.float32),
            jax.ShapeDtypeStruct((devices, LANES), jnp.float32),
        ),
        scratch_shapes=[
            pltpu.VMEM((SPAN, 8, LANES), jnp.float32),
            pltpu.VMEM((SPAN, LANES), jnp.float32),
            pltpu.VMEM((8 * LANES, SPAN), jnp.float32),
            pltpu.VMEM((LANES, 8, LANES), jnp.float32),
            pltpu.VMEM((LANES, LANES), jnp.float32),
            pltpu.VMEM((8 * LANES, LANES), jnp.float32),
        ],
        compiler_params=pltpu.CompilerParams(vmem_limit_bytes=12 << 20),
        name="krylov",
    )(moments, vectors, gathered, *edges, first, second, masks, voxel_feats, voxel_reg)


def finish_kernel(shared_ref, basis_ref, solution_ref, residual_ref):
    shared = shared_ref[...]
    lane = lax.broadcasted_iota(jnp.int32, (1, LANES), 1)

    def pick(row, k):
        return jnp.sum(jnp.where(lane == k, row, 0.0), axis=1, keepdims=True)

    largest = jnp.max(shared, axis=0, keepdims=True)
    smallest = jnp.min(shared, axis=0, keepdims=True)
    scale = [pick(largest, 10 + k) for k in range(4)]
    inverse = [pick(smallest, 14 + k) for k in range(4)]
    weight = [shared[:, 10 + k : 11 + k] * inverse[k] for k in range(4)]
    left = jnp.zeros_like(shared)
    right = jnp.zeros_like(shared)
    for k, (a, b) in enumerate(PAIRS):
        left = jnp.where(lane == k, weight[a], left)
        right = jnp.where(lane == k, weight[b], right)
    total = jnp.sum(shared * left * right, axis=0, keepdims=True)
    gram = [[None] * 4 for _ in range(4)]
    for k, (a, b) in enumerate(PAIRS):
        gram[a][b] = gram[b][a] = pick(total, k)
    growth = [scale[k + 1] * inverse[k] for k in range(3)]

    def product(left, right):
        terms = [
            left[a] * right[b] * gram[a][b]
            for a in range(4)
            for b in range(4)
            if left[a] is not None and right[b] is not None
        ]
        return functools.reduce(jnp.add, terms)

    def plus(left, factor, right):
        out = []
        for a, b in zip(left, right):
            out.append(a if b is None else factor * b if a is None else a + factor * b)
        return out

    def image(vector):
        return [None] + [None if vector[k] is None else vector[k] * growth[k] for k in range(3)]

    solution = [None] * 4
    residual = [jnp.ones((1, 1), jnp.float32), None, None, None]
    direction = list(residual)
    norm_now = product(residual, residual)
    for iteration in range(ITERS):
        carried = image(direction)
        alpha = norm_now / product(direction, carried)
        solution = plus(solution, alpha, direction)
        residual = plus(residual, -alpha, carried)
        if iteration + 1 < ITERS:
            norm_next = product(residual, residual)
            direction = plus(residual, norm_next / norm_now, direction)
            norm_now = norm_next
    back = [scale[0] * inverse[k] for k in range(4)]
    for out_ref, coefficients in ((solution_ref, solution), (residual_ref, residual)):
        total = None
        for k, c in enumerate(coefficients):
            if c is not None:
                term = (c * back[k]) * basis_ref[k]
                total = term if total is None else total + term
        out_ref[...] = total


def finish(shared, basis):
    _, bricks, voxels = basis.shape
    out = jax.ShapeDtypeStruct((bricks, voxels), jnp.float32)
    return pl.pallas_call(
        finish_kernel,
        out_shape=(out, out),
        compiler_params=pltpu.CompilerParams(vmem_limit_bytes=4 << 20),
        name="finish",
    )(shared, basis)


def shards(point_feats, point_targets, point_lists, brick_adjacency, voxel_feats, voxel_reg):
    feat_count = point_feats.shape[0]
    brick_total, slots = point_lists.shape
    local_bricks = voxel_feats.shape[0]
    devices = brick_total // local_bricks
    sending = pack(point_feats, point_targets, point_lists, devices)
    got = lax.all_to_all(sending, GX_GY, split_axis=0, concat_axis=0, tiled=True)

    first, second, third = prepare(voxel_feats, voxel_reg)
    mask = (brick_adjacency >= 0).astype(jnp.float32)
    mask = jnp.concatenate([mask, jnp.sum(mask, axis=1, keepdims=True)], axis=1)
    mask = jnp.pad(mask, ((0, 0), (0, LANES - 5)))
    early = (first, second, mask)
    along_even = lax.axis_index("gx_2") == 0
    across_even = lax.axis_index("gy") % 2 == 0
    early_low, early_high = swap(*along_messages(EARLY, early), GX, along_even)
    early_below, early_above = swap(*across_early(early), "gy", across_even)

    moments, vectors, gathered, to_low, to_high = find_moments(got, (first, second, third))
    low, high = swap(to_low, to_high, GX, along_even)
    first_lanes, second_lanes, mask_lanes = gather_early(
        first, second, mask, (early_low, early_high, early_below, early_above)
    )
    below, above = swap(
        *across_late(moments, vectors, low, high, early_low, early_high), "gy", across_even
    )
    basis, message = krylov(
        moments, vectors, gathered, (low, high, below, above), first_lanes, second_lanes, mask_lanes,
        voxel_feats, voxel_reg, devices,
    )
    shared = lax.all_to_all(message, GX_GY, split_axis=0, concat_axis=0, tiled=True)
    return finish(shared, basis)


def solution(mesh):
    torus = Mesh(mesh.devices.reshape(4, 4, 2, mesh.shape["gy"]), ("gx_0", "gx_1", "gx_2", "gy"))
    return jax.shard_map(
        shards,
        mesh=torus,
        in_specs=(
            P(None, GX_GY),
            P(GX_GY),
            P(GX_GY, None),
            P(GX_GY, None),
            P(GX_GY, None, None),
            P(GX_GY, None),
        ),
        out_specs=(P(GX_GY, None), P(GX_GY, None)),
        check_vma=False,
    )
```

```python
import functools

import jax
import jax.numpy as jnp
from jax import lax
from jax.experimental import pallas as pl
from jax.experimental.pallas import tpu as pltpu
from jax.sharding import Mesh
from jax.sharding import PartitionSpec as P

BX = 8
BY = 4
ITERS = 3
SLOTS = 8
LANES = 128
FEAT = 32
PITCH = 16
SPAN = 256
REACH = 3
GX_GY = ("gx_0", "gx_1", "gx_2", "gy")
GX = ("gx_0", "gx_1", "gx_2")
HIGHEST = lax.Precision.HIGHEST
PAIRS = tuple((a, b) for a in range(4) for b in range(a, 4))


coupling_weight = 1.0

EARLY = ((8, 2, False), (8, 1, False), (1, 2, False))
LATE = ((8, 1, True), (1, 3, True))
CORNER_ROWS = 24


def padded(rows):
    return (rows + 7) // 8 * 8


def along_rows(section):
    return padded(section[0] * section[1] * BY)


def beyond(section, away):
    return section[1] - away if section[2] else 0


def across_rows(section):
    rows, depth, _ = section
    return padded(rows * sum(BX + 2 * beyond(section, k) for k in range(1, depth + 1)))


def message_rows(sections, size):
    return sum(size(section) for section in sections)


def piece(ref, start, rows, index):
    if rows == 8 and len(ref.shape) == 3:
        return ref[index]
    return ref[start + rows * index : start + rows * (index + 1), :]


def brick_at(own, low, high, start, section, a, e):
    rows, depth, _ = section
    if a < 0:
        return piece(low, start, rows, (a + depth) * BY + e)
    if a >= BX:
        return piece(high, start, rows, (a - BX) * BY + e)
    return piece(own, 0, rows, a * BY + e)


def fill_across(sections, owns, low, high, to_low, to_high):
    source = target = 0
    for section, own in zip(sections, owns):
        rows, depth, _ = section
        index = 0
        for away in range(1, depth + 1):
            extra = beyond(section, away)
            for a in range(-extra, BX + extra):
                place = slice(target + rows * index, target + rows * (index + 1))
                to_low[place, :] = brick_at(own, low, high, source, section, a, away - 1)
                to_high[place, :] = brick_at(own, low, high, source, section, a, BY - away)
                index += 1
        used, whole = rows * index, across_rows(section)
        if used < whole:
            blank = jnp.zeros((whole - used, LANES), jnp.float32)
            to_low[target + used : target + whole, :] = blank
            to_high[target + used : target + whole, :] = blank
        source += along_rows(section)
        target += whole


def place_bricks(put, sections, which, own, along_low, along_high, across_low, across_high):
    section = sections[which]
    rows, depth, _ = section
    start = message_rows(sections[:which], along_rows)
    for a in range(-depth, BX + depth):
        for e in range(BY):
            put(a, e, brick_at(own, along_low, along_high, start, section, a, e))
    start = message_rows(sections[:which], across_rows)
    index = 0
    for away in range(1, depth + 1):
        extra = beyond(section, away)
        for a in range(-extra, BX + extra):
            put(a, -away, piece(across_low, start, rows, index))
            put(a, BY - 1 + away, piece(across_high, start, rows, index))
            index += 1


def lane_of(a, e):
    return (a + REACH) * PITCH + e + REACH


def to_lanes(records, lanes_ref):
    for t in range(8):
        lanes_ref[t * LANES : (t + 1) * LANES, :] = records[:, t, :].T


def times(matrix_ref, vector):
    total = None
    for t in range(8):
        for q in range(4):
            i = 8 * q + t
            row = t * LANES + q * FEAT
            term = matrix_ref[row : row + FEAT, :] * vector[i : i + 1, :]
            total = term if total is None else total + term
    return total


def pack_kernel(
    lists_hbm, feats_ref, targets_hbm, out_ref, lists_ref, feats, targets_ref, packed, arrived, left, small
):
    steps = arrived.shape[0]
    lists_copy = pltpu.make_async_copy(lists_hbm, lists_ref, small.at[0])
    targets_copy = pltpu.make_async_copy(targets_hbm, targets_ref, small.at[1])
    lists_copy.start()
    targets_copy.start()
    devices = out_ref.shape[0]
    bricks = lists_ref.shape[1]
    dests = devices // steps
    width = LANES * SLOTS
    points = bricks * SLOTS // steps
    arriving = [
        pltpu.make_async_copy(
            feats_ref.at[:, k * points : (k + 1) * points], feats.at[:, k * points : (k + 1) * points], arrived.at[k]
        )
        for k in range(steps)
    ]
    leaving = [
        pltpu.make_async_copy(
            packed.at[k * dests : (k + 1) * dests], out_ref.at[k * dests : (k + 1) * dests], left.at[k]
        )
        for k in range(steps)
    ]
    for copy in arriving:
        copy.start()
    lists_copy.wait()
    rows = bricks // LANES
    lane = lax.broadcasted_iota(jnp.int32, (SLOTS, LANES), 1)
    codes = []
    for block in range(rows):
        chosen = lists_ref[:, block * LANES : (block + 1) * LANES]
        offset = chosen - (lane + block * LANES) * SLOTS
        bits = jnp.where(chosen >= 0, lax.shift_left(1, jnp.clip(offset, 0, SLOTS - 1)), 0)
        codes.append(jnp.sum(bits, axis=0, keepdims=True))
    code = jnp.concatenate(codes, axis=0).astype(jnp.float32).astype(jnp.bfloat16)
    brick = lax.broadcasted_iota(jnp.int32, (LANES, width), 0)
    point = lax.broadcasted_iota(jnp.int32, (LANES, width), 1)
    spread = (lax.shift_right_logical(point, 3) == brick).astype(jnp.float32).astype(jnp.bfloat16)
    wide = jnp.dot(code, spread, preferred_element_type=jnp.float32).astype(jnp.int32)
    slot = lax.broadcasted_iota(jnp.int32, (rows, width), 1) & (SLOTS - 1)
    mask = (lax.shift_right_logical(wide, slot) & 1).astype(jnp.float32)
    targets_copy.wait()
    for k in range(steps):
        arriving[k].wait()
        for part in range(points // width):
            first = k * points + part * width
            row = mask[first // width : first // width + 1, :].astype(jnp.bfloat16)
            masked = feats[:, first : first + width] * row
            for piece_index in range(width // LANES):
                dest = (first + piece_index * LANES) // (2 * LANES)
                half = piece_index % 2
                packed[dest, half * FEAT : (half + 1) * FEAT, :] = masked[
                    :, piece_index * LANES : (piece_index + 1) * LANES
                ]
        for dest in range(k * dests, (k + 1) * dests):
            packed[dest, 2 * FEAT : 2 * FEAT + 2, :] = targets_ref[2 * dest : 2 * dest + 2, :]
        leaving[k].start()
    for copy in leaving:
        copy.wait()


def pack(point_feats, point_targets, point_lists, devices):
    points = point_feats.shape[1]
    steps = 8
    rows = 2 * FEAT + 2
    return pl.pallas_call(
        pack_kernel,
        in_specs=[
            pl.BlockSpec(memory_space=pl.ANY),
            pl.BlockSpec(memory_space=pl.ANY),
            pl.BlockSpec(memory_space=pl.ANY),
        ],
        out_specs=pl.BlockSpec(memory_space=pl.ANY),
        out_shape=jax.ShapeDtypeStruct((devices, rows, LANES), jnp.bfloat16),
        scratch_shapes=[
            pltpu.VMEM(point_lists.shape[::-1], jnp.int32),
            pltpu.VMEM((FEAT, points), jnp.bfloat16),
            pltpu.VMEM((points // LANES, LANES), jnp.bfloat16),
            pltpu.VMEM((devices, rows, LANES), jnp.bfloat16),
            pltpu.SemaphoreType.DMA((steps,)),
            pltpu.SemaphoreType.DMA((steps,)),
            pltpu.SemaphoreType.DMA((2,)),
        ],
        name="pack",
    )(point_lists.T, point_feats, point_targets.reshape(points // LANES, LANES))


def spread_rows(square, lane_group):
    square = square + pltpu.roll(square, 64, 1)
    square = square + pltpu.roll(square, 32, 1)
    record = square[0:8, :]
    for q in range(1, 4):
        record = jnp.where(lane_group == q, square[8 * q : 8 * q + 8, :], record)
    return record


def three_parts(x):
    high = x.astype(jnp.bfloat16)
    rest = x - high.astype(jnp.float32)
    middle = rest.astype(jnp.bfloat16)
    return high, middle, (rest - middle.astype(jnp.float32)).astype(jnp.bfloat16)


def prepare_kernel(feats_ref, reg_ref, *records):

    lane_group = lax.broadcasted_iota(jnp.int32, (1, LANES), 1) // FEAT
    together = 4

    def some(step, carry):
        for k in range(together):
            b = step * together + k
            feats = feats_ref[b]
            reg = reg_ref[pl.ds(b, 1), :]
            once = feats * reg
            parts = three_parts(jnp.concatenate([feats, once, once * reg], axis=0))
            left = jnp.concatenate(parts, axis=0)
            right = [part[:FEAT, :] for part in parts]
            right = jnp.concatenate([*right, jnp.zeros_like(right[0])], axis=0)
            product = lax.dot_general(
                left, right, (((1,), (1,)), ((), ())), preferred_element_type=jnp.float32
            )
            size = 3 * FEAT
            total = jnp.where(lane_group < 1, product[2 * size :, :], 0.0)
            total = total + jnp.where(lane_group < 2, product[size : 2 * size, :], 0.0)
            total = total + product[:size, :]
            for power, record in enumerate(records):
                record[b] = spread_rows(total[power * FEAT : (power + 1) * FEAT, :], lane_group)
        return carry

    lax.fori_loop(0, feats_ref.shape[0] // together, some, 0)


def prepare(voxel_feats, voxel_reg):
    bricks = voxel_feats.shape[0]
    record = jax.ShapeDtypeStruct((bricks, 8, LANES), jnp.float32)
    return pl.pallas_call(
        prepare_kernel,
        out_shape=(record, record, record),
        compiler_params=pltpu.CompilerParams(vmem_limit_bytes=10 << 20),
        cost_estimate=pl.CostEstimate(flops=600_000_000, bytes_accessed=5_000_000, transcendentals=0),
        name="prepare",
    )(voxel_feats, voxel_reg)


def gather_early_kernel(
    first_ref, second_ref, mask_ref, low_ref, high_ref, below_ref, above_ref,
    first_lanes, second_lanes, mask_lanes, first_store, second_store, mask_store,
):
    for store in (first_store, second_store, mask_store):
        store[...] = jnp.zeros_like(store)

    def put(store):
        def write(a, e, value):
            if len(store.shape) == 3:
                store[lane_of(a, e)] = value
            else:
                store[lane_of(a, e) : lane_of(a, e) + 1, :] = value

        return write

    edges = (low_ref, high_ref, below_ref, above_ref)
    place_bricks(put(first_store), EARLY, 0, first_ref, *edges)
    place_bricks(put(second_store), EARLY, 1, second_ref, *edges)
    place_bricks(put(mask_store), EARLY, 2, mask_ref, *edges)
    to_lanes(first_store, first_lanes)
    to_lanes(second_store, second_lanes)
    mask_lanes[...] = mask_store[...].T[:8, :]


def gather_early(first, second, mask, edges):
    lanes = jax.ShapeDtypeStruct((8 * LANES, SPAN), jnp.float32)
    return pl.pallas_call(
        gather_early_kernel,
        out_shape=(lanes, lanes, jax.ShapeDtypeStruct((8, SPAN), jnp.float32)),
        scratch_shapes=[
            pltpu.VMEM((SPAN, 8, LANES), jnp.float32),
            pltpu.VMEM((SPAN, 8, LANES), jnp.float32),
            pltpu.VMEM((SPAN, LANES), jnp.float32),
        ],
        compiler_params=pltpu.CompilerParams(vmem_limit_bytes=10 << 20),
        cost_estimate=pl.CostEstimate(flops=2_000_000, bytes_accessed=3_000_000, transcendentals=0),
        name="gather_early",
    )(first, second, mask, *edges)


def across_early_kernel(first_ref, second_ref, mask_ref, to_low, to_high):
    fill_across(EARLY, (first_ref, second_ref, mask_ref), None, None, to_low, to_high)


def across_early(owns):
    out = jax.ShapeDtypeStruct((message_rows(EARLY, across_rows), LANES), jnp.float32)
    return pl.pallas_call(
        across_early_kernel,
        out_shape=(out, out),
        compiler_params=pltpu.CompilerParams(vmem_limit_bytes=4 << 20),
        name="across_early",
    )(*owns)


def across_late_kernel(moments_ref, vectors_ref, low, high, early_low, early_high, to_low, to_high):
    fill_across(LATE, (moments_ref, vectors_ref), low, high, to_low, to_high)
    start = message_rows(LATE, across_rows)
    masks = message_rows(EARLY[:2], along_rows)
    for out, e in ((to_low, 0), (to_high, BY - 1)):
        rows = []
        for k, (source, index) in enumerate(((early_low, BY + e), (early_high, e))):
            out[start + 8 * k : start + 8 * k + 8, :] = source[8 * index : 8 * index + 8, :]
            rows.append(source[masks + index : masks + index + 1, :])
        rows.append(jnp.zeros((6, LANES), jnp.float32))
        out[start + 16 : start + CORNER_ROWS, :] = jnp.concatenate(rows, axis=0)


def across_late(moments, vectors, low, high, early_low, early_high):
    out = jax.ShapeDtypeStruct((message_rows(LATE, across_rows) + CORNER_ROWS, LANES), jnp.float32)
    return pl.pallas_call(
        across_late_kernel,
        out_shape=(out, out),
        compiler_params=pltpu.CompilerParams(vmem_limit_bytes=4 << 20),
        name="across_late",
    )(moments, vectors, low, high, early_low, early_high)


def along_messages(sections, owns):
    to_low, to_high = [], []
    for (rows, depth, _), own in zip(sections, owns):
        flat = own.reshape(-1, LANES)
        used = rows * depth * BY
        blank = ((0, padded(used) - used), (0, 0))
        to_low.append(jnp.pad(flat[:used], blank))
        to_high.append(jnp.pad(flat[flat.shape[0] - used :], blank))
    return jnp.concatenate(to_low), jnp.concatenate(to_high)


def swap(to_low, to_high, axis, even):
    count = lax.axis_size(axis)

    def pairs(start):
        return [pair for a in range(start, count - 1, 2) for pair in ((a, a + 1), (a + 1, a))]

    odd = jnp.logical_not(even)
    second = lax.ppermute(jnp.where(odd, to_high, to_low), axis, pairs(1))
    first = lax.ppermute(jnp.where(odd, to_low, to_high), axis, pairs(0))
    return jnp.where(odd, first, second), jnp.where(odd, second, first)


def moments_kernel(
    got_ref, first_ref, second_ref, third_ref, moments_ref, vectors_ref, gathered_ref, low_ref, high_ref,
    turned, lanes_ref, moment_lanes,
):
    for t in range(8):
        block = [record[:, t, :] for record in (first_ref, second_ref, third_ref)]
        block = jnp.concatenate([*block, jnp.zeros((BX * BY, LANES), jnp.float32)], axis=0)
        lanes_ref[t * LANES : (t + 1) * LANES, :] = block.T
    sources = got_ref.shape[0]
    for group in range(sources // 4):
        for half in range(2):
            block = got_ref[4 * group : 4 * group + 4, half * FEAT : (half + 1) * FEAT, :]
            turned[half, group] = block.astype(jnp.float32).reshape(LANES, LANES).T
    sums = []
    for half in range(2):
        total = jnp.zeros((FEAT, LANES), jnp.float32)
        for source in range(sources):
            feats = got_ref[source, half * FEAT : (half + 1) * FEAT, :].astype(jnp.float32)
            target = got_ref[source, 2 * FEAT : 2 * FEAT + 2, :].astype(jnp.float32)
            total = total + feats * target[half : half + 1, :]
        sums.append(total)

    groups = turned.shape[1]
    lane_group = lax.broadcasted_iota(jnp.int32, (1, LANES), 1) // FEAT
    for half in range(2):
        for pair in range(8):
            for k in range(2):
                b = 2 * pair + k
                points = turned[half, :, 8 * b : 8 * b + 8, :].reshape(groups * 8, LANES)
                square = lax.dot_general(
                    points.T.astype(jnp.bfloat16),
                    points.astype(jnp.bfloat16),
                    (((1,), (0,)), ((), ())),
                    preferred_element_type=jnp.float32,
                )
                own = jnp.zeros((FEAT, LANES), jnp.float32)
                for q in range(4):
                    own = own + jnp.where(lane_group == q, square[q * FEAT : (q + 1) * FEAT, :], 0.0)
                moments_ref[half * 16 + b] = spread_rows(own, lane_group)
    point = lax.broadcasted_iota(jnp.int32, (LANES, LANES), 0) // SLOTS
    lane = lax.broadcasted_iota(jnp.int32, (LANES, LANES), 1)
    values = jnp.zeros((FEAT, LANES), jnp.float32)
    for half in range(2):
        spread = (lane % (BX * BY) == point + half * 16).astype(jnp.float32)
        values = values + jnp.dot(
            sums[half], spread, precision=HIGHEST, preferred_element_type=jnp.float32
        )
    gathered_ref[...] = values
    values = times(lanes_ref, values)
    for t in range(8):
        block = [moments_ref[:, t, :], jnp.zeros((LANES - BX * BY, LANES), jnp.float32)]
        moment_lanes[t * LANES : (t + 1) * LANES, :] = jnp.concatenate(block, axis=0).T
    values = jnp.where(lane_group == 3, pltpu.roll(times(moment_lanes, values), 96, 1), values)
    values = jnp.concatenate([values, jnp.zeros((LANES - FEAT, LANES), jnp.float32)], axis=0).T
    bricks = BX * BY
    vectors = jnp.concatenate([values[k * bricks : (k + 1) * bricks, :FEAT] for k in range(4)], axis=1)
    vectors_ref[...] = vectors
    depth = LATE[0][1] * BY
    for k in range(depth):
        low_ref[8 * k : 8 * k + 8, :] = moments_ref[k]
        high_ref[8 * k : 8 * k + 8, :] = moments_ref[BX * BY - depth + k]
    deep = LATE[1][1] * BY
    blank = jnp.zeros((padded(deep) - deep, LANES), jnp.float32)
    low_ref[8 * depth :, :] = jnp.concatenate([vectors[:deep], blank], axis=0)
    high_ref[8 * depth :, :] = jnp.concatenate([vectors[BX * BY - deep : BX * BY], blank], axis=0)


def find_moments(got, records):
    devices = got.shape[0]
    bricks = BX * BY
    message = jax.ShapeDtypeStruct((message_rows(LATE, along_rows), LANES), jnp.float32)
    return pl.pallas_call(
        moments_kernel,
        out_shape=(
            jax.ShapeDtypeStruct((bricks, 8, LANES), jnp.float32),
            jax.ShapeDtypeStruct((bricks, LANES), jnp.float32),
            jax.ShapeDtypeStruct((FEAT, LANES), jnp.float32),
            message,
            message,
        ),
        scratch_shapes=[
            pltpu.VMEM((2, devices // 4, LANES, LANES), jnp.float32),
            pltpu.VMEM((8 * LANES, LANES), jnp.float32),
            pltpu.VMEM((8 * LANES, LANES), jnp.float32),
        ],
        compiler_params=pltpu.CompilerParams(vmem_limit_bytes=12 << 20),
        cost_estimate=pl.CostEstimate(flops=1_000_000_000, bytes_accessed=12_000_000, transcendentals=0),
        name="moments",
    )(got, *records)


def power_of_two(value):
    scale = jnp.ones_like(value)
    inverse = jnp.ones_like(value)
    for k in (64, 32, 16, 8, 4, 2, 1):
        up, down = 2.0**k, 2.0**-k
        large = value * down >= 1.0
        small = value * up <= 1.0
        value = jnp.where(large, value * down, jnp.where(small, value * up, value))
        scale = jnp.where(large, scale * up, jnp.where(small, scale * down, scale))
        inverse = jnp.where(large, inverse * down, jnp.where(small, inverse * up, inverse))
    return scale, inverse


def krylov_kernel(
    moments_ref, vectors_ref, gathered_ref, low_ref, high_ref, below_ref, above_ref, first_ref, second_ref, mask_ref,
    feats_ref, reg_ref, basis_ref, message_ref, moment_store, vector_store, moment_lanes,
    corner_store, corner_masks, corner_lanes,
):
    moment_store[...] = jnp.zeros_like(moment_store)
    corner_store[...] = jnp.zeros_like(corner_store)
    corner_masks[...] = jnp.zeros_like(corner_masks)
    vector_store[...] = jnp.zeros_like(vector_store)

    def put_moment(a, e, value):
        moment_store[lane_of(a, e)] = value

    def put_vector(a, e, value):
        vector_store[lane_of(a, e) : lane_of(a, e) + 1, :] = value

    edges = (low_ref, high_ref, below_ref, above_ref)
    place_bricks(put_moment, LATE, 0, moments_ref, *edges)
    place_bricks(put_vector, LATE, 1, vectors_ref, *edges)
    start = message_rows(LATE, across_rows)
    for ref, e in ((below_ref, -1), (above_ref, BY)):
        for k, a in enumerate((-1, BX)):
            place = lane_of(a, e) % LANES
            corner_store[place] = ref[start + 8 * k : start + 8 * k + 8, :]
            corner_masks[place : place + 1, :] = ref[start + 16 + k : start + 17 + k, :]
    to_lanes(moment_store, moment_lanes)
    to_lanes(corner_store, corner_lanes)
    vectors = vector_store[...].T
    lane = lax.broadcasted_iota(jnp.int32, (1, LANES), 1)
    front = (lane == lane_of(-1, -1)) | (lane == lane_of(-1, BY))
    rear = (lane == lane_of(BX, -1) % LANES) | (lane == lane_of(BX, BY) % LANES)

    def both_tiles(x):
        return jnp.concatenate([jnp.where(front, x, 0.0), jnp.where(rear, x, 0.0)], axis=1)

    masks = mask_ref[...] + both_tiles(corner_masks[...].T[:8, :])

    def coupled(z):
        near = masks[0:1] * pltpu.roll(z, PITCH, 1) + masks[1:2] * pltpu.roll(z, SPAN - PITCH, 1)
        near = near + masks[2:3] * pltpu.roll(z, 1, 1) + masks[3:4] * pltpu.roll(z, SPAN - 1, 1)
        return coupling_weight * (masks[4:5] * z - near)

    def system(z):
        return times(moment_lanes, z) + coupled(z)

    one = vectors[3 * FEAT :] + coupled(vectors[0:FEAT])
    corners = times(corner_lanes, jnp.where(front, one[:, :LANES], one[:, LANES:]))
    two = system(times(first_ref, one) + both_tiles(corners) + vectors[FEAT : 2 * FEAT])
    three = system(times(first_ref, two) + times(second_ref, one) + vectors[2 * FEAT : 3 * FEAT])
    gathered = gathered_ref[...]
    for b in range(BX * BY):
        place = lane_of(b // BY, b % BY)
        feats = feats_ref[b]
        columns = [gathered[:, b : b + 1]] + [values[:, place : place + 1] for values in (one, two, three)]
        for step, column in enumerate(columns):
            basis_ref[step, b : b + 1, :] = jnp.sum(feats * column, axis=0, keepdims=True)
    reg = reg_ref[...]
    basis = [basis_ref[0]]
    for step in range(1, 4):
        basis.append(basis_ref[step] + reg * basis[-1])
        basis_ref[step] = basis[-1]

    def folded(x, combine):
        rows = [x[8 * k : 8 * k + 8, :] for k in range(x.shape[0] // 8)]
        parts = [r[:, LANES * k : LANES * (k + 1)] for r in rows for k in range(x.shape[1] // LANES)]
        while len(parts) > 1:
            parts = [combine(parts[k], parts[k + 1]) for k in range(0, len(parts), 2)]
        return parts[0]

    peaks = [jnp.max(folded(jnp.abs(v), jnp.maximum), axis=0, keepdims=True) for v in basis]
    peaks = jnp.max(jnp.concatenate(peaks + peaks, axis=0), axis=1, keepdims=True)
    scale, inverse = power_of_two(jnp.broadcast_to(peaks, (8, LANES)))
    scaled = [v * inverse[k : k + 1, 0:1] for k, v in enumerate(basis)]
    sums = [jnp.sum(folded(scaled[a] * scaled[b], jnp.add), axis=0, keepdims=True) for a, b in PAIRS]
    sums = jnp.concatenate(sums + [jnp.zeros((16 - len(PAIRS), LANES), jnp.float32)], axis=0)
    sums = jnp.sum(sums, axis=1, keepdims=True)
    row = jnp.zeros((1, LANES), jnp.float32)
    for k in range(len(PAIRS)):
        row = jnp.where(lane == k, sums[k : k + 1, :], row)
    for k in range(4):
        row = jnp.where(lane == 10 + k, scale[k : k + 1, :], row)
        row = jnp.where(lane == 14 + k, inverse[k : k + 1, :], row)
    message_ref[...] = jnp.broadcast_to(row, message_ref.shape)


def krylov(moments, vectors, gathered, edges, first, second, masks, voxel_feats, voxel_reg, devices):
    bricks, _, voxels = voxel_feats.shape
    return pl.pallas_call(
        krylov_kernel,
        out_shape=(
            jax.ShapeDtypeStruct((4, bricks, voxels), jnp.float32),
            jax.ShapeDtypeStruct((devices, LANES), jnp.float32),
        ),
        scratch_shapes=[
            pltpu.VMEM((SPAN, 8, LANES), jnp.float32),
            pltpu.VMEM((SPAN, LANES), jnp.float32),
            pltpu.VMEM((8 * LANES, SPAN), jnp.float32),
            pltpu.VMEM((LANES, 8, LANES), jnp.float32),
            pltpu.VMEM((LANES, LANES), jnp.float32),
            pltpu.VMEM((8 * LANES, LANES), jnp.float32),
        ],
        compiler_params=pltpu.CompilerParams(vmem_limit_bytes=12 << 20),
        name="krylov",
    )(moments, vectors, gathered, *edges, first, second, masks, voxel_feats, voxel_reg)


def finish_kernel(shared_ref, basis_ref, solution_ref, residual_ref):
    shared = shared_ref[...]
    lane = lax.broadcasted_iota(jnp.int32, (1, LANES), 1)

    def pick(row, k):
        return jnp.sum(jnp.where(lane == k, row, 0.0), axis=1, keepdims=True)

    largest = jnp.max(shared, axis=0, keepdims=True)
    smallest = jnp.min(shared, axis=0, keepdims=True)
    scale = [pick(largest, 10 + k) for k in range(4)]
    inverse = [pick(smallest, 14 + k) for k in range(4)]
    weight = [shared[:, 10 + k : 11 + k] * inverse[k] for k in range(4)]
    left = jnp.zeros_like(shared)
    right = jnp.zeros_like(shared)
    for k, (a, b) in enumerate(PAIRS):
        left = jnp.where(lane == k, weight[a], left)
        right = jnp.where(lane == k, weight[b], right)
    total = jnp.sum(shared * left * right, axis=0, keepdims=True)
    gram = [[None] * 4 for _ in range(4)]
    for k, (a, b) in enumerate(PAIRS):
        gram[a][b] = gram[b][a] = pick(total, k)
    growth = [scale[k + 1] * inverse[k] for k in range(3)]

    def product(left, right):
        terms = [
            left[a] * right[b] * gram[a][b]
            for a in range(4)
            for b in range(4)
            if left[a] is not None and right[b] is not None
        ]
        return functools.reduce(jnp.add, terms)

    def plus(left, factor, right):
        out = []
        for a, b in zip(left, right):
            out.append(a if b is None else factor * b if a is None else a + factor * b)
        return out

    def image(vector):
        return [None] + [None if vector[k] is None else vector[k] * growth[k] for k in range(3)]

    solution = [None] * 4
    residual = [jnp.ones((1, 1), jnp.float32), None, None, None]
    direction = list(residual)
    norm_now = product(residual, residual)
    for iteration in range(ITERS):
        carried = image(direction)
        alpha = norm_now / product(direction, carried)
        solution = plus(solution, alpha, direction)
        residual = plus(residual, -alpha, carried)
        if iteration + 1 < ITERS:
            norm_next = product(residual, residual)
            direction = plus(residual, norm_next / norm_now, direction)
            norm_now = norm_next
    back = [scale[0] * inverse[k] for k in range(4)]
    for out_ref, coefficients in ((solution_ref, solution), (residual_ref, residual)):
        total = None
        for k, c in enumerate(coefficients):
            if c is not None:
                term = (c * back[k]) * basis_ref[k]
                total = term if total is None else total + term
        out_ref[...] = total


def finish(shared, basis):
    _, bricks, voxels = basis.shape
    out = jax.ShapeDtypeStruct((bricks, voxels), jnp.float32)
    return pl.pallas_call(
        finish_kernel,
        out_shape=(out, out),
        compiler_params=pltpu.CompilerParams(vmem_limit_bytes=4 << 20),
        name="finish",
    )(shared, basis)


def shards(point_feats, point_targets, point_lists, brick_adjacency, voxel_feats, voxel_reg):
    feat_count = point_feats.shape[0]
    brick_total, slots = point_lists.shape
    local_bricks = voxel_feats.shape[0]
    devices = brick_total // local_bricks
    sending = pack(point_feats, point_targets, point_lists, devices)
    got = lax.all_to_all(sending, GX_GY, split_axis=0, concat_axis=0, tiled=True)

    first, second, third = prepare(voxel_feats, voxel_reg)
    mask = (brick_adjacency >= 0).astype(jnp.float32)
    mask = jnp.concatenate([mask, jnp.sum(mask, axis=1, keepdims=True)], axis=1)
    mask = jnp.pad(mask, ((0, 0), (0, LANES - 5)))
    early = (first, second, mask)
    along_even = lax.axis_index("gx_2") == 0
    across_even = lax.axis_index("gy") % 2 == 0
    early_low, early_high = swap(*along_messages(EARLY, early), GX, along_even)
    early_below, early_above = swap(*across_early(early), "gy", across_even)

    moments, vectors, gathered, to_low, to_high = find_moments(got, (first, second, third))
    low, high = swap(to_low, to_high, GX, along_even)
    first_lanes, second_lanes, mask_lanes = gather_early(
        first, second, mask, (early_low, early_high, early_below, early_above)
    )
    below, above = swap(
        *across_late(moments, vectors, low, high, early_low, early_high), "gy", across_even
    )
    basis, message = krylov(
        moments, vectors, gathered, (low, high, below, above), first_lanes, second_lanes, mask_lanes,
        voxel_feats, voxel_reg, devices,
    )
    shared = lax.all_to_all(message, GX_GY, split_axis=0, concat_axis=0, tiled=True)
    return finish(shared, basis)


def solution(mesh):
    torus = Mesh(mesh.devices.reshape(4, 4, 2, mesh.shape["gy"]), ("gx_0", "gx_1", "gx_2", "gy"))
    return jax.shard_map(
        shards,
        mesh=torus,
        in_specs=(
            P(None, GX_GY),
            P(GX_GY),
            P(GX_GY, None),
            P(GX_GY, None),
            P(GX_GY, None, None),
            P(GX_GY, None),
        ),
        out_specs=(P(GX_GY, None), P(GX_GY, None)),
        check_vma=False,
    )
```

```python
import functools

import jax
import jax.numpy as jnp
from jax import lax
from jax.experimental import pallas as pl
from jax.experimental.pallas import tpu as pltpu
from jax.sharding import Mesh
from jax.sharding import PartitionSpec as P

BX = 8
BY = 4
ITERS = 3
SLOTS = 8
LANES = 128
FEAT = 32
PITCH = 16
SPAN = 256
REACH = 3
GX_GY = ("gx_0", "gx_1", "gx_2", "gy")
GX = ("gx_0", "gx_1", "gx_2")
HIGHEST = lax.Precision.HIGHEST
PAIRS = tuple((a, b) for a in range(4) for b in range(a, 4))


coupling_weight = 1.0

EARLY = ((8, 2, False), (8, 1, False), (1, 2, False))
LATE = ((8, 1, True), (1, 3, True))
CORNER_ROWS = 24


def padded(rows):
    return (rows + 7) // 8 * 8


def along_rows(section):
    return padded(section[0] * section[1] * BY)


def beyond(section, away):
    return section[1] - away if section[2] else 0


def across_rows(section):
    rows, depth, _ = section
    return padded(rows * sum(BX + 2 * beyond(section, k) for k in range(1, depth + 1)))


def message_rows(sections, size):
    return sum(size(section) for section in sections)


def piece(ref, start, rows, index):
    if rows == 8 and len(ref.shape) == 3:
        return ref[index]
    return ref[start + rows * index : start + rows * (index + 1), :]


def brick_at(own, low, high, start, section, a, e):
    rows, depth, _ = section
    if a < 0:
        return piece(low, start, rows, (a + depth) * BY + e)
    if a >= BX:
        return piece(high, start, rows, (a - BX) * BY + e)
    return piece(own, 0, rows, a * BY + e)


def fill_across(sections, owns, low, high, to_low, to_high):
    source = target = 0
    for section, own in zip(sections, owns):
        rows, depth, _ = section
        index = 0
        for away in range(1, depth + 1):
            extra = beyond(section, away)
            for a in range(-extra, BX + extra):
                place = slice(target + rows * index, target + rows * (index + 1))
                to_low[place, :] = brick_at(own, low, high, source, section, a, away - 1)
                to_high[place, :] = brick_at(own, low, high, source, section, a, BY - away)
                index += 1
        used, whole = rows * index, across_rows(section)
        if used < whole:
            blank = jnp.zeros((whole - used, LANES), jnp.float32)
            to_low[target + used : target + whole, :] = blank
            to_high[target + used : target + whole, :] = blank
        source += along_rows(section)
        target += whole


def place_bricks(put, sections, which, own, along_low, along_high, across_low, across_high):
    section = sections[which]
    rows, depth, _ = section
    start = message_rows(sections[:which], along_rows)
    for a in range(-depth, BX + depth):
        for e in range(BY):
            put(a, e, brick_at(own, along_low, along_high, start, section, a, e))
    start = message_rows(sections[:which], across_rows)
    index = 0
    for away in range(1, depth + 1):
        extra = beyond(section, away)
        for a in range(-extra, BX + extra):
            put(a, -away, piece(across_low, start, rows, index))
            put(a, BY - 1 + away, piece(across_high, start, rows, index))
            index += 1


def lane_of(a, e):
    return (a + REACH) * PITCH + e + REACH


def to_lanes(records, lanes_ref):
    for t in range(8):
        lanes_ref[t * LANES : (t + 1) * LANES, :] = records[:, t, :].T


def times(matrix_ref, vector):
    total = None
    for t in range(8):
        for q in range(4):
            i = 8 * q + t
            row = t * LANES + q * FEAT
            term = matrix_ref[row : row + FEAT, :] * vector[i : i + 1, :]
            total = term if total is None else total + term
    return total


def pack_kernel(
    lists_hbm, feats_ref, targets_hbm, out_ref, lists_ref, feats, targets_ref, packed, arrived, left, small
):
    steps = arrived.shape[0]
    lists_copy = pltpu.make_async_copy(lists_hbm, lists_ref, small.at[0])
    targets_copy = pltpu.make_async_copy(targets_hbm, targets_ref, small.at[1])
    lists_copy.start()
    targets_copy.start()
    devices = out_ref.shape[0]
    bricks = lists_ref.shape[1]
    dests = devices // steps
    width = LANES * SLOTS
    points = bricks * SLOTS // steps
    arriving = [
        pltpu.make_async_copy(
            feats_ref.at[:, k * points : (k + 1) * points], feats.at[:, k * points : (k + 1) * points], arrived.at[k]
        )
        for k in range(steps)
    ]
    leaving = [
        pltpu.make_async_copy(
            packed.at[k * dests : (k + 1) * dests], out_ref.at[k * dests : (k + 1) * dests], left.at[k]
        )
        for k in range(steps)
    ]
    for copy in arriving:
        copy.start()
    lists_copy.wait()
    rows = bricks // LANES
    lane = lax.broadcasted_iota(jnp.int32, (SLOTS, LANES), 1)
    codes = []
    for block in range(rows):
        chosen = lists_ref[:, block * LANES : (block + 1) * LANES]
        offset = chosen - (lane + block * LANES) * SLOTS
        bits = jnp.where(chosen >= 0, lax.shift_left(1, jnp.clip(offset, 0, SLOTS - 1)), 0)
        codes.append(jnp.sum(bits, axis=0, keepdims=True))
    code = jnp.concatenate(codes, axis=0).astype(jnp.float32).astype(jnp.bfloat16)
    brick = lax.broadcasted_iota(jnp.int32, (LANES, width), 0)
    point = lax.broadcasted_iota(jnp.int32, (LANES, width), 1)
    spread = (lax.shift_right_logical(point, 3) == brick).astype(jnp.float32).astype(jnp.bfloat16)
    wide = jnp.dot(code, spread, preferred_element_type=jnp.float32).astype(jnp.int32)
    slot = lax.broadcasted_iota(jnp.int32, (rows, width), 1) & (SLOTS - 1)
    mask = (lax.shift_right_logical(wide, slot) & 1).astype(jnp.float32)
    targets_copy.wait()
    for k in range(steps):
        arriving[k].wait()
        for part in range(points // width):
            first = k * points + part * width
            row = mask[first // width : first // width + 1, :].astype(jnp.bfloat16)
            masked = feats[:, first : first + width] * row
            for piece_index in range(width // LANES):
                dest = (first + piece_index * LANES) // (2 * LANES)
                half = piece_index % 2
                packed[dest, half * FEAT : (half + 1) * FEAT, :] = masked[
                    :, piece_index * LANES : (piece_index + 1) * LANES
                ]
        for dest in range(k * dests, (k + 1) * dests):
            packed[dest, 2 * FEAT : 2 * FEAT + 2, :] = targets_ref[2 * dest : 2 * dest + 2, :]
        leaving[k].start()
    for copy in leaving:
        copy.wait()


def pack(point_feats, point_targets, point_lists, devices):
    points = point_feats.shape[1]
    steps = 8
    rows = 2 * FEAT + 2
    return pl.pallas_call(
        pack_kernel,
        in_specs=[
            pl.BlockSpec(memory_space=pl.ANY),
            pl.BlockSpec(memory_space=pl.ANY),
            pl.BlockSpec(memory_space=pl.ANY),
        ],
        out_specs=pl.BlockSpec(memory_space=pl.ANY),
        out_shape=jax.ShapeDtypeStruct((devices, rows, LANES), jnp.bfloat16),
        scratch_shapes=[
            pltpu.VMEM(point_lists.shape[::-1], jnp.int32),
            pltpu.VMEM((FEAT, points), jnp.bfloat16),
            pltpu.VMEM((points // LANES, LANES), jnp.bfloat16),
            pltpu.VMEM((devices, rows, LANES), jnp.bfloat16),
            pltpu.SemaphoreType.DMA((steps,)),
            pltpu.SemaphoreType.DMA((steps,)),
            pltpu.SemaphoreType.DMA((2,)),
        ],
        name="pack",
    )(point_lists.T, point_feats, point_targets.reshape(points // LANES, LANES))


def spread_rows(square, lane_group):
    square = square + pltpu.roll(square, 64, 1)
    square = square + pltpu.roll(square, 32, 1)
    record = square[0:8, :]
    for q in range(1, 4):
        record = jnp.where(lane_group == q, square[8 * q : 8 * q + 8, :], record)
    return record


def three_parts(x):
    high = x.astype(jnp.bfloat16)
    rest = x - high.astype(jnp.float32)
    middle = rest.astype(jnp.bfloat16)
    return high, middle, (rest - middle.astype(jnp.float32)).astype(jnp.bfloat16)


def prepare_kernel(feats_ref, reg_ref, *records):

    lane_group = lax.broadcasted_iota(jnp.int32, (1, LANES), 1) // FEAT
    together = 4

    def some(step, carry):
        for k in range(together):
            b = step * together + k
            feats = feats_ref[b]
            reg = reg_ref[pl.ds(b, 1), :]
            once = feats * reg
            parts = three_parts(jnp.concatenate([feats, once, once * reg], axis=0))
            left = jnp.concatenate(parts, axis=0)
            right = [part[:FEAT, :] for part in parts]
            right = jnp.concatenate([*right, jnp.zeros_like(right[0])], axis=0)
            product = lax.dot_general(
                left, right, (((1,), (1,)), ((), ())), preferred_element_type=jnp.float32
            )
            size = 3 * FEAT
            total = jnp.where(lane_group < 1, product[2 * size :, :], 0.0)
            total = total + jnp.where(lane_group < 2, product[size : 2 * size, :], 0.0)
            total = total + product[:size, :]
            for power, record in enumerate(records):
                record[b] = spread_rows(total[power * FEAT : (power + 1) * FEAT, :], lane_group)
        return carry

    lax.fori_loop(0, feats_ref.shape[0] // together, some, 0)


def prepare(voxel_feats, voxel_reg):
    bricks = voxel_feats.shape[0]
    record = jax.ShapeDtypeStruct((bricks, 8, LANES), jnp.float32)
    return pl.pallas_call(
        prepare_kernel,
        out_shape=(record, record, record),
        compiler_params=pltpu.CompilerParams(vmem_limit_bytes=10 << 20),
        cost_estimate=pl.CostEstimate(flops=600_000_000, bytes_accessed=5_000_000, transcendentals=0),
        name="prepare",
    )(voxel_feats, voxel_reg)


def gather_early_kernel(
    first_ref, second_ref, mask_ref, low_ref, high_ref, below_ref, above_ref, moments_ref, late_low, late_high,
    gathered_ref, feats_ref, first_lanes, second_lanes, mask_lanes, moment_lanes, start_ref,
    first_store, second_store, mask_store, moment_store,
):
    for store in (first_store, second_store, mask_store, moment_store):
        store[...] = jnp.zeros_like(store)
    for a in range(-1, BX + 1):
        for e in range(BY):
            moment_store[lane_of(a, e)] = brick_at(moments_ref, late_low, late_high, 0, LATE[0], a, e)
    to_lanes(moment_store, moment_lanes)
    gathered = gathered_ref[...]
    for b in range(BX * BY):
        start_ref[b : b + 1, :] = jnp.sum(feats_ref[b] * gathered[:, b : b + 1], axis=0, keepdims=True)

    def put(store):
        def write(a, e, value):
            if len(store.shape) == 3:
                store[lane_of(a, e)] = value
            else:
                store[lane_of(a, e) : lane_of(a, e) + 1, :] = value

        return write

    edges = (low_ref, high_ref, below_ref, above_ref)
    place_bricks(put(first_store), EARLY, 0, first_ref, *edges)
    place_bricks(put(second_store), EARLY, 1, second_ref, *edges)
    place_bricks(put(mask_store), EARLY, 2, mask_ref, *edges)
    to_lanes(first_store, first_lanes)
    to_lanes(second_store, second_lanes)
    mask_lanes[...] = mask_store[...].T[:8, :]


def gather_early(first, second, mask, edges, moments, late, gathered, voxel_feats):
    lanes = jax.ShapeDtypeStruct((8 * LANES, SPAN), jnp.float32)
    bricks, _, voxels = voxel_feats.shape
    store = pltpu.VMEM((SPAN, 8, LANES), jnp.float32)
    return pl.pallas_call(
        gather_early_kernel,
        out_shape=(
            lanes,
            lanes,
            jax.ShapeDtypeStruct((8, SPAN), jnp.float32),
            lanes,
            jax.ShapeDtypeStruct((bricks, voxels), jnp.float32),
        ),
        scratch_shapes=[store, store, pltpu.VMEM((SPAN, LANES), jnp.float32), store],
        compiler_params=pltpu.CompilerParams(vmem_limit_bytes=12 << 20),
        cost_estimate=pl.CostEstimate(flops=3_000_000, bytes_accessed=5_000_000, transcendentals=0),
        name="gather_early",
    )(first, second, mask, *edges, moments, *late, gathered, voxel_feats)


def across_early_kernel(first_ref, second_ref, mask_ref, to_low, to_high):
    fill_across(EARLY, (first_ref, second_ref, mask_ref), None, None, to_low, to_high)


def across_early(owns):
    out = jax.ShapeDtypeStruct((message_rows(EARLY, across_rows), LANES), jnp.float32)
    return pl.pallas_call(
        across_early_kernel,
        out_shape=(out, out),
        compiler_params=pltpu.CompilerParams(vmem_limit_bytes=4 << 20),
        name="across_early",
    )(*owns)


def across_late_kernel(moments_ref, vectors_ref, low, high, early_low, early_high, to_low, to_high):
    fill_across(LATE, (moments_ref, vectors_ref), low, high, to_low, to_high)
    start = message_rows(LATE, across_rows)
    masks = message_rows(EARLY[:2], along_rows)
    for out, e in ((to_low, 0), (to_high, BY - 1)):
        rows = []
        for k, (source, index) in enumerate(((early_low, BY + e), (early_high, e))):
            out[start + 8 * k : start + 8 * k + 8, :] = source[8 * index : 8 * index + 8, :]
            rows.append(source[masks + index : masks + index + 1, :])
        rows.append(jnp.zeros((6, LANES), jnp.float32))
        out[start + 16 : start + CORNER_ROWS, :] = jnp.concatenate(rows, axis=0)


def across_late(moments, vectors, low, high, early_low, early_high):
    out = jax.ShapeDtypeStruct((message_rows(LATE, across_rows) + CORNER_ROWS, LANES), jnp.float32)
    return pl.pallas_call(
        across_late_kernel,
        out_shape=(out, out),
        compiler_params=pltpu.CompilerParams(vmem_limit_bytes=4 << 20),
        name="across_late",
    )(moments, vectors, low, high, early_low, early_high)


def along_messages(sections, owns):
    to_low, to_high = [], []
    for (rows, depth, _), own in zip(sections, owns):
        flat = own.reshape(-1, LANES)
        used = rows * depth * BY
        blank = ((0, padded(used) - used), (0, 0))
        to_low.append(jnp.pad(flat[:used], blank))
        to_high.append(jnp.pad(flat[flat.shape[0] - used :], blank))
    return jnp.concatenate(to_low), jnp.concatenate(to_high)


def swap(to_low, to_high, axis, even):
    count = lax.axis_size(axis)

    def pairs(start):
        return [pair for a in range(start, count - 1, 2) for pair in ((a, a + 1), (a + 1, a))]

    odd = jnp.logical_not(even)
    second = lax.ppermute(jnp.where(odd, to_high, to_low), axis, pairs(1))
    first = lax.ppermute(jnp.where(odd, to_low, to_high), axis, pairs(0))
    return jnp.where(odd, first, second), jnp.where(odd, second, first)


def moments_kernel(
    got_ref, first_ref, second_ref, third_ref, moments_ref, vectors_ref, gathered_ref, low_ref, high_ref,
    turned, lanes_ref, moment_lanes,
):
    for t in range(8):
        block = [record[:, t, :] for record in (first_ref, second_ref, third_ref)]
        block = jnp.concatenate([*block, jnp.zeros((BX * BY, LANES), jnp.float32)], axis=0)
        lanes_ref[t * LANES : (t + 1) * LANES, :] = block.T
    sources = got_ref.shape[0]
    for group in range(sources // 4):
        for half in range(2):
            block = got_ref[4 * group : 4 * group + 4, half * FEAT : (half + 1) * FEAT, :]
            turned[half, group] = block.astype(jnp.float32).reshape(LANES, LANES).T
    sums = []
    for half in range(2):
        total = jnp.zeros((FEAT, LANES), jnp.float32)
        for source in range(sources):
            feats = got_ref[source, half * FEAT : (half + 1) * FEAT, :].astype(jnp.float32)
            target = got_ref[source, 2 * FEAT : 2 * FEAT + 2, :].astype(jnp.float32)
            total = total + feats * target[half : half + 1, :]
        sums.append(total)

    groups = turned.shape[1]
    lane_group = lax.broadcasted_iota(jnp.int32, (1, LANES), 1) // FEAT
    for half in range(2):
        for pair in range(8):
            for k in range(2):
                b = 2 * pair + k
                points = turned[half, :, 8 * b : 8 * b + 8, :].reshape(groups * 8, LANES)
                square = lax.dot_general(
                    points.T.astype(jnp.bfloat16),
                    points.astype(jnp.bfloat16),
                    (((1,), (0,)), ((), ())),
                    preferred_element_type=jnp.float32,
                )
                own = jnp.zeros((FEAT, LANES), jnp.float32)
                for q in range(4):
                    own = own + jnp.where(lane_group == q, square[q * FEAT : (q + 1) * FEAT, :], 0.0)
                moments_ref[half * 16 + b] = spread_rows(own, lane_group)
    point = lax.broadcasted_iota(jnp.int32, (LANES, LANES), 0) // SLOTS
    lane = lax.broadcasted_iota(jnp.int32, (LANES, LANES), 1)
    values = jnp.zeros((FEAT, LANES), jnp.float32)
    for half in range(2):
        spread = (lane % (BX * BY) == point + half * 16).astype(jnp.float32)
        values = values + jnp.dot(
            sums[half], spread, precision=HIGHEST, preferred_element_type=jnp.float32
        )
    gathered_ref[...] = values
    values = times(lanes_ref, values)
    for t in range(8):
        block = [moments_ref[:, t, :], jnp.zeros((LANES - BX * BY, LANES), jnp.float32)]
        moment_lanes[t * LANES : (t + 1) * LANES, :] = jnp.concatenate(block, axis=0).T
    values = jnp.where(lane_group == 3, pltpu.roll(times(moment_lanes, values), 96, 1), values)
    values = jnp.concatenate([values, jnp.zeros((LANES - FEAT, LANES), jnp.float32)], axis=0).T
    bricks = BX * BY
    vectors = jnp.concatenate([values[k * bricks : (k + 1) * bricks, :FEAT] for k in range(4)], axis=1)
    vectors_ref[...] = vectors
    depth = LATE[0][1] * BY
    for k in range(depth):
        low_ref[8 * k : 8 * k + 8, :] = moments_ref[k]
        high_ref[8 * k : 8 * k + 8, :] = moments_ref[BX * BY - depth + k]
    deep = LATE[1][1] * BY
    blank = jnp.zeros((padded(deep) - deep, LANES), jnp.float32)
    low_ref[8 * depth :, :] = jnp.concatenate([vectors[:deep], blank], axis=0)
    high_ref[8 * depth :, :] = jnp.concatenate([vectors[BX * BY - deep : BX * BY], blank], axis=0)


def find_moments(got, records):
    devices = got.shape[0]
    bricks = BX * BY
    message = jax.ShapeDtypeStruct((message_rows(LATE, along_rows), LANES), jnp.float32)
    return pl.pallas_call(
        moments_kernel,
        out_shape=(
            jax.ShapeDtypeStruct((bricks, 8, LANES), jnp.float32),
            jax.ShapeDtypeStruct((bricks, LANES), jnp.float32),
            jax.ShapeDtypeStruct((FEAT, LANES), jnp.float32),
            message,
            message,
        ),
        scratch_shapes=[
            pltpu.VMEM((2, devices // 4, LANES, LANES), jnp.float32),
            pltpu.VMEM((8 * LANES, LANES), jnp.float32),
            pltpu.VMEM((8 * LANES, LANES), jnp.float32),
        ],
        compiler_params=pltpu.CompilerParams(vmem_limit_bytes=12 << 20),
        cost_estimate=pl.CostEstimate(flops=1_000_000_000, bytes_accessed=12_000_000, transcendentals=0),
        name="moments",
    )(got, *records)


def power_of_two(value):
    scale = jnp.ones_like(value)
    inverse = jnp.ones_like(value)
    for k in (64, 32, 16, 8, 4, 2, 1):
        up, down = 2.0**k, 2.0**-k
        large = value * down >= 1.0
        small = value * up <= 1.0
        value = jnp.where(large, value * down, jnp.where(small, value * up, value))
        scale = jnp.where(large, scale * up, jnp.where(small, scale * down, scale))
        inverse = jnp.where(large, inverse * down, jnp.where(small, inverse * up, inverse))
    return scale, inverse


def krylov_kernel(
    moment_lanes, vectors_ref, start_ref, low_ref, high_ref, below_ref, above_ref, first_ref, second_ref, mask_ref,
    feats_ref, reg_ref, basis_ref, message_ref, vector_store, corner_store, corner_masks, corner_lanes,
):
    corner_store[...] = jnp.zeros_like(corner_store)
    corner_masks[...] = jnp.zeros_like(corner_masks)
    vector_store[...] = jnp.zeros_like(vector_store)

    def put_vector(a, e, value):
        vector_store[lane_of(a, e) : lane_of(a, e) + 1, :] = value

    edges = (low_ref, high_ref, below_ref, above_ref)
    place_bricks(put_vector, LATE, 1, vectors_ref, *edges)
    start = message_rows(LATE, across_rows)
    for ref, e in ((below_ref, -1), (above_ref, BY)):
        for k, a in enumerate((-1, BX)):
            place = lane_of(a, e) % LANES
            corner_store[(lane_of(a, e) + 8) % LANES] = ref[start + 8 * k : start + 8 * k + 8, :]
            corner_masks[place : place + 1, :] = ref[start + 16 + k : start + 17 + k, :]
        for a in range(BX):
            corner_store[lane_of(a, e) % LANES] = piece(ref, 0, 8, a)
    to_lanes(corner_store, corner_lanes)
    vectors = vector_store[...].T
    lane = lax.broadcasted_iota(jnp.int32, (1, LANES), 1)
    front = (lane == lane_of(-1, -1)) | (lane == lane_of(-1, BY))
    rear = (lane == lane_of(BX, -1) % LANES) | (lane == lane_of(BX, BY) % LANES)

    column = lane % PITCH
    beside = (column == REACH - 1) | (column == REACH + BY)
    beside_front = beside & (lane >= lane_of(0, -1))
    beside_rear = beside & (lane < lane_of(0, -1) - 8)

    def both_tiles(x):
        return jnp.concatenate([jnp.where(front, x, 0.0), jnp.where(rear, x, 0.0)], axis=1)

    def beside_times(z):
        x = times(corner_lanes, jnp.where(beside_front, z[:, :LANES], z[:, LANES:]))
        return jnp.concatenate([jnp.where(beside_front, x, 0.0), jnp.where(beside_rear, x, 0.0)], axis=1)

    masks = mask_ref[...] + both_tiles(corner_masks[...].T[:8, :])

    def coupled(z):
        near = masks[0:1] * pltpu.roll(z, PITCH, 1) + masks[1:2] * pltpu.roll(z, SPAN - PITCH, 1)
        near = near + masks[2:3] * pltpu.roll(z, 1, 1) + masks[3:4] * pltpu.roll(z, SPAN - 1, 1)
        return coupling_weight * (masks[4:5] * z - near)

    def system(z):
        return times(moment_lanes, z) + coupled(z)

    one = vectors[3 * FEAT :] + coupled(vectors[0:FEAT])
    corners = pltpu.roll(jnp.where(front, one[:, :LANES], one[:, LANES:]), 8, 1)
    corners = pltpu.roll(times(corner_lanes, corners), LANES - 8, 1)
    second_z = times(first_ref, one) + both_tiles(corners) + vectors[FEAT : 2 * FEAT]
    two = system(second_z) + beside_times(second_z)
    three = system(times(first_ref, two) + times(second_ref, one) + vectors[2 * FEAT : 3 * FEAT])
    basis_ref[0] = start_ref[...]
    for b in range(BX * BY):
        place = lane_of(b // BY, b % BY)
        feats = feats_ref[b]
        for step, values in enumerate((one, two, three)):
            basis_ref[step + 1, b : b + 1, :] = jnp.sum(feats * values[:, place : place + 1], axis=0, keepdims=True)
    reg = reg_ref[...]
    basis = [basis_ref[0]]
    for step in range(1, 4):
        basis.append(basis_ref[step] + reg * basis[-1])
        basis_ref[step] = basis[-1]

    def folded(x, combine):
        rows = [x[8 * k : 8 * k + 8, :] for k in range(x.shape[0] // 8)]
        parts = [r[:, LANES * k : LANES * (k + 1)] for r in rows for k in range(x.shape[1] // LANES)]
        while len(parts) > 1:
            parts = [combine(parts[k], parts[k + 1]) for k in range(0, len(parts), 2)]
        return parts[0]

    peaks = [jnp.max(folded(jnp.abs(v), jnp.maximum), axis=0, keepdims=True) for v in basis]
    peaks = jnp.max(jnp.concatenate(peaks + peaks, axis=0), axis=1, keepdims=True)
    scale, inverse = power_of_two(jnp.broadcast_to(peaks, (8, LANES)))
    scaled = [v * inverse[k : k + 1, 0:1] for k, v in enumerate(basis)]
    sums = [jnp.sum(folded(scaled[a] * scaled[b], jnp.add), axis=0, keepdims=True) for a, b in PAIRS]
    sums = jnp.concatenate(sums + [jnp.zeros((16 - len(PAIRS), LANES), jnp.float32)], axis=0)
    sums = jnp.sum(sums, axis=1, keepdims=True)
    row = jnp.zeros((1, LANES), jnp.float32)
    for k in range(len(PAIRS)):
        row = jnp.where(lane == k, sums[k : k + 1, :], row)
    for k in range(4):
        row = jnp.where(lane == 10 + k, scale[k : k + 1, :], row)
        row = jnp.where(lane == 14 + k, inverse[k : k + 1, :], row)
    message_ref[...] = jnp.broadcast_to(row, message_ref.shape)


def krylov(moment_lanes, vectors, start, edges, first, second, masks, voxel_feats, voxel_reg, devices):
    bricks, _, voxels = voxel_feats.shape
    return pl.pallas_call(
        krylov_kernel,
        out_shape=(
            jax.ShapeDtypeStruct((4, bricks, voxels), jnp.float32),
            jax.ShapeDtypeStruct((devices, LANES), jnp.float32),
        ),
        scratch_shapes=[
            pltpu.VMEM((SPAN, LANES), jnp.float32),
            pltpu.VMEM((LANES, 8, LANES), jnp.float32),
            pltpu.VMEM((LANES, LANES), jnp.float32),
            pltpu.VMEM((8 * LANES, LANES), jnp.float32),
        ],
        compiler_params=pltpu.CompilerParams(vmem_limit_bytes=12 << 20),
        name="krylov",
    )(moment_lanes, vectors, start, *edges, first, second, masks, voxel_feats, voxel_reg)


def finish_kernel(shared_ref, basis_ref, solution_ref, residual_ref):
    shared = shared_ref[...]
    lane = lax.broadcasted_iota(jnp.int32, (1, LANES), 1)

    def pick(row, k):
        return jnp.sum(jnp.where(lane == k, row, 0.0), axis=1, keepdims=True)

    largest = jnp.max(shared, axis=0, keepdims=True)
    smallest = jnp.min(shared, axis=0, keepdims=True)
    scale = [pick(largest, 10 + k) for k in range(4)]
    inverse = [pick(smallest, 14 + k) for k in range(4)]
    weight = [shared[:, 10 + k : 11 + k] * inverse[k] for k in range(4)]
    left = jnp.zeros_like(shared)
    right = jnp.zeros_like(shared)
    for k, (a, b) in enumerate(PAIRS):
        left = jnp.where(lane == k, weight[a], left)
        right = jnp.where(lane == k, weight[b], right)
    total = jnp.sum(shared * left * right, axis=0, keepdims=True)
    gram = [[None] * 4 for _ in range(4)]
    for k, (a, b) in enumerate(PAIRS):
        gram[a][b] = gram[b][a] = pick(total, k)
    growth = [scale[k + 1] * inverse[k] for k in range(3)]

    def product(left, right):
        terms = [
            left[a] * right[b] * gram[a][b]
            for a in range(4)
            for b in range(4)
            if left[a] is not None and right[b] is not None
        ]
        return functools.reduce(jnp.add, terms)

    def plus(left, factor, right):
        out = []
        for a, b in zip(left, right):
            out.append(a if b is None else factor * b if a is None else a + factor * b)
        return out

    def image(vector):
        return [None] + [None if vector[k] is None else vector[k] * growth[k] for k in range(3)]

    solution = [None] * 4
    residual = [jnp.ones((1, 1), jnp.float32), None, None, None]
    direction = list(residual)
    norm_now = product(residual, residual)
    for iteration in range(ITERS):
        carried = image(direction)
        alpha = norm_now / product(direction, carried)
        solution = plus(solution, alpha, direction)
        residual = plus(residual, -alpha, carried)
        if iteration + 1 < ITERS:
            norm_next = product(residual, residual)
            direction = plus(residual, norm_next / norm_now, direction)
            norm_now = norm_next
    back = [scale[0] * inverse[k] for k in range(4)]
    for out_ref, coefficients in ((solution_ref, solution), (residual_ref, residual)):
        total = None
        for k, c in enumerate(coefficients):
            if c is not None:
                term = (c * back[k]) * basis_ref[k]
                total = term if total is None else total + term
        out_ref[...] = total


def finish(shared, basis):
    _, bricks, voxels = basis.shape
    out = jax.ShapeDtypeStruct((bricks, voxels), jnp.float32)
    return pl.pallas_call(
        finish_kernel,
        out_shape=(out, out),
        compiler_params=pltpu.CompilerParams(vmem_limit_bytes=4 << 20),
        name="finish",
    )(shared, basis)


def shards(point_feats, point_targets, point_lists, brick_adjacency, voxel_feats, voxel_reg):
    feat_count = point_feats.shape[0]
    brick_total, slots = point_lists.shape
    local_bricks = voxel_feats.shape[0]
    devices = brick_total // local_bricks
    sending = pack(point_feats, point_targets, point_lists, devices)
    got = lax.all_to_all(sending, GX_GY, split_axis=0, concat_axis=0, tiled=True)

    first, second, third = prepare(voxel_feats, voxel_reg)
    mask = (brick_adjacency >= 0).astype(jnp.float32)
    mask = jnp.concatenate([mask, jnp.sum(mask, axis=1, keepdims=True)], axis=1)
    mask = jnp.pad(mask, ((0, 0), (0, LANES - 5)))
    early = (first, second, mask)
    along_even = lax.axis_index("gx_2") == 0
    across_even = lax.axis_index("gy") % 2 == 0
    early_low, early_high = swap(*along_messages(EARLY, early), GX, along_even)
    early_below, early_above = swap(*across_early(early), "gy", across_even)

    moments, vectors, gathered, to_low, to_high = find_moments(got, (first, second, third))
    low, high = swap(to_low, to_high, GX, along_even)
    first_lanes, second_lanes, mask_lanes, moment_lanes, start = gather_early(
        first, second, mask, (early_low, early_high, early_below, early_above),
        moments, (low, high), gathered, voxel_feats,
    )
    below, above = swap(
        *across_late(moments, vectors, low, high, early_low, early_high), "gy", across_even
    )
    basis, message = krylov(
        moment_lanes, vectors, start, (low, high, below, above), first_lanes, second_lanes, mask_lanes,
        voxel_feats, voxel_reg, devices,
    )
    shared = lax.all_to_all(message, GX_GY, split_axis=0, concat_axis=0, tiled=True)
    return finish(shared, basis)


def solution(mesh):
    torus = Mesh(mesh.devices.reshape(4, 4, 2, mesh.shape["gy"]), ("gx_0", "gx_1", "gx_2", "gy"))
    return jax.shard_map(
        shards,
        mesh=torus,
        in_specs=(
            P(None, GX_GY),
            P(GX_GY),
            P(GX_GY, None),
            P(GX_GY, None),
            P(GX_GY, None, None),
            P(GX_GY, None),
        ),
        out_specs=(P(GX_GY, None), P(GX_GY, None)),
        check_vma=False,
    )
```

```python
import functools

import jax
import jax.numpy as jnp
from jax import lax
from jax.experimental import pallas as pl
from jax.experimental.pallas import tpu as pltpu
from jax.sharding import Mesh
from jax.sharding import PartitionSpec as P

BX = 8
BY = 4
ITERS = 3
SLOTS = 8
LANES = 128
FEAT = 32
PITCH = 16
SPAN = 256
REACH = 3
GX_GY = ("gx_0", "gx_1", "gx_2", "gy")
GX = ("gx_0", "gx_1", "gx_2")
HIGHEST = lax.Precision.HIGHEST
PAIRS = tuple((a, b) for a in range(4) for b in range(a, 4))


coupling_weight = 1.0

EARLY = ((8, 2, False), (8, 1, False), (1, 2, False))
LATE = ((8, 1, True), (1, 3, True))
CORNER_ROWS = 24


def padded(rows):
    return (rows + 7) // 8 * 8


def along_rows(section):
    return padded(section[0] * section[1] * BY)


def beyond(section, away):
    return section[1] - away if section[2] else 0


def across_rows(section):
    rows, depth, _ = section
    return padded(rows * sum(BX + 2 * beyond(section, k) for k in range(1, depth + 1)))


def message_rows(sections, size):
    return sum(size(section) for section in sections)


def piece(ref, start, rows, index):
    if rows == 8 and len(ref.shape) == 3:
        return ref[index]
    return ref[start + rows * index : start + rows * (index + 1), :]


def brick_at(own, low, high, start, section, a, e):
    rows, depth, _ = section
    if a < 0:
        return piece(low, start, rows, (a + depth) * BY + e)
    if a >= BX:
        return piece(high, start, rows, (a - BX) * BY + e)
    return piece(own, 0, rows, a * BY + e)


def fill_across(sections, owns, low, high, to_low, to_high):
    source = target = 0
    for section, own in zip(sections, owns):
        rows, depth, _ = section
        index = 0
        for away in range(1, depth + 1):
            extra = beyond(section, away)
            for a in range(-extra, BX + extra):
                place = slice(target + rows * index, target + rows * (index + 1))
                to_low[place, :] = brick_at(own, low, high, source, section, a, away - 1)
                to_high[place, :] = brick_at(own, low, high, source, section, a, BY - away)
                index += 1
        used, whole = rows * index, across_rows(section)
        if used < whole:
            blank = jnp.zeros((whole - used, LANES), jnp.float32)
            to_low[target + used : target + whole, :] = blank
            to_high[target + used : target + whole, :] = blank
        source += along_rows(section)
        target += whole


def place_bricks(put, sections, which, own, along_low, along_high, across_low, across_high):
    section = sections[which]
    rows, depth, _ = section
    start = message_rows(sections[:which], along_rows)
    for a in range(-depth, BX + depth):
        for e in range(BY):
            put(a, e, brick_at(own, along_low, along_high, start, section, a, e))
    start = message_rows(sections[:which], across_rows)
    index = 0
    for away in range(1, depth + 1):
        extra = beyond(section, away)
        for a in range(-extra, BX + extra):
            put(a, -away, piece(across_low, start, rows, index))
            put(a, BY - 1 + away, piece(across_high, start, rows, index))
            index += 1


def lane_of(a, e):
    return (a + REACH) * PITCH + e + REACH


def to_lanes(records, lanes_ref):
    for t in range(8):
        lanes_ref[t * LANES : (t + 1) * LANES, :] = records[:, t, :].T


def times(matrix_ref, vector):
    total = None
    for t in range(8):
        for q in range(4):
            i = 8 * q + t
            row = t * LANES + q * FEAT
            term = matrix_ref[row : row + FEAT, :] * vector[i : i + 1, :]
            total = term if total is None else total + term
    return total


def pack_kernel(
    lists_hbm, feats_ref, targets_hbm, out_ref, lists_ref, feats, targets_ref, packed, arrived, left, small
):
    steps = arrived.shape[0]
    lists_copy = pltpu.make_async_copy(lists_hbm, lists_ref, small.at[0])
    targets_copy = pltpu.make_async_copy(targets_hbm, targets_ref, small.at[1])
    lists_copy.start()
    targets_copy.start()
    devices = out_ref.shape[0]
    bricks = lists_ref.shape[1]
    dests = devices // steps
    width = LANES * SLOTS
    points = bricks * SLOTS // steps
    arriving = [
        pltpu.make_async_copy(
            feats_ref.at[:, k * points : (k + 1) * points], feats.at[:, k * points : (k + 1) * points], arrived.at[k]
        )
        for k in range(steps)
    ]
    leaving = [
        pltpu.make_async_copy(
            packed.at[k * dests : (k + 1) * dests], out_ref.at[k * dests : (k + 1) * dests], left.at[k]
        )
        for k in range(steps)
    ]
    for copy in arriving:
        copy.start()
    lists_copy.wait()
    rows = bricks // LANES
    lane = lax.broadcasted_iota(jnp.int32, (SLOTS, LANES), 1)
    codes = []
    for block in range(rows):
        chosen = lists_ref[:, block * LANES : (block + 1) * LANES]
        offset = chosen - (lane + block * LANES) * SLOTS
        bits = jnp.where(chosen >= 0, lax.shift_left(1, jnp.clip(offset, 0, SLOTS - 1)), 0)
        codes.append(jnp.sum(bits, axis=0, keepdims=True))
    code = jnp.concatenate(codes, axis=0).astype(jnp.float32).astype(jnp.bfloat16)
    brick = lax.broadcasted_iota(jnp.int32, (LANES, width), 0)
    point = lax.broadcasted_iota(jnp.int32, (LANES, width), 1)
    spread = (lax.shift_right_logical(point, 3) == brick).astype(jnp.float32).astype(jnp.bfloat16)
    wide = jnp.dot(code, spread, preferred_element_type=jnp.float32).astype(jnp.int32)
    slot = lax.broadcasted_iota(jnp.int32, (rows, width), 1) & (SLOTS - 1)
    mask = (lax.shift_right_logical(wide, slot) & 1).astype(jnp.float32)
    targets_copy.wait()
    for k in range(steps):
        arriving[k].wait()
        for part in range(points // width):
            first = k * points + part * width
            row = mask[first // width : first // width + 1, :].astype(jnp.bfloat16)
            masked = feats[:, first : first + width] * row
            for piece_index in range(width // LANES):
                dest = (first + piece_index * LANES) // (2 * LANES)
                half = piece_index % 2
                packed[dest, half * FEAT : (half + 1) * FEAT, :] = masked[
                    :, piece_index * LANES : (piece_index + 1) * LANES
                ]
        for dest in range(k * dests, (k + 1) * dests):
            packed[dest, 2 * FEAT : 2 * FEAT + 2, :] = targets_ref[2 * dest : 2 * dest + 2, :]
        leaving[k].start()
    for copy in leaving:
        copy.wait()


def pack(point_feats, point_targets, point_lists, devices):
    points = point_feats.shape[1]
    steps = 8
    rows = 2 * FEAT + 2
    return pl.pallas_call(
        pack_kernel,
        in_specs=[
            pl.BlockSpec(memory_space=pl.ANY),
            pl.BlockSpec(memory_space=pl.ANY),
            pl.BlockSpec(memory_space=pl.ANY),
        ],
        out_specs=pl.BlockSpec(memory_space=pl.ANY),
        out_shape=jax.ShapeDtypeStruct((devices, rows, LANES), jnp.bfloat16),
        scratch_shapes=[
            pltpu.VMEM(point_lists.shape[::-1], jnp.int32),
            pltpu.VMEM((FEAT, points), jnp.bfloat16),
            pltpu.VMEM((points // LANES, LANES), jnp.bfloat16),
            pltpu.VMEM((devices, rows, LANES), jnp.bfloat16),
            pltpu.SemaphoreType.DMA((steps,)),
            pltpu.SemaphoreType.DMA((steps,)),
            pltpu.SemaphoreType.DMA((2,)),
        ],
        name="pack",
    )(point_lists.T, point_feats, point_targets.reshape(points // LANES, LANES))


def spread_rows(square, lane_group):
    square = square + pltpu.roll(square, 64, 1)
    square = square + pltpu.roll(square, 32, 1)
    record = square[0:8, :]
    for q in range(1, 4):
        record = jnp.where(lane_group == q, square[8 * q : 8 * q + 8, :], record)
    return record


def three_parts(x):
    high = x.astype(jnp.bfloat16)
    rest = x - high.astype(jnp.float32)
    middle = rest.astype(jnp.bfloat16)
    return high, middle, (rest - middle.astype(jnp.float32)).astype(jnp.bfloat16)


def prepare_kernel(feats_ref, reg_ref, *records):

    lane_group = lax.broadcasted_iota(jnp.int32, (1, LANES), 1) // FEAT
    together = 4

    def some(step, carry):
        for k in range(together):
            b = step * together + k
            feats = feats_ref[b]
            reg = reg_ref[pl.ds(b, 1), :]
            once = feats * reg
            parts = three_parts(jnp.concatenate([feats, once, once * reg], axis=0))
            left = jnp.concatenate(parts, axis=0)
            right = [part[:FEAT, :] for part in parts]
            right = jnp.concatenate([*right, jnp.zeros_like(right[0])], axis=0)
            product = lax.dot_general(
                left, right, (((1,), (1,)), ((), ())), preferred_element_type=jnp.float32
            )
            size = 3 * FEAT
            total = jnp.where(lane_group < 1, product[2 * size :, :], 0.0)
            total = total + jnp.where(lane_group < 2, product[size : 2 * size, :], 0.0)
            total = total + product[:size, :]
            for power, record in enumerate(records):
                record[b] = spread_rows(total[power * FEAT : (power + 1) * FEAT, :], lane_group)
        return carry

    lax.fori_loop(0, feats_ref.shape[0] // together, some, 0)


def prepare(voxel_feats, voxel_reg):
    bricks = voxel_feats.shape[0]
    record = jax.ShapeDtypeStruct((bricks, 8, LANES), jnp.float32)
    return pl.pallas_call(
        prepare_kernel,
        out_shape=(record, record, record),
        compiler_params=pltpu.CompilerParams(vmem_limit_bytes=10 << 20),
        cost_estimate=pl.CostEstimate(flops=600_000_000, bytes_accessed=5_000_000, transcendentals=0),
        name="prepare",
    )(voxel_feats, voxel_reg)


def gather_early_kernel(
    first_ref, second_ref, mask_ref, low_ref, high_ref, below_ref, above_ref, moments_ref, late_low, late_high,
    first_lanes, second_lanes, mask_lanes, moment_lanes,
    first_store, second_store, mask_store, moment_store,
):
    for store in (first_store, second_store, mask_store, moment_store):
        store[...] = jnp.zeros_like(store)
    for a in range(-1, BX + 1):
        for e in range(BY):
            moment_store[lane_of(a, e)] = brick_at(moments_ref, late_low, late_high, 0, LATE[0], a, e)
    to_lanes(moment_store, moment_lanes)

    def put(store):
        def write(a, e, value):
            if len(store.shape) == 3:
                store[lane_of(a, e)] = value
            else:
                store[lane_of(a, e) : lane_of(a, e) + 1, :] = value

        return write

    edges = (low_ref, high_ref, below_ref, above_ref)
    place_bricks(put(first_store), EARLY, 0, first_ref, *edges)
    place_bricks(put(second_store), EARLY, 1, second_ref, *edges)
    place_bricks(put(mask_store), EARLY, 2, mask_ref, *edges)
    to_lanes(first_store, first_lanes)
    to_lanes(second_store, second_lanes)
    mask_lanes[...] = mask_store[...].T[:8, :]


def gather_early(first, second, mask, edges, moments, late):
    lanes = jax.ShapeDtypeStruct((8 * LANES, SPAN), jnp.float32)
    store = pltpu.VMEM((SPAN, 8, LANES), jnp.float32)
    return pl.pallas_call(
        gather_early_kernel,
        out_shape=(
            lanes,
            lanes,
            jax.ShapeDtypeStruct((8, SPAN), jnp.float32),
            lanes,
        ),
        scratch_shapes=[store, store, pltpu.VMEM((SPAN, LANES), jnp.float32), store],
        compiler_params=pltpu.CompilerParams(vmem_limit_bytes=8 << 20),
        cost_estimate=pl.CostEstimate(flops=3_000_000, bytes_accessed=5_000_000, transcendentals=0),
        name="gather_early",
    )(first, second, mask, *edges, moments, *late)


def across_early_kernel(first_ref, second_ref, mask_ref, to_low, to_high):
    fill_across(EARLY, (first_ref, second_ref, mask_ref), None, None, to_low, to_high)


def across_early(owns):
    out = jax.ShapeDtypeStruct((message_rows(EARLY, across_rows), LANES), jnp.float32)
    return pl.pallas_call(
        across_early_kernel,
        out_shape=(out, out),
        compiler_params=pltpu.CompilerParams(vmem_limit_bytes=4 << 20),
        name="across_early",
    )(*owns)


def across_late_kernel(moments_ref, vectors_ref, low, high, early_low, early_high, to_low, to_high):
    fill_across(LATE, (moments_ref, vectors_ref), low, high, to_low, to_high)
    start = message_rows(LATE, across_rows)
    masks = message_rows(EARLY[:2], along_rows)
    for out, e in ((to_low, 0), (to_high, BY - 1)):
        rows = []
        for k, (source, index) in enumerate(((early_low, BY + e), (early_high, e))):
            out[start + 8 * k : start + 8 * k + 8, :] = source[8 * index : 8 * index + 8, :]
            rows.append(source[masks + index : masks + index + 1, :])
        rows.append(jnp.zeros((6, LANES), jnp.float32))
        out[start + 16 : start + CORNER_ROWS, :] = jnp.concatenate(rows, axis=0)


def across_late(moments, vectors, low, high, early_low, early_high):
    out = jax.ShapeDtypeStruct((message_rows(LATE, across_rows) + CORNER_ROWS, LANES), jnp.float32)
    return pl.pallas_call(
        across_late_kernel,
        out_shape=(out, out),
        compiler_params=pltpu.CompilerParams(vmem_limit_bytes=4 << 20),
        name="across_late",
    )(moments, vectors, low, high, early_low, early_high)


def along_messages(sections, owns):
    to_low, to_high = [], []
    for (rows, depth, _), own in zip(sections, owns):
        flat = own.reshape(-1, LANES)
        used = rows * depth * BY
        blank = ((0, padded(used) - used), (0, 0))
        to_low.append(jnp.pad(flat[:used], blank))
        to_high.append(jnp.pad(flat[flat.shape[0] - used :], blank))
    return jnp.concatenate(to_low), jnp.concatenate(to_high)


def swap(to_low, to_high, axis, even):
    count = lax.axis_size(axis)

    def pairs(start):
        return [pair for a in range(start, count - 1, 2) for pair in ((a, a + 1), (a + 1, a))]

    second = lax.ppermute(jnp.where(even, to_low, to_high), axis, pairs(1))
    first = lax.ppermute(jnp.where(even, to_high, to_low), axis, pairs(0))
    return jnp.where(even, second, first), jnp.where(even, first, second)


def moments_kernel(
    got_ref, first_ref, second_ref, third_ref, moments_ref, vectors_ref, gathered_ref, low_ref, high_ref,
    turned, lanes_ref, moment_lanes,
):
    for t in range(8):
        block = [record[:, t, :] for record in (first_ref, second_ref, third_ref)]
        block = jnp.concatenate([*block, jnp.zeros((BX * BY, LANES), jnp.float32)], axis=0)
        lanes_ref[t * LANES : (t + 1) * LANES, :] = block.T
    sources = got_ref.shape[0]
    for group in range(sources // 4):
        for half in range(2):
            block = got_ref[4 * group : 4 * group + 4, half * FEAT : (half + 1) * FEAT, :]
            turned[half, group] = block.astype(jnp.float32).reshape(LANES, LANES).T
    sums = []
    for half in range(2):
        total = jnp.zeros((FEAT, LANES), jnp.float32)
        for source in range(sources):
            feats = got_ref[source, half * FEAT : (half + 1) * FEAT, :].astype(jnp.float32)
            target = got_ref[source, 2 * FEAT : 2 * FEAT + 2, :].astype(jnp.float32)
            total = total + feats * target[half : half + 1, :]
        sums.append(total)

    groups = turned.shape[1]
    lane_group = lax.broadcasted_iota(jnp.int32, (1, LANES), 1) // FEAT
    for half in range(2):
        for pair in range(8):
            for k in range(2):
                b = 2 * pair + k
                points = turned[half, :, 8 * b : 8 * b + 8, :].reshape(groups * 8, LANES)
                square = lax.dot_general(
                    points.T.astype(jnp.bfloat16),
                    points.astype(jnp.bfloat16),
                    (((1,), (0,)), ((), ())),
                    preferred_element_type=jnp.float32,
                )
                own = jnp.zeros((FEAT, LANES), jnp.float32)
                for q in range(4):
                    own = own + jnp.where(lane_group == q, square[q * FEAT : (q + 1) * FEAT, :], 0.0)
                moments_ref[half * 16 + b] = spread_rows(own, lane_group)
    point = lax.broadcasted_iota(jnp.int32, (LANES, LANES), 0) // SLOTS
    lane = lax.broadcasted_iota(jnp.int32, (LANES, LANES), 1)
    values = jnp.zeros((FEAT, LANES), jnp.float32)
    for half in range(2):
        spread = (lane % (BX * BY) == point + half * 16).astype(jnp.float32)
        values = values + jnp.dot(
            sums[half], spread, precision=HIGHEST, preferred_element_type=jnp.float32
        )
    gathered_ref[...] = values
    values = times(lanes_ref, values)
    for t in range(8):
        block = [moments_ref[:, t, :], jnp.zeros((LANES - BX * BY, LANES), jnp.float32)]
        moment_lanes[t * LANES : (t + 1) * LANES, :] = jnp.concatenate(block, axis=0).T
    values = jnp.where(lane_group == 3, pltpu.roll(times(moment_lanes, values), 96, 1), values)
    values = jnp.concatenate([values, jnp.zeros((LANES - FEAT, LANES), jnp.float32)], axis=0).T
    bricks = BX * BY
    vectors = jnp.concatenate([values[k * bricks : (k + 1) * bricks, :FEAT] for k in range(4)], axis=1)
    vectors_ref[...] = vectors
    depth = LATE[0][1] * BY
    for k in range(depth):
        low_ref[8 * k : 8 * k + 8, :] = moments_ref[k]
        high_ref[8 * k : 8 * k + 8, :] = moments_ref[BX * BY - depth + k]
    deep = LATE[1][1] * BY
    blank = jnp.zeros((padded(deep) - deep, LANES), jnp.float32)
    low_ref[8 * depth :, :] = jnp.concatenate([vectors[:deep], blank], axis=0)
    high_ref[8 * depth :, :] = jnp.concatenate([vectors[BX * BY - deep : BX * BY], blank], axis=0)


def find_moments(got, records):
    devices = got.shape[0]
    bricks = BX * BY
    message = jax.ShapeDtypeStruct((message_rows(LATE, along_rows), LANES), jnp.float32)
    return pl.pallas_call(
        moments_kernel,
        out_shape=(
            jax.ShapeDtypeStruct((bricks, 8, LANES), jnp.float32),
            jax.ShapeDtypeStruct((bricks, LANES), jnp.float32),
            jax.ShapeDtypeStruct((FEAT, LANES), jnp.float32),
            message,
            message,
        ),
        scratch_shapes=[
            pltpu.VMEM((2, devices // 4, LANES, LANES), jnp.float32),
            pltpu.VMEM((8 * LANES, LANES), jnp.float32),
            pltpu.VMEM((8 * LANES, LANES), jnp.float32),
        ],
        compiler_params=pltpu.CompilerParams(vmem_limit_bytes=12 << 20),
        cost_estimate=pl.CostEstimate(flops=1_000_000_000, bytes_accessed=12_000_000, transcendentals=0),
        name="moments",
    )(got, *records)


def power_of_two(value):
    scale = jnp.ones_like(value)
    inverse = jnp.ones_like(value)
    for k in (64, 32, 16, 8, 4, 2, 1):
        up, down = 2.0**k, 2.0**-k
        large = value * down >= 1.0
        small = value * up <= 1.0
        value = jnp.where(large, value * down, jnp.where(small, value * up, value))
        scale = jnp.where(large, scale * up, jnp.where(small, scale * down, scale))
        inverse = jnp.where(large, inverse * down, jnp.where(small, inverse * up, inverse))
    return scale, inverse


def krylov_kernel(
    moment_lanes, vectors_ref, gathered_ref, low_ref, high_ref, below_ref, above_ref, first_ref, second_ref, mask_ref,
    feats_ref, reg_ref, basis_ref, message_ref, vector_store, corner_store, corner_masks, corner_lanes,
):
    corner_store[...] = jnp.zeros_like(corner_store)
    corner_masks[...] = jnp.zeros_like(corner_masks)
    vector_store[...] = jnp.zeros_like(vector_store)

    def put_vector(a, e, value):
        vector_store[lane_of(a, e) : lane_of(a, e) + 1, :] = value

    edges = (low_ref, high_ref, below_ref, above_ref)
    place_bricks(put_vector, LATE, 1, vectors_ref, *edges)
    start = message_rows(LATE, across_rows)
    for ref, e in ((below_ref, -1), (above_ref, BY)):
        for k, a in enumerate((-1, BX)):
            place = lane_of(a, e) % LANES
            corner_store[(lane_of(a, e) + 8) % LANES] = ref[start + 8 * k : start + 8 * k + 8, :]
            corner_masks[place : place + 1, :] = ref[start + 16 + k : start + 17 + k, :]
        for a in range(BX):
            corner_store[lane_of(a, e) % LANES] = piece(ref, 0, 8, a)
    to_lanes(corner_store, corner_lanes)
    vectors = vector_store[...].T
    lane = lax.broadcasted_iota(jnp.int32, (1, LANES), 1)
    front = (lane == lane_of(-1, -1)) | (lane == lane_of(-1, BY))
    rear = (lane == lane_of(BX, -1) % LANES) | (lane == lane_of(BX, BY) % LANES)

    column = lane % PITCH
    beside = (column == REACH - 1) | (column == REACH + BY)
    beside_front = beside & (lane >= lane_of(0, -1))
    beside_rear = beside & (lane < lane_of(0, -1) - 8)

    def both_tiles(x):
        return jnp.concatenate([jnp.where(front, x, 0.0), jnp.where(rear, x, 0.0)], axis=1)

    def beside_times(z):
        x = times(corner_lanes, jnp.where(beside_front, z[:, :LANES], z[:, LANES:]))
        return jnp.concatenate([jnp.where(beside_front, x, 0.0), jnp.where(beside_rear, x, 0.0)], axis=1)

    masks = mask_ref[...] + both_tiles(corner_masks[...].T[:8, :])

    def coupled(z):
        near = masks[0:1] * pltpu.roll(z, PITCH, 1) + masks[1:2] * pltpu.roll(z, SPAN - PITCH, 1)
        near = near + masks[2:3] * pltpu.roll(z, 1, 1) + masks[3:4] * pltpu.roll(z, SPAN - 1, 1)
        return coupling_weight * (masks[4:5] * z - near)

    def system(z):
        return times(moment_lanes, z) + coupled(z)

    one = vectors[3 * FEAT :] + coupled(vectors[0:FEAT])
    corners = pltpu.roll(jnp.where(front, one[:, :LANES], one[:, LANES:]), 8, 1)
    corners = pltpu.roll(times(corner_lanes, corners), LANES - 8, 1)
    second_z = times(first_ref, one) + both_tiles(corners) + vectors[FEAT : 2 * FEAT]
    two = system(second_z) + beside_times(second_z)
    three = system(times(first_ref, two) + times(second_ref, one) + vectors[2 * FEAT : 3 * FEAT])
    gathered = gathered_ref[...]
    for b in range(BX * BY):
        place = lane_of(b // BY, b % BY)
        feats = feats_ref[b]
        columns = [gathered[:, b : b + 1]] + [values[:, place : place + 1] for values in (one, two, three)]
        for step, column in enumerate(columns):
            basis_ref[step, b : b + 1, :] = jnp.sum(feats * column, axis=0, keepdims=True)
    reg = reg_ref[...]
    basis = [basis_ref[0]]
    for step in range(1, 4):
        basis.append(basis_ref[step] + reg * basis[-1])
        basis_ref[step] = basis[-1]

    def folded(x, combine):
        rows = [x[8 * k : 8 * k + 8, :] for k in range(x.shape[0] // 8)]
        parts = [r[:, LANES * k : LANES * (k + 1)] for r in rows for k in range(x.shape[1] // LANES)]
        while len(parts) > 1:
            parts = [combine(parts[k], parts[k + 1]) for k in range(0, len(parts), 2)]
        return parts[0]

    peaks = [jnp.max(folded(jnp.abs(v), jnp.maximum), axis=0, keepdims=True) for v in basis]
    peaks = jnp.max(jnp.concatenate(peaks + peaks, axis=0), axis=1, keepdims=True)
    scale, inverse = power_of_two(jnp.broadcast_to(peaks, (8, LANES)))
    scaled = [v * inverse[k : k + 1, 0:1] for k, v in enumerate(basis)]
    sums = [jnp.sum(folded(scaled[a] * scaled[b], jnp.add), axis=0, keepdims=True) for a, b in PAIRS]
    sums = jnp.concatenate(sums + [jnp.zeros((16 - len(PAIRS), LANES), jnp.float32)], axis=0)
    sums = jnp.sum(sums, axis=1, keepdims=True)
    row = jnp.zeros((1, LANES), jnp.float32)
    for k in range(len(PAIRS)):
        row = jnp.where(lane == k, sums[k : k + 1, :], row)
    for k in range(4):
        row = jnp.where(lane == 10 + k, scale[k : k + 1, :], row)
        row = jnp.where(lane == 14 + k, inverse[k : k + 1, :], row)
    message_ref[...] = jnp.broadcast_to(row, message_ref.shape)


def krylov(moment_lanes, vectors, gathered, edges, first, second, masks, voxel_feats, voxel_reg, devices):
    bricks, _, voxels = voxel_feats.shape
    return pl.pallas_call(
        krylov_kernel,
        out_shape=(
            jax.ShapeDtypeStruct((4, bricks, voxels), jnp.float32),
            jax.ShapeDtypeStruct((devices, LANES), jnp.float32),
        ),
        scratch_shapes=[
            pltpu.VMEM((SPAN, LANES), jnp.float32),
            pltpu.VMEM((LANES, 8, LANES), jnp.float32),
            pltpu.VMEM((LANES, LANES), jnp.float32),
            pltpu.VMEM((8 * LANES, LANES), jnp.float32),
        ],
        compiler_params=pltpu.CompilerParams(vmem_limit_bytes=8 << 20),
        name="krylov",
    )(moment_lanes, vectors, gathered, *edges, first, second, masks, voxel_feats, voxel_reg)


def finish_kernel(shared_ref, basis_ref, solution_ref, residual_ref):
    shared = shared_ref[...]
    lane = lax.broadcasted_iota(jnp.int32, (1, LANES), 1)

    def pick(row, k):
        return jnp.sum(jnp.where(lane == k, row, 0.0), axis=1, keepdims=True)

    largest = jnp.max(shared, axis=0, keepdims=True)
    smallest = jnp.min(shared, axis=0, keepdims=True)
    scale = [pick(largest, 10 + k) for k in range(4)]
    inverse = [pick(smallest, 14 + k) for k in range(4)]
    weight = [shared[:, 10 + k : 11 + k] * inverse[k] for k in range(4)]
    left = jnp.zeros_like(shared)
    right = jnp.zeros_like(shared)
    for k, (a, b) in enumerate(PAIRS):
        left = jnp.where(lane == k, weight[a], left)
        right = jnp.where(lane == k, weight[b], right)
    total = jnp.sum(shared * left * right, axis=0, keepdims=True)
    gram = [[None] * 4 for _ in range(4)]
    for k, (a, b) in enumerate(PAIRS):
        gram[a][b] = gram[b][a] = pick(total, k)
    growth = [scale[k + 1] * inverse[k] for k in range(3)]

    def product(left, right):
        terms = [
            left[a] * right[b] * gram[a][b]
            for a in range(4)
            for b in range(4)
            if left[a] is not None and right[b] is not None
        ]
        return functools.reduce(jnp.add, terms)

    def plus(left, factor, right):
        out = []
        for a, b in zip(left, right):
            out.append(a if b is None else factor * b if a is None else a + factor * b)
        return out

    def image(vector):
        return [None] + [None if vector[k] is None else vector[k] * growth[k] for k in range(3)]

    solution = [None] * 4
    residual = [jnp.ones((1, 1), jnp.float32), None, None, None]
    direction = list(residual)
    norm_now = product(residual, residual)
    for iteration in range(ITERS):
        carried = image(direction)
        alpha = norm_now / product(direction, carried)
        solution = plus(solution, alpha, direction)
        residual = plus(residual, -alpha, carried)
        if iteration + 1 < ITERS:
            norm_next = product(residual, residual)
            direction = plus(residual, norm_next / norm_now, direction)
            norm_now = norm_next
    back = [scale[0] * inverse[k] for k in range(4)]
    for out_ref, coefficients in ((solution_ref, solution), (residual_ref, residual)):
        total = None
        for k, c in enumerate(coefficients):
            if c is not None:
                term = (c * back[k]) * basis_ref[k]
                total = term if total is None else total + term
        out_ref[...] = total


def finish(shared, basis):
    _, bricks, voxels = basis.shape
    out = jax.ShapeDtypeStruct((bricks, voxels), jnp.float32)
    return pl.pallas_call(
        finish_kernel,
        out_shape=(out, out),
        compiler_params=pltpu.CompilerParams(vmem_limit_bytes=4 << 20),
        name="finish",
    )(shared, basis)


def shards(point_feats, point_targets, point_lists, brick_adjacency, voxel_feats, voxel_reg):
    feat_count = point_feats.shape[0]
    brick_total, slots = point_lists.shape
    local_bricks = voxel_feats.shape[0]
    devices = brick_total // local_bricks
    sending = pack(point_feats, point_targets, point_lists, devices)
    got = lax.all_to_all(sending, GX_GY, split_axis=0, concat_axis=0, tiled=True)

    first, second, third = prepare(voxel_feats, voxel_reg)
    mask = (brick_adjacency >= 0).astype(jnp.float32)
    mask = jnp.concatenate([mask, jnp.sum(mask, axis=1, keepdims=True)], axis=1)
    mask = jnp.pad(mask, ((0, 0), (0, LANES - 5)))
    early = (first, second, mask)
    along_even = lax.axis_index("gx_2") == 0
    across_even = lax.axis_index("gy") % 2 == 0
    early_low, early_high = swap(*along_messages(EARLY, early), GX, along_even)
    early_below, early_above = swap(*across_early(early), "gy", across_even)

    moments, vectors, gathered, to_low, to_high = find_moments(got, (first, second, third))
    low, high = swap(to_low, to_high, GX, along_even)
    first_lanes, second_lanes, mask_lanes, moment_lanes = gather_early(
        first, second, mask, (early_low, early_high, early_below, early_above),
        moments, (low, high),
    )
    below, above = swap(
        *across_late(moments, vectors, low, high, early_low, early_high), "gy", across_even
    )
    basis, message = krylov(
        moment_lanes, vectors, gathered, (low, high, below, above), first_lanes, second_lanes, mask_lanes,
        voxel_feats, voxel_reg, devices,
    )
    shared = lax.all_to_all(message, GX_GY, split_axis=0, concat_axis=0, tiled=True)
    return finish(shared, basis)


def solution(mesh):
    torus = Mesh(mesh.devices.reshape(4, 4, 2, mesh.shape["gy"]), ("gx_0", "gx_1", "gx_2", "gy"))
    return jax.shard_map(
        shards,
        mesh=torus,
        in_specs=(
            P(None, GX_GY),
            P(GX_GY),
            P(GX_GY, None),
            P(GX_GY, None),
            P(GX_GY, None, None),
            P(GX_GY, None),
        ),
        out_specs=(P(GX_GY, None), P(GX_GY, None)),
        check_vma=False,
    )
```

```python
import functools

import jax
import jax.numpy as jnp
from jax import lax
from jax.experimental import pallas as pl
from jax.experimental.pallas import tpu as pltpu
from jax.sharding import Mesh
from jax.sharding import PartitionSpec as P

BX = 8
BY = 4
ITERS = 3
SLOTS = 8
LANES = 128
FEAT = 32
PITCH = 16
SPAN = 256
REACH = 3
GX_GY = ("gx_0", "gx_1", "gx_2", "gy")
GX = ("gx_0", "gx_1", "gx_2")
HIGHEST = lax.Precision.HIGHEST
PAIRS = tuple((a, b) for a in range(4) for b in range(a, 4))


coupling_weight = 1.0

EARLY = ((8, 2, False), (8, 1, False), (1, 2, False))
LATE = ((8, 1, True), (1, 3, True))
CORNER_ROWS = 24


def padded(rows):
    return (rows + 7) // 8 * 8


def along_rows(section):
    return padded(section[0] * section[1] * BY)


def beyond(section, away):
    return section[1] - away if section[2] else 0


def across_rows(section):
    rows, depth, _ = section
    return padded(rows * sum(BX + 2 * beyond(section, k) for k in range(1, depth + 1)))


def message_rows(sections, size):
    return sum(size(section) for section in sections)


def piece(ref, start, rows, index):
    if rows == 8 and len(ref.shape) == 3:
        return ref[index]
    return ref[start + rows * index : start + rows * (index + 1), :]


def brick_at(own, low, high, start, section, a, e):
    rows, depth, _ = section
    if a < 0:
        return piece(low, start, rows, (a + depth) * BY + e)
    if a >= BX:
        return piece(high, start, rows, (a - BX) * BY + e)
    return piece(own, 0, rows, a * BY + e)


def fill_across(sections, owns, low, high, to_low, to_high):
    source = target = 0
    for section, own in zip(sections, owns):
        rows, depth, _ = section
        index = 0
        for away in range(1, depth + 1):
            extra = beyond(section, away)
            for a in range(-extra, BX + extra):
                place = slice(target + rows * index, target + rows * (index + 1))
                to_low[place, :] = brick_at(own, low, high, source, section, a, away - 1)
                to_high[place, :] = brick_at(own, low, high, source, section, a, BY - away)
                index += 1
        used, whole = rows * index, across_rows(section)
        if used < whole:
            blank = jnp.zeros((whole - used, LANES), jnp.float32)
            to_low[target + used : target + whole, :] = blank
            to_high[target + used : target + whole, :] = blank
        source += along_rows(section)
        target += whole


def place_bricks(put, sections, which, own, along_low, along_high, across_low, across_high):
    section = sections[which]
    rows, depth, _ = section
    start = message_rows(sections[:which], along_rows)
    for a in range(-depth, BX + depth):
        for e in range(BY):
            put(a, e, brick_at(own, along_low, along_high, start, section, a, e))
    start = message_rows(sections[:which], across_rows)
    index = 0
    for away in range(1, depth + 1):
        extra = beyond(section, away)
        for a in range(-extra, BX + extra):
            put(a, -away, piece(across_low, start, rows, index))
            put(a, BY - 1 + away, piece(across_high, start, rows, index))
            index += 1


def lane_of(a, e):
    return (a + REACH) * PITCH + e + REACH


def to_lanes(records, lanes_ref):
    for t in range(8):
        lanes_ref[t * LANES : (t + 1) * LANES, :] = records[:, t, :].T


def times(matrix_ref, vector):
    total = None
    for t in range(8):
        for q in range(4):
            i = 8 * q + t
            row = t * LANES + q * FEAT
            term = matrix_ref[row : row + FEAT, :] * vector[i : i + 1, :]
            total = term if total is None else total + term
    return total


def pack_kernel(
    lists_hbm, feats_ref, targets_hbm, out_ref, lists_ref, feats, targets_ref, packed, arrived, left, small
):
    steps = arrived.shape[0]
    lists_copy = pltpu.make_async_copy(lists_hbm, lists_ref, small.at[0])
    targets_copy = pltpu.make_async_copy(targets_hbm, targets_ref, small.at[1])
    lists_copy.start()
    targets_copy.start()
    devices = out_ref.shape[0]
    bricks = lists_ref.shape[1]
    dests = devices // steps
    width = LANES * SLOTS
    points = bricks * SLOTS // steps
    arriving = [
        pltpu.make_async_copy(
            feats_ref.at[:, k * points : (k + 1) * points], feats.at[:, k * points : (k + 1) * points], arrived.at[k]
        )
        for k in range(steps)
    ]
    leaving = [
        pltpu.make_async_copy(
            packed.at[k * dests : (k + 1) * dests], out_ref.at[k * dests : (k + 1) * dests], left.at[k]
        )
        for k in range(steps)
    ]
    for copy in arriving:
        copy.start()
    lists_copy.wait()
    rows = bricks // LANES
    lane = lax.broadcasted_iota(jnp.int32, (SLOTS, LANES), 1)
    codes = []
    for block in range(rows):
        chosen = lists_ref[:, block * LANES : (block + 1) * LANES]
        offset = chosen - (lane + block * LANES) * SLOTS
        bits = jnp.where(chosen >= 0, lax.shift_left(1, jnp.clip(offset, 0, SLOTS - 1)), 0)
        codes.append(jnp.sum(bits, axis=0, keepdims=True))
    code = jnp.concatenate(codes, axis=0).astype(jnp.float32).astype(jnp.bfloat16)
    brick = lax.broadcasted_iota(jnp.int32, (LANES, width), 0)
    point = lax.broadcasted_iota(jnp.int32, (LANES, width), 1)
    spread = (lax.shift_right_logical(point, 3) == brick).astype(jnp.float32).astype(jnp.bfloat16)
    wide = jnp.dot(code, spread, preferred_element_type=jnp.float32).astype(jnp.int32)
    slot = lax.broadcasted_iota(jnp.int32, (rows, width), 1) & (SLOTS - 1)
    mask = (lax.shift_right_logical(wide, slot) & 1).astype(jnp.float32)
    targets_copy.wait()
    for k in range(steps):
        arriving[k].wait()
        for part in range(points // width):
            first = k * points + part * width
            row = mask[first // width : first // width + 1, :].astype(jnp.bfloat16)
            masked = feats[:, first : first + width] * row
            for piece_index in range(width // LANES):
                dest = (first + piece_index * LANES) // (2 * LANES)
                half = piece_index % 2
                packed[dest, half * FEAT : (half + 1) * FEAT, :] = masked[
                    :, piece_index * LANES : (piece_index + 1) * LANES
                ]
        for dest in range(k * dests, (k + 1) * dests):
            packed[dest, 2 * FEAT : 2 * FEAT + 2, :] = targets_ref[2 * dest : 2 * dest + 2, :]
        leaving[k].start()
    for copy in leaving:
        copy.wait()


def pack(point_feats, point_targets, point_lists, devices):
    points = point_feats.shape[1]
    steps = 8
    rows = 2 * FEAT + 2
    return pl.pallas_call(
        pack_kernel,
        in_specs=[
            pl.BlockSpec(memory_space=pl.ANY),
            pl.BlockSpec(memory_space=pl.ANY),
            pl.BlockSpec(memory_space=pl.ANY),
        ],
        out_specs=pl.BlockSpec(memory_space=pl.ANY),
        out_shape=jax.ShapeDtypeStruct((devices, rows, LANES), jnp.bfloat16),
        scratch_shapes=[
            pltpu.VMEM(point_lists.shape[::-1], jnp.int32),
            pltpu.VMEM((FEAT, points), jnp.bfloat16),
            pltpu.VMEM((points // LANES, LANES), jnp.bfloat16),
            pltpu.VMEM((devices, rows, LANES), jnp.bfloat16),
            pltpu.SemaphoreType.DMA((steps,)),
            pltpu.SemaphoreType.DMA((steps,)),
            pltpu.SemaphoreType.DMA((2,)),
        ],
        name="pack",
    )(point_lists.T, point_feats, point_targets.reshape(points // LANES, LANES))


def spread_rows(square, lane_group):
    square = square + pltpu.roll(square, 64, 1)
    square = square + pltpu.roll(square, 32, 1)
    record = square[0:8, :]
    for q in range(1, 4):
        record = jnp.where(lane_group == q, square[8 * q : 8 * q + 8, :], record)
    return record


def three_parts(x):
    high = x.astype(jnp.bfloat16)
    rest = x - high.astype(jnp.float32)
    middle = rest.astype(jnp.bfloat16)
    return high, middle, (rest - middle.astype(jnp.float32)).astype(jnp.bfloat16)


def prepare_kernel(feats_ref, reg_ref, *records):

    lane_group = lax.broadcasted_iota(jnp.int32, (1, LANES), 1) // FEAT
    together = 4

    def some(step, carry):
        for k in range(together):
            b = step * together + k
            feats = feats_ref[b]
            reg = reg_ref[pl.ds(b, 1), :]
            once = feats * reg
            parts = three_parts(jnp.concatenate([feats, once, once * reg], axis=0))
            left = jnp.concatenate(parts, axis=0)
            right = [part[:FEAT, :] for part in parts]
            right = jnp.concatenate([*right, jnp.zeros_like(right[0])], axis=0)
            product = lax.dot_general(
                left, right, (((1,), (1,)), ((), ())), preferred_element_type=jnp.float32
            )
            size = 3 * FEAT
            total = jnp.where(lane_group < 1, product[2 * size :, :], 0.0)
            total = total + jnp.where(lane_group < 2, product[size : 2 * size, :], 0.0)
            total = total + product[:size, :]
            for power, record in enumerate(records):
                record[b] = spread_rows(total[power * FEAT : (power + 1) * FEAT, :], lane_group)
        return carry

    lax.fori_loop(0, feats_ref.shape[0] // together, some, 0)


def prepare(voxel_feats, voxel_reg):
    bricks = voxel_feats.shape[0]
    record = jax.ShapeDtypeStruct((bricks, 8, LANES), jnp.float32)
    return pl.pallas_call(
        prepare_kernel,
        out_shape=(record, record, record),
        compiler_params=pltpu.CompilerParams(vmem_limit_bytes=10 << 20),
        cost_estimate=pl.CostEstimate(flops=600_000_000, bytes_accessed=5_000_000, transcendentals=0),
        name="prepare",
    )(voxel_feats, voxel_reg)


def gather_early_kernel(
    first_ref, second_ref, mask_ref, low_ref, high_ref, below_ref, above_ref, moments_ref, late_low, late_high,
    first_lanes, second_lanes, mask_lanes, moment_lanes,
    first_store, second_store, mask_store, moment_store,
):
    for store in (first_store, second_store, mask_store, moment_store):
        store[...] = jnp.zeros_like(store)
    for a in range(-1, BX + 1):
        for e in range(BY):
            moment_store[lane_of(a, e)] = brick_at(moments_ref, late_low, late_high, 0, LATE[0], a, e)
    to_lanes(moment_store, moment_lanes)

    def put(store):
        def write(a, e, value):
            if len(store.shape) == 3:
                store[lane_of(a, e)] = value
            else:
                store[lane_of(a, e) : lane_of(a, e) + 1, :] = value

        return write

    edges = (low_ref, high_ref, below_ref, above_ref)
    place_bricks(put(first_store), EARLY, 0, first_ref, *edges)
    place_bricks(put(second_store), EARLY, 1, second_ref, *edges)
    place_bricks(put(mask_store), EARLY, 2, mask_ref, *edges)
    to_lanes(first_store, first_lanes)
    to_lanes(second_store, second_lanes)
    mask_lanes[...] = mask_store[...].T[:8, :]


def gather_early(first, second, mask, edges, moments, late):
    lanes = jax.ShapeDtypeStruct((8 * LANES, SPAN), jnp.float32)
    store = pltpu.VMEM((SPAN, 8, LANES), jnp.float32)
    return pl.pallas_call(
        gather_early_kernel,
        out_shape=(
            lanes,
            lanes,
            jax.ShapeDtypeStruct((8, SPAN), jnp.float32),
            lanes,
        ),
        scratch_shapes=[store, store, pltpu.VMEM((SPAN, LANES), jnp.float32), store],
        compiler_params=pltpu.CompilerParams(vmem_limit_bytes=8 << 20),
        cost_estimate=pl.CostEstimate(flops=3_000_000, bytes_accessed=5_000_000, transcendentals=0),
        name="gather_early",
    )(first, second, mask, *edges, moments, *late)


def across_early_kernel(first_ref, second_ref, mask_ref, to_low, to_high):
    fill_across(EARLY, (first_ref, second_ref, mask_ref), None, None, to_low, to_high)


def across_early(owns):
    out = jax.ShapeDtypeStruct((message_rows(EARLY, across_rows), LANES), jnp.float32)
    return pl.pallas_call(
        across_early_kernel,
        out_shape=(out, out),
        compiler_params=pltpu.CompilerParams(vmem_limit_bytes=4 << 20),
        name="across_early",
    )(*owns)


def across_late_kernel(moments_ref, vectors_ref, low, high, early_low, early_high, to_low, to_high):
    fill_across(LATE, (moments_ref, vectors_ref), low, high, to_low, to_high)
    start = message_rows(LATE, across_rows)
    masks = message_rows(EARLY[:2], along_rows)
    for out, e in ((to_low, 0), (to_high, BY - 1)):
        rows = []
        for k, (source, index) in enumerate(((early_low, BY + e), (early_high, e))):
            out[start + 8 * k : start + 8 * k + 8, :] = source[8 * index : 8 * index + 8, :]
            rows.append(source[masks + index : masks + index + 1, :])
        rows.append(jnp.zeros((6, LANES), jnp.float32))
        out[start + 16 : start + CORNER_ROWS, :] = jnp.concatenate(rows, axis=0)


def across_late(moments, vectors, low, high, early_low, early_high):
    out = jax.ShapeDtypeStruct((message_rows(LATE, across_rows) + CORNER_ROWS, LANES), jnp.float32)
    return pl.pallas_call(
        across_late_kernel,
        out_shape=(out, out),
        compiler_params=pltpu.CompilerParams(vmem_limit_bytes=4 << 20),
        name="across_late",
    )(moments, vectors, low, high, early_low, early_high)


def along_messages(sections, owns):
    to_low, to_high = [], []
    for (rows, depth, _), own in zip(sections, owns):
        flat = own.reshape(-1, LANES)
        used = rows * depth * BY
        blank = ((0, padded(used) - used), (0, 0))
        to_low.append(jnp.pad(flat[:used], blank))
        to_high.append(jnp.pad(flat[flat.shape[0] - used :], blank))
    return jnp.concatenate(to_low), jnp.concatenate(to_high)


def swap(to_low, to_high, axis, even):
    count = lax.axis_size(axis)

    def pairs(start):
        return [pair for a in range(start, count - 1, 2) for pair in ((a, a + 1), (a + 1, a))]

    if axis != GX:
        odd = jnp.logical_not(even)
        second = lax.ppermute(jnp.where(odd, to_high, to_low), axis, pairs(1))
        first = lax.ppermute(jnp.where(odd, to_low, to_high), axis, pairs(0))
        return jnp.where(odd, first, second), jnp.where(odd, second, first)
    second = lax.ppermute(jnp.where(even, to_low, to_high), axis, pairs(1))
    first = lax.ppermute(jnp.where(even, to_high, to_low), axis, pairs(0))
    return jnp.where(even, second, first), jnp.where(even, first, second)


def moments_kernel(
    got_ref, first_ref, second_ref, third_ref, moments_ref, vectors_ref, gathered_ref, low_ref, high_ref,
    turned, lanes_ref, moment_lanes,
):
    for t in range(8):
        block = [record[:, t, :] for record in (first_ref, second_ref, third_ref)]
        block = jnp.concatenate([*block, jnp.zeros((BX * BY, LANES), jnp.float32)], axis=0)
        lanes_ref[t * LANES : (t + 1) * LANES, :] = block.T
    sources = got_ref.shape[0]
    for group in range(sources // 4):
        for half in range(2):
            block = got_ref[4 * group : 4 * group + 4, half * FEAT : (half + 1) * FEAT, :]
            turned[half, group] = block.astype(jnp.float32).reshape(LANES, LANES).T
    sums = []
    for half in range(2):
        total = jnp.zeros((FEAT, LANES), jnp.float32)
        for source in range(sources):
            feats = got_ref[source, half * FEAT : (half + 1) * FEAT, :].astype(jnp.float32)
            target = got_ref[source, 2 * FEAT : 2 * FEAT + 2, :].astype(jnp.float32)
            total = total + feats * target[half : half + 1, :]
        sums.append(total)

    groups = turned.shape[1]
    lane_group = lax.broadcasted_iota(jnp.int32, (1, LANES), 1) // FEAT
    for half in range(2):
        for pair in range(8):
            for k in range(2):
                b = 2 * pair + k
                points = turned[half, :, 8 * b : 8 * b + 8, :].reshape(groups * 8, LANES)
                square = lax.dot_general(
                    points.T.astype(jnp.bfloat16),
                    points.astype(jnp.bfloat16),
                    (((1,), (0,)), ((), ())),
                    preferred_element_type=jnp.float32,
                )
                own = jnp.zeros((FEAT, LANES), jnp.float32)
                for q in range(4):
                    own = own + jnp.where(lane_group == q, square[q * FEAT : (q + 1) * FEAT, :], 0.0)
                moments_ref[half * 16 + b] = spread_rows(own, lane_group)
    point = lax.broadcasted_iota(jnp.int32, (LANES, LANES), 0) // SLOTS
    lane = lax.broadcasted_iota(jnp.int32, (LANES, LANES), 1)
    values = jnp.zeros((FEAT, LANES), jnp.float32)
    for half in range(2):
        spread = (lane % (BX * BY) == point + half * 16).astype(jnp.float32)
        values = values + jnp.dot(
            sums[half], spread, precision=HIGHEST, preferred_element_type=jnp.float32
        )
    gathered_ref[...] = values
    values = times(lanes_ref, values)
    for t in range(8):
        block = [moments_ref[:, t, :], jnp.zeros((LANES - BX * BY, LANES), jnp.float32)]
        moment_lanes[t * LANES : (t + 1) * LANES, :] = jnp.concatenate(block, axis=0).T
    values = jnp.where(lane_group == 3, pltpu.roll(times(moment_lanes, values), 96, 1), values)
    values = jnp.concatenate([values, jnp.zeros((LANES - FEAT, LANES), jnp.float32)], axis=0).T
    bricks = BX * BY
    vectors = jnp.concatenate([values[k * bricks : (k + 1) * bricks, :FEAT] for k in range(4)], axis=1)
    vectors_ref[...] = vectors
    depth = LATE[0][1] * BY
    for k in range(depth):
        low_ref[8 * k : 8 * k + 8, :] = moments_ref[k]
        high_ref[8 * k : 8 * k + 8, :] = moments_ref[BX * BY - depth + k]
    deep = LATE[1][1] * BY
    blank = jnp.zeros((padded(deep) - deep, LANES), jnp.float32)
    low_ref[8 * depth :, :] = jnp.concatenate([vectors[:deep], blank], axis=0)
    high_ref[8 * depth :, :] = jnp.concatenate([vectors[BX * BY - deep : BX * BY], blank], axis=0)


def find_moments(got, records):
    devices = got.shape[0]
    bricks = BX * BY
    message = jax.ShapeDtypeStruct((message_rows(LATE, along_rows), LANES), jnp.float32)
    return pl.pallas_call(
        moments_kernel,
        out_shape=(
            jax.ShapeDtypeStruct((bricks, 8, LANES), jnp.float32),
            jax.ShapeDtypeStruct((bricks, LANES), jnp.float32),
            jax.ShapeDtypeStruct((FEAT, LANES), jnp.float32),
            message,
            message,
        ),
        scratch_shapes=[
            pltpu.VMEM((2, devices // 4, LANES, LANES), jnp.float32),
            pltpu.VMEM((8 * LANES, LANES), jnp.float32),
            pltpu.VMEM((8 * LANES, LANES), jnp.float32),
        ],
        compiler_params=pltpu.CompilerParams(vmem_limit_bytes=12 << 20),
        cost_estimate=pl.CostEstimate(flops=1_000_000_000, bytes_accessed=12_000_000, transcendentals=0),
        name="moments",
    )(got, *records)


def power_of_two(value):
    scale = jnp.ones_like(value)
    inverse = jnp.ones_like(value)
    for k in (64, 32, 16, 8, 4, 2, 1):
        up, down = 2.0**k, 2.0**-k
        large = value * down >= 1.0
        small = value * up <= 1.0
        value = jnp.where(large, value * down, jnp.where(small, value * up, value))
        scale = jnp.where(large, scale * up, jnp.where(small, scale * down, scale))
        inverse = jnp.where(large, inverse * down, jnp.where(small, inverse * up, inverse))
    return scale, inverse


def krylov_kernel(
    moment_lanes, vectors_ref, gathered_ref, low_ref, high_ref, below_ref, above_ref, first_ref, second_ref, mask_ref,
    feats_ref, reg_ref, basis_ref, message_ref, vector_store, corner_store, corner_masks, corner_lanes,
):
    corner_store[...] = jnp.zeros_like(corner_store)
    corner_masks[...] = jnp.zeros_like(corner_masks)
    vector_store[...] = jnp.zeros_like(vector_store)

    def put_vector(a, e, value):
        vector_store[lane_of(a, e) : lane_of(a, e) + 1, :] = value

    edges = (low_ref, high_ref, below_ref, above_ref)
    place_bricks(put_vector, LATE, 1, vectors_ref, *edges)
    start = message_rows(LATE, across_rows)
    for ref, e in ((below_ref, -1), (above_ref, BY)):
        for k, a in enumerate((-1, BX)):
            place = lane_of(a, e) % LANES
            corner_store[(lane_of(a, e) + 8) % LANES] = ref[start + 8 * k : start + 8 * k + 8, :]
            corner_masks[place : place + 1, :] = ref[start + 16 + k : start + 17 + k, :]
        for a in range(BX):
            corner_store[lane_of(a, e) % LANES] = piece(ref, 0, 8, a)
    to_lanes(corner_store, corner_lanes)
    vectors = vector_store[...].T
    lane = lax.broadcasted_iota(jnp.int32, (1, LANES), 1)
    front = (lane == lane_of(-1, -1)) | (lane == lane_of(-1, BY))
    rear = (lane == lane_of(BX, -1) % LANES) | (lane == lane_of(BX, BY) % LANES)

    column = lane % PITCH
    beside = (column == REACH - 1) | (column == REACH + BY)
    beside_front = beside & (lane >= lane_of(0, -1))
    beside_rear = beside & (lane < lane_of(0, -1) - 8)

    def both_tiles(x):
        return jnp.concatenate([jnp.where(front, x, 0.0), jnp.where(rear, x, 0.0)], axis=1)

    def beside_times(z):
        x = times(corner_lanes, jnp.where(beside_front, z[:, :LANES], z[:, LANES:]))
        return jnp.concatenate([jnp.where(beside_front, x, 0.0), jnp.where(beside_rear, x, 0.0)], axis=1)

    masks = mask_ref[...] + both_tiles(corner_masks[...].T[:8, :])

    def coupled(z):
        near = masks[0:1] * pltpu.roll(z, PITCH, 1) + masks[1:2] * pltpu.roll(z, SPAN - PITCH, 1)
        near = near + masks[2:3] * pltpu.roll(z, 1, 1) + masks[3:4] * pltpu.roll(z, SPAN - 1, 1)
        return coupling_weight * (masks[4:5] * z - near)

    def system(z):
        return times(moment_lanes, z) + coupled(z)

    one = vectors[3 * FEAT :] + coupled(vectors[0:FEAT])
    corners = pltpu.roll(jnp.where(front, one[:, :LANES], one[:, LANES:]), 8, 1)
    corners = pltpu.roll(times(corner_lanes, corners), LANES - 8, 1)
    second_z = times(first_ref, one) + both_tiles(corners) + vectors[FEAT : 2 * FEAT]
    two = system(second_z) + beside_times(second_z)
    three = system(times(first_ref, two) + times(second_ref, one) + vectors[2 * FEAT : 3 * FEAT])
    gathered = gathered_ref[...]
    for b in range(BX * BY):
        place = lane_of(b // BY, b % BY)
        feats = feats_ref[b]
        columns = [gathered[:, b : b + 1]] + [values[:, place : place + 1] for values in (one, two, three)]
        for step, column in enumerate(columns):
            basis_ref[step, b : b + 1, :] = jnp.sum(feats * column, axis=0, keepdims=True)
    reg = reg_ref[...]
    basis = [basis_ref[0]]
    for step in range(1, 4):
        basis.append(basis_ref[step] + reg * basis[-1])
        basis_ref[step] = basis[-1]

    def folded(x, combine):
        rows = [x[8 * k : 8 * k + 8, :] for k in range(x.shape[0] // 8)]
        parts = [r[:, LANES * k : LANES * (k + 1)] for r in rows for k in range(x.shape[1] // LANES)]
        while len(parts) > 1:
            parts = [combine(parts[k], parts[k + 1]) for k in range(0, len(parts), 2)]
        return parts[0]

    peaks = [jnp.max(folded(jnp.abs(v), jnp.maximum), axis=0, keepdims=True) for v in basis]
    peaks = jnp.max(jnp.concatenate(peaks + peaks, axis=0), axis=1, keepdims=True)
    scale, inverse = power_of_two(jnp.broadcast_to(peaks, (8, LANES)))
    scaled = [v * inverse[k : k + 1, 0:1] for k, v in enumerate(basis)]
    sums = [jnp.sum(folded(scaled[a] * scaled[b], jnp.add), axis=0, keepdims=True) for a, b in PAIRS]
    sums = jnp.concatenate(sums + [jnp.zeros((16 - len(PAIRS), LANES), jnp.float32)], axis=0)
    sums = jnp.sum(sums, axis=1, keepdims=True)
    row = jnp.zeros((1, LANES), jnp.float32)
    for k in range(len(PAIRS)):
        row = jnp.where(lane == k, sums[k : k + 1, :], row)
    for k in range(4):
        row = jnp.where(lane == 10 + k, scale[k : k + 1, :], row)
        row = jnp.where(lane == 14 + k, inverse[k : k + 1, :], row)
    message_ref[...] = jnp.broadcast_to(row, message_ref.shape)


def krylov(moment_lanes, vectors, gathered, edges, first, second, masks, voxel_feats, voxel_reg, devices):
    bricks, _, voxels = voxel_feats.shape
    return pl.pallas_call(
        krylov_kernel,
        out_shape=(
            jax.ShapeDtypeStruct((4, bricks, voxels), jnp.float32),
            jax.ShapeDtypeStruct((devices, LANES), jnp.float32),
        ),
        scratch_shapes=[
            pltpu.VMEM((SPAN, LANES), jnp.float32),
            pltpu.VMEM((LANES, 8, LANES), jnp.float32),
            pltpu.VMEM((LANES, LANES), jnp.float32),
            pltpu.VMEM((8 * LANES, LANES), jnp.float32),
        ],
        compiler_params=pltpu.CompilerParams(vmem_limit_bytes=8 << 20),
        name="krylov",
    )(moment_lanes, vectors, gathered, *edges, first, second, masks, voxel_feats, voxel_reg)


def finish_kernel(shared_ref, basis_ref, solution_ref, residual_ref):
    shared = shared_ref[...]
    lane = lax.broadcasted_iota(jnp.int32, (1, LANES), 1)

    def pick(row, k):
        return jnp.sum(jnp.where(lane == k, row, 0.0), axis=1, keepdims=True)

    largest = jnp.max(shared, axis=0, keepdims=True)
    smallest = jnp.min(shared, axis=0, keepdims=True)
    scale = [pick(largest, 10 + k) for k in range(4)]
    inverse = [pick(smallest, 14 + k) for k in range(4)]
    weight = [shared[:, 10 + k : 11 + k] * inverse[k] for k in range(4)]
    left = jnp.zeros_like(shared)
    right = jnp.zeros_like(shared)
    for k, (a, b) in enumerate(PAIRS):
        left = jnp.where(lane == k, weight[a], left)
        right = jnp.where(lane == k, weight[b], right)
    total = jnp.sum(shared * left * right, axis=0, keepdims=True)
    gram = [[None] * 4 for _ in range(4)]
    for k, (a, b) in enumerate(PAIRS):
        gram[a][b] = gram[b][a] = pick(total, k)
    growth = [scale[k + 1] * inverse[k] for k in range(3)]

    def product(left, right):
        terms = [
            left[a] * right[b] * gram[a][b]
            for a in range(4)
            for b in range(4)
            if left[a] is not None and right[b] is not None
        ]
        return functools.reduce(jnp.add, terms)

    def plus(left, factor, right):
        out = []
        for a, b in zip(left, right):
            out.append(a if b is None else factor * b if a is None else a + factor * b)
        return out

    def image(vector):
        return [None] + [None if vector[k] is None else vector[k] * growth[k] for k in range(3)]

    solution = [None] * 4
    residual = [jnp.ones((1, 1), jnp.float32), None, None, None]
    direction = list(residual)
    norm_now = product(residual, residual)
    for iteration in range(ITERS):
        carried = image(direction)
        alpha = norm_now / product(direction, carried)
        solution = plus(solution, alpha, direction)
        residual = plus(residual, -alpha, carried)
        if iteration + 1 < ITERS:
            norm_next = product(residual, residual)
            direction = plus(residual, norm_next / norm_now, direction)
            norm_now = norm_next
    back = [scale[0] * inverse[k] for k in range(4)]
    for out_ref, coefficients in ((solution_ref, solution), (residual_ref, residual)):
        total = None
        for k, c in enumerate(coefficients):
            if c is not None:
                term = (c * back[k]) * basis_ref[k]
                total = term if total is None else total + term
        out_ref[...] = total


def finish(shared, basis):
    _, bricks, voxels = basis.shape
    out = jax.ShapeDtypeStruct((bricks, voxels), jnp.float32)
    return pl.pallas_call(
        finish_kernel,
        out_shape=(out, out),
        compiler_params=pltpu.CompilerParams(vmem_limit_bytes=4 << 20),
        name="finish",
    )(shared, basis)


def shards(point_feats, point_targets, point_lists, brick_adjacency, voxel_feats, voxel_reg):
    feat_count = point_feats.shape[0]
    brick_total, slots = point_lists.shape
    local_bricks = voxel_feats.shape[0]
    devices = brick_total // local_bricks
    sending = pack(point_feats, point_targets, point_lists, devices)
    got = lax.all_to_all(sending, GX_GY, split_axis=0, concat_axis=0, tiled=True)

    first, second, third = prepare(voxel_feats, voxel_reg)
    mask = (brick_adjacency >= 0).astype(jnp.float32)
    mask = jnp.concatenate([mask, jnp.sum(mask, axis=1, keepdims=True)], axis=1)
    mask = jnp.pad(mask, ((0, 0), (0, LANES - 5)))
    early = (first, second, mask)
    along_even = lax.axis_index("gx_2") == 0
    across_even = lax.axis_index("gy") % 2 == 0
    early_low, early_high = swap(*along_messages(EARLY, early), GX, along_even)
    early_below, early_above = swap(*across_early(early), "gy", across_even)

    moments, vectors, gathered, to_low, to_high = find_moments(got, (first, second, third))
    low, high = swap(to_low, to_high, GX, along_even)
    first_lanes, second_lanes, mask_lanes, moment_lanes = gather_early(
        first, second, mask, (early_low, early_high, early_below, early_above),
        moments, (low, high),
    )
    below, above = swap(
        *across_late(moments, vectors, low, high, early_low, early_high), "gy", across_even
    )
    basis, message = krylov(
        moment_lanes, vectors, gathered, (low, high, below, above), first_lanes, second_lanes, mask_lanes,
        voxel_feats, voxel_reg, devices,
    )
    shared = lax.all_to_all(message, GX_GY, split_axis=0, concat_axis=0, tiled=True)
    return finish(shared, basis)


def solution(mesh):
    torus = Mesh(mesh.devices.reshape(4, 4, 2, mesh.shape["gy"]), ("gx_0", "gx_1", "gx_2", "gy"))
    return jax.shard_map(
        shards,
        mesh=torus,
        in_specs=(
            P(None, GX_GY),
            P(GX_GY),
            P(GX_GY, None),
            P(GX_GY, None),
            P(GX_GY, None, None),
            P(GX_GY, None),
        ),
        out_specs=(P(GX_GY, None), P(GX_GY, None)),
        check_vma=False,
    )
```

```python
import functools

import jax
import jax.numpy as jnp
from jax import lax
from jax.experimental import pallas as pl
from jax.experimental.pallas import tpu as pltpu
from jax.sharding import Mesh
from jax.sharding import PartitionSpec as P

BX = 8
BY = 4
ITERS = 3
SLOTS = 8
LANES = 128
FEAT = 32
PITCH = 16
SPAN = 256
REACH = 3
GX_GY = ("gx_0", "gx_1", "gx_2", "gy")
GX = ("gx_0", "gx_1", "gx_2")
HIGHEST = lax.Precision.HIGHEST
PAIRS = tuple((a, b) for a in range(4) for b in range(a, 4))


coupling_weight = 1.0

EARLY = ((8, 2, False), (8, 1, False), (1, 2, False))
LATE = ((8, 1, True), (1, 3, True))
CORNER_ROWS = 24


def padded(rows):
    return (rows + 7) // 8 * 8


def along_rows(section):
    return padded(section[0] * section[1] * BY)


def beyond(section, away):
    return section[1] - away if section[2] else 0


def across_rows(section):
    rows, depth, _ = section
    return padded(rows * sum(BX + 2 * beyond(section, k) for k in range(1, depth + 1)))


def message_rows(sections, size):
    return sum(size(section) for section in sections)


def piece(ref, start, rows, index):
    if rows == 8 and len(ref.shape) == 3:
        return ref[index]
    return ref[start + rows * index : start + rows * (index + 1), :]


def brick_at(own, low, high, start, section, a, e):
    rows, depth, _ = section
    if a < 0:
        return piece(low, start, rows, (a + depth) * BY + e)
    if a >= BX:
        return piece(high, start, rows, (a - BX) * BY + e)
    return piece(own, 0, rows, a * BY + e)


def fill_across(sections, owns, low, high, to_low, to_high):
    source = target = 0
    for section, own in zip(sections, owns):
        rows, depth, _ = section
        index = 0
        for away in range(1, depth + 1):
            extra = beyond(section, away)
            for a in range(-extra, BX + extra):
                place = slice(target + rows * index, target + rows * (index + 1))
                to_low[place, :] = brick_at(own, low, high, source, section, a, away - 1)
                to_high[place, :] = brick_at(own, low, high, source, section, a, BY - away)
                index += 1
        used, whole = rows * index, across_rows(section)
        if used < whole:
            blank = jnp.zeros((whole - used, LANES), jnp.float32)
            to_low[target + used : target + whole, :] = blank
            to_high[target + used : target + whole, :] = blank
        source += along_rows(section)
        target += whole


def place_bricks(put, sections, which, own, along_low, along_high, across_low, across_high):
    section = sections[which]
    rows, depth, _ = section
    start = message_rows(sections[:which], along_rows)
    for a in range(-depth, BX + depth):
        for e in range(BY):
            put(a, e, brick_at(own, along_low, along_high, start, section, a, e))
    start = message_rows(sections[:which], across_rows)
    index = 0
    for away in range(1, depth + 1):
        extra = beyond(section, away)
        for a in range(-extra, BX + extra):
            put(a, -away, piece(across_low, start, rows, index))
            put(a, BY - 1 + away, piece(across_high, start, rows, index))
            index += 1


def lane_of(a, e):
    return (a + REACH) * PITCH + e + REACH


def to_lanes(records, lanes_ref):
    for t in range(8):
        lanes_ref[t * LANES : (t + 1) * LANES, :] = records[:, t, :].T


def times(matrix_ref, vector):
    total = None
    for t in range(8):
        for q in range(4):
            i = 8 * q + t
            row = t * LANES + q * FEAT
            term = matrix_ref[row : row + FEAT, :] * vector[i : i + 1, :]
            total = term if total is None else total + term
    return total


def pack_kernel(
    lists_hbm, feats_ref, targets_hbm, out_ref, lists_ref, feats, targets_ref, packed, arrived, left, small
):
    steps = arrived.shape[0]
    lists_copy = pltpu.make_async_copy(lists_hbm, lists_ref, small.at[0])
    targets_copy = pltpu.make_async_copy(targets_hbm, targets_ref, small.at[1])
    lists_copy.start()
    targets_copy.start()
    devices = out_ref.shape[0]
    bricks = lists_ref.shape[1]
    dests = devices // steps
    width = LANES * SLOTS
    points = bricks * SLOTS // steps
    arriving = [
        pltpu.make_async_copy(
            feats_ref.at[:, k * points : (k + 1) * points], feats.at[:, k * points : (k + 1) * points], arrived.at[k]
        )
        for k in range(steps)
    ]
    leaving = [
        pltpu.make_async_copy(
            packed.at[k * dests : (k + 1) * dests], out_ref.at[k * dests : (k + 1) * dests], left.at[k]
        )
        for k in range(steps)
    ]
    for copy in arriving:
        copy.start()
    lists_copy.wait()
    rows = bricks // LANES
    lane = lax.broadcasted_iota(jnp.int32, (SLOTS, LANES), 1)
    codes = []
    for block in range(rows):
        chosen = lists_ref[:, block * LANES : (block + 1) * LANES]
        offset = chosen - (lane + block * LANES) * SLOTS
        bits = jnp.where(chosen >= 0, lax.shift_left(1, jnp.clip(offset, 0, SLOTS - 1)), 0)
        codes.append(jnp.sum(bits, axis=0, keepdims=True))
    code = jnp.concatenate(codes, axis=0).astype(jnp.float32).astype(jnp.bfloat16)
    brick = lax.broadcasted_iota(jnp.int32, (LANES, width), 0)
    point = lax.broadcasted_iota(jnp.int32, (LANES, width), 1)
    spread = (lax.shift_right_logical(point, 3) == brick).astype(jnp.float32).astype(jnp.bfloat16)
    wide = jnp.dot(code, spread, preferred_element_type=jnp.float32).astype(jnp.int32)
    slot = lax.broadcasted_iota(jnp.int32, (rows, width), 1) & (SLOTS - 1)
    mask = (lax.shift_right_logical(wide, slot) & 1).astype(jnp.float32)
    targets_copy.wait()
    for k in range(steps):
        arriving[k].wait()
        for part in range(points // width):
            first = k * points + part * width
            row = mask[first // width : first // width + 1, :].astype(jnp.bfloat16)
            masked = feats[:, first : first + width] * row
            for piece_index in range(width // LANES):
                dest = (first + piece_index * LANES) // (2 * LANES)
                half = piece_index % 2
                packed[dest, half * FEAT : (half + 1) * FEAT, :] = masked[
                    :, piece_index * LANES : (piece_index + 1) * LANES
                ]
        for dest in range(k * dests, (k + 1) * dests):
            packed[dest, 2 * FEAT : 2 * FEAT + 2, :] = targets_ref[2 * dest : 2 * dest + 2, :]
        leaving[k].start()
    for copy in leaving:
        copy.wait()


def pack(point_feats, point_targets, point_lists, devices):
    points = point_feats.shape[1]
    steps = 8
    rows = 2 * FEAT + 2
    return pl.pallas_call(
        pack_kernel,
        in_specs=[
            pl.BlockSpec(memory_space=pl.ANY),
            pl.BlockSpec(memory_space=pl.ANY),
            pl.BlockSpec(memory_space=pl.ANY),
        ],
        out_specs=pl.BlockSpec(memory_space=pl.ANY),
        out_shape=jax.ShapeDtypeStruct((devices, rows, LANES), jnp.bfloat16),
        scratch_shapes=[
            pltpu.VMEM(point_lists.shape[::-1], jnp.int32),
            pltpu.VMEM((FEAT, points), jnp.bfloat16),
            pltpu.VMEM((points // LANES, LANES), jnp.bfloat16),
            pltpu.VMEM((devices, rows, LANES), jnp.bfloat16),
            pltpu.SemaphoreType.DMA((steps,)),
            pltpu.SemaphoreType.DMA((steps,)),
            pltpu.SemaphoreType.DMA((2,)),
        ],
        name="pack",
    )(point_lists.T, point_feats, point_targets.reshape(points // LANES, LANES))


def spread_rows(square, lane_group):
    square = square + pltpu.roll(square, 64, 1)
    square = square + pltpu.roll(square, 32, 1)
    record = square[0:8, :]
    for q in range(1, 4):
        record = jnp.where(lane_group == q, square[8 * q : 8 * q + 8, :], record)
    return record


def three_parts(x):
    high = x.astype(jnp.bfloat16)
    rest = x - high.astype(jnp.float32)
    middle = rest.astype(jnp.bfloat16)
    return high, middle, (rest - middle.astype(jnp.float32)).astype(jnp.bfloat16)


def prepare_kernel(feats_ref, reg_ref, *records):

    lane_group = lax.broadcasted_iota(jnp.int32, (1, LANES), 1) // FEAT
    together = 4

    def some(step, carry):
        for k in range(together):
            b = step * together + k
            feats = feats_ref[b]
            reg = reg_ref[pl.ds(b, 1), :]
            once = feats * reg
            parts = three_parts(jnp.concatenate([feats, once, once * reg], axis=0))
            left = jnp.concatenate(parts, axis=0)
            right = [part[:FEAT, :] for part in parts]
            right = jnp.concatenate([*right, jnp.zeros_like(right[0])], axis=0)
            product = lax.dot_general(
                left, right, (((1,), (1,)), ((), ())), preferred_element_type=jnp.float32
            )
            size = 3 * FEAT
            total = jnp.where(lane_group < 1, product[2 * size :, :], 0.0)
            total = total + jnp.where(lane_group < 2, product[size : 2 * size, :], 0.0)
            total = total + product[:size, :]
            for power, record in enumerate(records):
                record[b] = spread_rows(total[power * FEAT : (power + 1) * FEAT, :], lane_group)
        return carry

    lax.fori_loop(0, feats_ref.shape[0] // together, some, 0)


def prepare(voxel_feats, voxel_reg):
    bricks = voxel_feats.shape[0]
    record = jax.ShapeDtypeStruct((bricks, 8, LANES), jnp.float32)
    return pl.pallas_call(
        prepare_kernel,
        out_shape=(record, record, record),
        compiler_params=pltpu.CompilerParams(vmem_limit_bytes=10 << 20),
        cost_estimate=pl.CostEstimate(flops=600_000_000, bytes_accessed=5_000_000, transcendentals=0),
        name="prepare",
    )(voxel_feats, voxel_reg)


def gather_early_kernel(
    first_ref, second_ref, mask_ref, low_ref, high_ref, below_ref, above_ref, moments_ref, late_low, late_high,
    first_lanes, second_lanes, mask_lanes, moment_lanes,
    first_store, second_store, mask_store, moment_store,
):
    for store in (first_store, second_store, mask_store, moment_store):
        store[...] = jnp.zeros_like(store)
    for a in range(-1, BX + 1):
        for e in range(BY):
            moment_store[lane_of(a, e)] = brick_at(moments_ref, late_low, late_high, 0, LATE[0], a, e)
    to_lanes(moment_store, moment_lanes)

    def put(store):
        def write(a, e, value):
            if len(store.shape) == 3:
                store[lane_of(a, e)] = value
            else:
                store[lane_of(a, e) : lane_of(a, e) + 1, :] = value

        return write

    edges = (low_ref, high_ref, below_ref, above_ref)
    place_bricks(put(first_store), EARLY, 0, first_ref, *edges)
    place_bricks(put(second_store), EARLY, 1, second_ref, *edges)
    place_bricks(put(mask_store), EARLY, 2, mask_ref, *edges)
    to_lanes(first_store, first_lanes)
    to_lanes(second_store, second_lanes)
    mask_lanes[...] = mask_store[...].T[:8, :]


def gather_early(first, second, mask, edges, moments, late):
    lanes = jax.ShapeDtypeStruct((8 * LANES, SPAN), jnp.float32)
    store = pltpu.VMEM((SPAN, 8, LANES), jnp.float32)
    return pl.pallas_call(
        gather_early_kernel,
        out_shape=(
            lanes,
            lanes,
            jax.ShapeDtypeStruct((8, SPAN), jnp.float32),
            lanes,
        ),
        scratch_shapes=[store, store, pltpu.VMEM((SPAN, LANES), jnp.float32), store],
        compiler_params=pltpu.CompilerParams(vmem_limit_bytes=8 << 20),
        cost_estimate=pl.CostEstimate(flops=3_000_000, bytes_accessed=5_000_000, transcendentals=0),
        name="gather_early",
    )(first, second, mask, *edges, moments, *late)


def across_early_kernel(first_ref, second_ref, mask_ref, to_low, to_high):
    fill_across(EARLY, (first_ref, second_ref, mask_ref), None, None, to_low, to_high)


def across_early(owns):
    out = jax.ShapeDtypeStruct((message_rows(EARLY, across_rows), LANES), jnp.float32)
    return pl.pallas_call(
        across_early_kernel,
        out_shape=(out, out),
        compiler_params=pltpu.CompilerParams(vmem_limit_bytes=4 << 20),
        name="across_early",
    )(*owns)


def across_late_kernel(moments_ref, vectors_ref, low, high, early_low, early_high, to_low, to_high):
    fill_across(LATE, (moments_ref, vectors_ref), low, high, to_low, to_high)
    start = message_rows(LATE, across_rows)
    masks = message_rows(EARLY[:2], along_rows)
    for out, e in ((to_low, 0), (to_high, BY - 1)):
        rows = []
        for k, (source, index) in enumerate(((early_low, BY + e), (early_high, e))):
            out[start + 8 * k : start + 8 * k + 8, :] = source[8 * index : 8 * index + 8, :]
            rows.append(source[masks + index : masks + index + 1, :])
        rows.append(jnp.zeros((6, LANES), jnp.float32))
        out[start + 16 : start + CORNER_ROWS, :] = jnp.concatenate(rows, axis=0)


def across_late(moments, vectors, low, high, early_low, early_high):
    out = jax.ShapeDtypeStruct((message_rows(LATE, across_rows) + CORNER_ROWS, LANES), jnp.float32)
    return pl.pallas_call(
        across_late_kernel,
        out_shape=(out, out),
        compiler_params=pltpu.CompilerParams(vmem_limit_bytes=4 << 20),
        name="across_late",
    )(moments, vectors, low, high, early_low, early_high)


def along_messages(sections, owns):
    to_low, to_high = [], []
    for (rows, depth, _), own in zip(sections, owns):
        flat = own.reshape(-1, LANES)
        used = rows * depth * BY
        blank = ((0, padded(used) - used), (0, 0))
        to_low.append(jnp.pad(flat[:used], blank))
        to_high.append(jnp.pad(flat[flat.shape[0] - used :], blank))
    return jnp.concatenate(to_low), jnp.concatenate(to_high)


def swap(to_low, to_high, axis, even):
    count = lax.axis_size(axis)

    def pairs(start):
        return [pair for a in range(start, count - 1, 2) for pair in ((a, a + 1), (a + 1, a))]

    second = lax.ppermute(jnp.where(even, to_low, to_high), axis, pairs(1))
    first = lax.ppermute(jnp.where(even, to_high, to_low), axis, pairs(0))
    return jnp.where(even, second, first), jnp.where(even, first, second)


def moments_kernel(
    got_ref, first_ref, second_ref, third_ref, moments_ref, vectors_ref, gathered_ref, low_ref, high_ref,
    turned, lanes_ref, moment_lanes,
):
    for t in range(8):
        block = [record[:, t, :] for record in (first_ref, second_ref, third_ref)]
        block = jnp.concatenate([*block, jnp.zeros((BX * BY, LANES), jnp.float32)], axis=0)
        lanes_ref[t * LANES : (t + 1) * LANES, :] = block.T
    sources = got_ref.shape[0]
    for group in range(sources // 4):
        for half in range(2):
            block = got_ref[4 * group : 4 * group + 4, half * FEAT : (half + 1) * FEAT, :]
            turned[half, group] = block.astype(jnp.float32).reshape(LANES, LANES).T
    sums = []
    for half in range(2):
        total = jnp.zeros((FEAT, LANES), jnp.float32)
        for source in range(sources):
            feats = got_ref[source, half * FEAT : (half + 1) * FEAT, :].astype(jnp.float32)
            target = got_ref[source, 2 * FEAT : 2 * FEAT + 2, :].astype(jnp.float32)
            total = total + feats * target[half : half + 1, :]
        sums.append(total)

    groups = turned.shape[1]
    lane_group = lax.broadcasted_iota(jnp.int32, (1, LANES), 1) // FEAT
    for half in range(2):
        for pair in range(8):
            for k in range(2):
                b = 2 * pair + k
                points = turned[half, :, 8 * b : 8 * b + 8, :].reshape(groups * 8, LANES)
                square = lax.dot_general(
                    points.T.astype(jnp.bfloat16),
                    points.astype(jnp.bfloat16),
                    (((1,), (0,)), ((), ())),
                    preferred_element_type=jnp.float32,
                )
                own = jnp.zeros((FEAT, LANES), jnp.float32)
                for q in range(4):
                    own = own + jnp.where(lane_group == q, square[q * FEAT : (q + 1) * FEAT, :], 0.0)
                moments_ref[half * 16 + b] = spread_rows(own, lane_group)
    point = lax.broadcasted_iota(jnp.int32, (2 * LANES, LANES), 0) // SLOTS
    lane = lax.broadcasted_iota(jnp.int32, (2 * LANES, LANES), 1)
    spread = (lane % (BX * BY) == point).astype(jnp.float32)
    values = jnp.dot(
        jnp.concatenate(sums, axis=1), spread, precision=HIGHEST, preferred_element_type=jnp.float32
    )
    gathered_ref[...] = values
    values = times(lanes_ref, values)
    for t in range(8):
        block = [moments_ref[:, t, :], jnp.zeros((LANES - BX * BY, LANES), jnp.float32)]
        moment_lanes[t * LANES : (t + 1) * LANES, :] = jnp.concatenate(block, axis=0).T
    values = jnp.where(lane_group == 3, pltpu.roll(times(moment_lanes, values), 96, 1), values)
    values = jnp.concatenate([values, jnp.zeros((LANES - FEAT, LANES), jnp.float32)], axis=0).T
    bricks = BX * BY
    vectors = jnp.concatenate([values[k * bricks : (k + 1) * bricks, :FEAT] for k in range(4)], axis=1)
    vectors_ref[...] = vectors
    depth = LATE[0][1] * BY
    for k in range(depth):
        low_ref[8 * k : 8 * k + 8, :] = moments_ref[k]
        high_ref[8 * k : 8 * k + 8, :] = moments_ref[BX * BY - depth + k]
    deep = LATE[1][1] * BY
    blank = jnp.zeros((padded(deep) - deep, LANES), jnp.float32)
    low_ref[8 * depth :, :] = jnp.concatenate([vectors[:deep], blank], axis=0)
    high_ref[8 * depth :, :] = jnp.concatenate([vectors[BX * BY - deep : BX * BY], blank], axis=0)


def find_moments(got, records):
    devices = got.shape[0]
    bricks = BX * BY
    message = jax.ShapeDtypeStruct((message_rows(LATE, along_rows), LANES), jnp.float32)
    return pl.pallas_call(
        moments_kernel,
        out_shape=(
            jax.ShapeDtypeStruct((bricks, 8, LANES), jnp.float32),
            jax.ShapeDtypeStruct((bricks, LANES), jnp.float32),
            jax.ShapeDtypeStruct((FEAT, LANES), jnp.float32),
            message,
            message,
        ),
        scratch_shapes=[
            pltpu.VMEM((2, devices // 4, LANES, LANES), jnp.float32),
            pltpu.VMEM((8 * LANES, LANES), jnp.float32),
            pltpu.VMEM((8 * LANES, LANES), jnp.float32),
        ],
        compiler_params=pltpu.CompilerParams(vmem_limit_bytes=12 << 20),
        cost_estimate=pl.CostEstimate(flops=1_000_000_000, bytes_accessed=12_000_000, transcendentals=0),
        name="moments",
    )(got, *records)


def power_of_two(value):
    scale = jnp.ones_like(value)
    inverse = jnp.ones_like(value)
    for k in (64, 32, 16, 8, 4, 2, 1):
        up, down = 2.0**k, 2.0**-k
        large = value * down >= 1.0
        small = value * up <= 1.0
        value = jnp.where(large, value * down, jnp.where(small, value * up, value))
        scale = jnp.where(large, scale * up, jnp.where(small, scale * down, scale))
        inverse = jnp.where(large, inverse * down, jnp.where(small, inverse * up, inverse))
    return scale, inverse


def krylov_kernel(
    moment_lanes, vectors_ref, gathered_ref, low_ref, high_ref, below_ref, above_ref, first_ref, second_ref, mask_ref,
    feats_ref, reg_ref, basis_ref, message_ref, vector_store, corner_store, corner_masks, corner_lanes,
):
    corner_store[...] = jnp.zeros_like(corner_store)
    corner_masks[...] = jnp.zeros_like(corner_masks)
    vector_store[...] = jnp.zeros_like(vector_store)

    def put_vector(a, e, value):
        vector_store[lane_of(a, e) : lane_of(a, e) + 1, :] = value

    edges = (low_ref, high_ref, below_ref, above_ref)
    place_bricks(put_vector, LATE, 1, vectors_ref, *edges)
    start = message_rows(LATE, across_rows)
    for ref, e in ((below_ref, -1), (above_ref, BY)):
        for k, a in enumerate((-1, BX)):
            place = lane_of(a, e) % LANES
            corner_store[(lane_of(a, e) + 8) % LANES] = ref[start + 8 * k : start + 8 * k + 8, :]
            corner_masks[place : place + 1, :] = ref[start + 16 + k : start + 17 + k, :]
        for a in range(BX):
            corner_store[lane_of(a, e) % LANES] = piece(ref, 0, 8, a)
    to_lanes(corner_store, corner_lanes)
    vectors = vector_store[...].T
    lane = lax.broadcasted_iota(jnp.int32, (1, LANES), 1)
    front = (lane == lane_of(-1, -1)) | (lane == lane_of(-1, BY))
    rear = (lane == lane_of(BX, -1) % LANES) | (lane == lane_of(BX, BY) % LANES)

    column = lane % PITCH
    beside = (column == REACH - 1) | (column == REACH + BY)
    beside_front = beside & (lane >= lane_of(0, -1))
    beside_rear = beside & (lane < lane_of(0, -1) - 8)

    def both_tiles(x):
        return jnp.concatenate([jnp.where(front, x, 0.0), jnp.where(rear, x, 0.0)], axis=1)

    def beside_times(z):
        x = times(corner_lanes, jnp.where(beside_front, z[:, :LANES], z[:, LANES:]))
        return jnp.concatenate([jnp.where(beside_front, x, 0.0), jnp.where(beside_rear, x, 0.0)], axis=1)

    masks = mask_ref[...] + both_tiles(corner_masks[...].T[:8, :])

    def coupled(z):
        near = masks[0:1] * pltpu.roll(z, PITCH, 1) + masks[1:2] * pltpu.roll(z, SPAN - PITCH, 1)
        near = near + masks[2:3] * pltpu.roll(z, 1, 1) + masks[3:4] * pltpu.roll(z, SPAN - 1, 1)
        return coupling_weight * (masks[4:5] * z - near)

    def system(z):
        return times(moment_lanes, z) + coupled(z)

    one = vectors[3 * FEAT :] + coupled(vectors[0:FEAT])
    corners = pltpu.roll(jnp.where(front, one[:, :LANES], one[:, LANES:]), 8, 1)
    corners = pltpu.roll(times(corner_lanes, corners), LANES - 8, 1)
    second_z = times(first_ref, one) + both_tiles(corners) + vectors[FEAT : 2 * FEAT]
    two = system(second_z) + beside_times(second_z)
    three = system(times(first_ref, two) + times(second_ref, one) + vectors[2 * FEAT : 3 * FEAT])
    gathered = gathered_ref[...]
    for b in range(BX * BY):
        place = lane_of(b // BY, b % BY)
        feats = feats_ref[b]
        columns = [gathered[:, b : b + 1]] + [values[:, place : place + 1] for values in (one, two, three)]
        for step, column in enumerate(columns):
            basis_ref[step, b : b + 1, :] = jnp.sum(feats * column, axis=0, keepdims=True)
    reg = reg_ref[...]
    basis = [basis_ref[0]]
    for step in range(1, 4):
        basis.append(basis_ref[step] + reg * basis[-1])
        basis_ref[step] = basis[-1]

    def folded(x, combine):
        rows = [x[8 * k : 8 * k + 8, :] for k in range(x.shape[0] // 8)]
        parts = [r[:, LANES * k : LANES * (k + 1)] for r in rows for k in range(x.shape[1] // LANES)]
        while len(parts) > 1:
            parts = [combine(parts[k], parts[k + 1]) for k in range(0, len(parts), 2)]
        return parts[0]

    peaks = [jnp.max(folded(jnp.abs(v), jnp.maximum), axis=0, keepdims=True) for v in basis]
    peaks = jnp.max(jnp.concatenate(peaks + peaks, axis=0), axis=1, keepdims=True)
    scale, inverse = power_of_two(jnp.broadcast_to(peaks, (8, LANES)))
    scaled = [v * inverse[k : k + 1, 0:1] for k, v in enumerate(basis)]
    sums = [jnp.sum(folded(scaled[a] * scaled[b], jnp.add), axis=0, keepdims=True) for a, b in PAIRS]
    sums = jnp.concatenate(sums + [jnp.zeros((16 - len(PAIRS), LANES), jnp.float32)], axis=0)
    sums = jnp.sum(sums, axis=1, keepdims=True)
    row = jnp.zeros((1, LANES), jnp.float32)
    for k in range(len(PAIRS)):
        row = jnp.where(lane == k, sums[k : k + 1, :], row)
    for k in range(4):
        row = jnp.where(lane == 10 + k, scale[k : k + 1, :], row)
        row = jnp.where(lane == 14 + k, inverse[k : k + 1, :], row)
    message_ref[...] = jnp.broadcast_to(row, message_ref.shape)


def krylov(moment_lanes, vectors, gathered, edges, first, second, masks, voxel_feats, voxel_reg, devices):
    bricks, _, voxels = voxel_feats.shape
    return pl.pallas_call(
        krylov_kernel,
        out_shape=(
            jax.ShapeDtypeStruct((4, bricks, voxels), jnp.float32),
            jax.ShapeDtypeStruct((devices, LANES), jnp.float32),
        ),
        scratch_shapes=[
            pltpu.VMEM((SPAN, LANES), jnp.float32),
            pltpu.VMEM((LANES, 8, LANES), jnp.float32),
            pltpu.VMEM((LANES, LANES), jnp.float32),
            pltpu.VMEM((8 * LANES, LANES), jnp.float32),
        ],
        compiler_params=pltpu.CompilerParams(vmem_limit_bytes=8 << 20),
        name="krylov",
    )(moment_lanes, vectors, gathered, *edges, first, second, masks, voxel_feats, voxel_reg)


def finish_kernel(shared_ref, basis_ref, solution_ref, residual_ref):
    shared = shared_ref[...]
    lane = lax.broadcasted_iota(jnp.int32, (1, LANES), 1)

    def pick(row, k):
        return jnp.sum(jnp.where(lane == k, row, 0.0), axis=1, keepdims=True)

    largest = jnp.max(shared, axis=0, keepdims=True)
    smallest = jnp.min(shared, axis=0, keepdims=True)
    scale = [pick(largest, 10 + k) for k in range(4)]
    inverse = [pick(smallest, 14 + k) for k in range(4)]
    weight = [shared[:, 10 + k : 11 + k] * inverse[k] for k in range(4)]
    left = jnp.zeros_like(shared)
    right = jnp.zeros_like(shared)
    for k, (a, b) in enumerate(PAIRS):
        left = jnp.where(lane == k, weight[a], left)
        right = jnp.where(lane == k, weight[b], right)
    total = jnp.sum(shared * left * right, axis=0, keepdims=True)
    gram = [[None] * 4 for _ in range(4)]
    for k, (a, b) in enumerate(PAIRS):
        gram[a][b] = gram[b][a] = pick(total, k)
    growth = [scale[k + 1] * inverse[k] for k in range(3)]

    def product(left, right):
        terms = [
            left[a] * right[b] * gram[a][b]
            for a in range(4)
            for b in range(4)
            if left[a] is not None and right[b] is not None
        ]
        return functools.reduce(jnp.add, terms)

    def plus(left, factor, right):
        out = []
        for a, b in zip(left, right):
            out.append(a if b is None else factor * b if a is None else a + factor * b)
        return out

    def image(vector):
        return [None] + [None if vector[k] is None else vector[k] * growth[k] for k in range(3)]

    solution = [None] * 4
    residual = [jnp.ones((1, 1), jnp.float32), None, None, None]
    direction = list(residual)
    norm_now = product(residual, residual)
    for iteration in range(ITERS):
        carried = image(direction)
        alpha = norm_now / product(direction, carried)
        solution = plus(solution, alpha, direction)
        residual = plus(residual, -alpha, carried)
        if iteration + 1 < ITERS:
            norm_next = product(residual, residual)
            direction = plus(residual, norm_next / norm_now, direction)
            norm_now = norm_next
    back = [scale[0] * inverse[k] for k in range(4)]
    for out_ref, coefficients in ((solution_ref, solution), (residual_ref, residual)):
        total = None
        for k, c in enumerate(coefficients):
            if c is not None:
                term = (c * back[k]) * basis_ref[k]
                total = term if total is None else total + term
        out_ref[...] = total


def finish(shared, basis):
    _, bricks, voxels = basis.shape
    out = jax.ShapeDtypeStruct((bricks, voxels), jnp.float32)
    return pl.pallas_call(
        finish_kernel,
        out_shape=(out, out),
        compiler_params=pltpu.CompilerParams(vmem_limit_bytes=4 << 20),
        name="finish",
    )(shared, basis)


def shards(point_feats, point_targets, point_lists, brick_adjacency, voxel_feats, voxel_reg):
    feat_count = point_feats.shape[0]
    brick_total, slots = point_lists.shape
    local_bricks = voxel_feats.shape[0]
    devices = brick_total // local_bricks
    sending = pack(point_feats, point_targets, point_lists, devices)
    got = lax.all_to_all(sending, GX_GY, split_axis=0, concat_axis=0, tiled=True)

    first, second, third = prepare(voxel_feats, voxel_reg)
    mask = (brick_adjacency >= 0).astype(jnp.float32)
    mask = jnp.concatenate([mask, jnp.sum(mask, axis=1, keepdims=True)], axis=1)
    mask = jnp.pad(mask, ((0, 0), (0, LANES - 5)))
    early = (first, second, mask)
    along_even = lax.axis_index("gx_2") == 0
    across_even = lax.axis_index("gy") % 2 == 0
    early_low, early_high = swap(*along_messages(EARLY, early), GX, along_even)
    early_below, early_above = swap(*across_early(early), "gy", across_even)

    moments, vectors, gathered, to_low, to_high = find_moments(got, (first, second, third))
    low, high = swap(to_low, to_high, GX, along_even)
    first_lanes, second_lanes, mask_lanes, moment_lanes = gather_early(
        first, second, mask, (early_low, early_high, early_below, early_above),
        moments, (low, high),
    )
    below, above = swap(
        *across_late(moments, vectors, low, high, early_low, early_high), "gy", across_even
    )
    basis, message = krylov(
        moment_lanes, vectors, gathered, (low, high, below, above), first_lanes, second_lanes, mask_lanes,
        voxel_feats, voxel_reg, devices,
    )
    shared = lax.all_to_all(message, GX_GY, split_axis=0, concat_axis=0, tiled=True)
    return finish(shared, basis)


def solution(mesh):
    torus = Mesh(mesh.devices.reshape(4, 4, 2, mesh.shape["gy"]), ("gx_0", "gx_1", "gx_2", "gy"))
    return jax.shard_map(
        shards,
        mesh=torus,
        in_specs=(
            P(None, GX_GY),
            P(GX_GY),
            P(GX_GY, None),
            P(GX_GY, None),
            P(GX_GY, None, None),
            P(GX_GY, None),
        ),
        out_specs=(P(GX_GY, None), P(GX_GY, None)),
        check_vma=False,
    )
```
